32 devices in a mesh: seq: 4 (over x, core), mp: 8 (over z, y).
Axes of the slice: x: 2, y: 2, z: 4, core: 2. Of those that a mesh axis runs over, the one named last changes fastest.
Arguments:
- tokens: bfloat16 [2, 6144, 1024], P(None, ('seq', 'mp')), may hold values from -6 to 6
- ln1_gain: float32 [1024], replicated, may hold values from 0.1 to 1.9
- ln1_bias: float32 [1024], replicated, may hold values from -1.75 to 1.75
- ln2_gain: float32 [1024], replicated, may hold values from 0.1 to 1.9
- ln2_bias: float32 [1024], replicated, may hold values from -1.75 to 1.75
- q_weight: bfloat16 [1024, 1024], P('seq', 'mp'), may hold values from -0.1875 to 0.1875
- k_weight: bfloat16 [1024, 1024], P('seq', 'mp'), may hold values from -0.1875 to 0.1875
- value_weight: bfloat16 [1024, 1024], P('seq', 'mp'), may hold values from -0.1875 to 0.1875
- out_weight: bfloat16 [1024, 1024], P('mp', 'seq'), may hold values from -2 to 2
- up_weight: bfloat16 [1024, 4096], P('seq', 'mp'), may hold values from -0.1875 to 0.1875
- down_weight: bfloat16 [4096, 1024], P('mp', 'seq'), may hold values from -0.09375 to 0.09375
- lengths: int32 [2, 4, 3], P(None, 'seq'), may hold values from 1 to 1024, 1536 in all within a row
- cotangent: bfloat16 [2, 6144, 1024], P(None, ('seq', 'mp')), may hold values from -12 to 12
Outputs:
- mixed: bfloat16 [2, 6144, 1024], P(None, ('seq', 'mp'))
- grad_tokens: float32 [2, 6144, 1024], P(None, ('seq', 'mp'))
- grad_ln1_gain: float32 [1024], replicated
- grad_ln1_bias: float32 [1024], replicated
- grad_ln2_gain: float32 [1024], replicated
- grad_ln2_bias: float32 [1024], replicated
- grad_q_weight: float32 [1024, 1024], P('seq', 'mp')
- grad_k_weight: float32 [1024, 1024], P('seq', 'mp')
- grad_v_weight: float32 [1024, 1024], P('seq', 'mp')
- grad_out_weight: float32 [1024, 1024], P('mp', 'seq')
- grad_up_weight: float32 [1024, 4096], P('seq', 'mp')
- grad_down_weight: float32 [4096, 1024], P('mp', 'seq')
The draws below stay inside these ranges and needn't reach their ends.
Inputs may be any that keep to these rules, and one draw needn't show every extreme that they name: lengths[m, s] lists the 3 documents of row group s of micro-batch m in order; each row sums to 1536, and its longest document holds exactly 1024 tokens.
All inputs are finite; a program needn't handle non-finite values.
Results may differ from the reference program's by a relative error of at most 0.013.
Values may be sent and summed in bfloat16 or wider, within the bound.
No kernel may reach another device: no remote copies, remote signals or barrier semaphores. Data moves between devices by JAX's collectives and lax.ppermute only.
A program may use at most 192 MiB of HBM per device.

```python
import math
import jax
import jax.numpy as jnp
import numpy as np
from jax import lax

D = 1024
HEADS = 16
HEAD_DIM = 64
FF = 4096
ROT = 16
FEATS = 64
TOK_GRP = 1536
DOCS = 3
MICRO = 2
GROUP_ROWS = 6144
N_SEQ = 4


def spiked(array, own_key, source, target, blocks, factor):
    def block_of(axis_at):
        return (jnp.arange(array.shape[axis_at]) // (array.shape[axis_at] // blocks)).reshape((-1,) + (1,) * (array.ndim - 1 - axis_at))

    near = jax.random.permutation(own_key, blocks)[block_of(target)]
    second = (block_of(target) + blocks // 2) % blocks
    return jnp.where((block_of(source) == near) | (block_of(source) == second), factor * array, array)


def block_levels(own_key, shape, split, smallest, top_value):
    gain = 1.0
    for axis_at, shards_of in split:
        heights = jax.random.uniform(jax.random.fold_in(jax.random.fold_in(own_key, 6), axis_at), (shards_of,), jnp.float32, smallest / len(split), top_value / len(split))
        gain = gain * jnp.repeat(jnp.exp(heights), shape[axis_at] // shards_of).reshape((-1,) + (1,) * (len(shape) - 1 - axis_at))
    return gain


def length_profile(number_of, total, limit, slope):
    portions = [(1 << 20) // math.isqrt(standing ** slope) + 1 for standing in range(2, number_of + 1)]
    spare, given = total - limit - (number_of - 1), [1] * (number_of - 1)
    while spare > 0:
        free = [i for i in range(number_of - 1) if given[i] < limit]
        whole, left = sum([portions[i] for i in free]), spare
        for i in free:
            addition = min(limit - given[i], max(1, left * portions[i] // whole), spare)
            given[i] = given[i] + addition
            spare = spare - addition
    return np.array([limit] + given)


def ragged(rng, amount, total, most, skew):
    if amount == 2:
        one = jax.random.randint(rng, (), max(1, total - most), min(most, total - 1) + 1)
        return jnp.stack([one, total - one])
    tallies = jnp.asarray(length_profile(amount, total, most, skew), jnp.int32)
    pairs = (amount - 1) // 2
    donor, sink = tallies[1:1 + 2 * pairs:2], tallies[2:2 + 2 * pairs:2]
    slack = jnp.minimum(donor - 1, most - sink)
    moved = jax.random.randint(jax.random.fold_in(rng, 1), (pairs,), 0, 1 << 20) % (slack + 1)
    tallies = tallies.at[1:1 + 2 * pairs:2].set(donor - moved).at[2:2 + 2 * pairs:2].set(sink + moved)
    return tallies[jax.random.permutation(jax.random.fold_in(rng, 2), amount)]


def gaussian(own_key, shape, deviation, bound, cuts=(), kind=jnp.bfloat16):
    gain = block_levels(own_key, shape, cuts, -0.22, 0.18) if cuts else 1.0
    values = jax.random.normal(own_key, shape, jnp.float32) * deviation * gain
    return jnp.minimum(jnp.maximum(values, -bound), bound).astype(kind)


def noise_with(rng, shape, scale, bound, cuts, heavy, kind=jnp.bfloat16):
    result = scale * jax.random.normal(rng, shape, jnp.float32)
    if cuts:
        result = result * block_levels(rng, shape, cuts, -0.22, 0.18)
    return jnp.clip(spiked(result, jax.random.fold_in(rng, 3), *heavy), -bound, bound).astype(kind)


def setup_inputs(seed: int = 0) -> dict:
    seeds = jax.random.split(jax.random.key(seed), 14)
    tokens = gaussian(seeds[0], (MICRO, GROUP_ROWS, D), 1.0, 6.0, ((1, 32),))
    ln1_gain = jnp.clip(1.0 + 0.18 * jax.random.normal(seeds[1], (D,), jnp.float32), 0.1, 1.9)
    ln1_bias = gaussian(seeds[2], (D,), 0.3, 1.75, (), jnp.float32)
    ln2_gain = jnp.clip(1.0 + 0.18 * jax.random.normal(seeds[3], (D,), jnp.float32), 0.1, 1.9)
    ln2_bias = gaussian(seeds[4], (D,), 0.3, 1.75, (), jnp.float32)
    q_weight = gaussian(seeds[5], (D, D), D ** -0.5, 0.1875, ((0, 4), (1, 8)))
    k_weight = gaussian(seeds[6], (D, D), D ** -0.5, 0.1875, ((0, 4), (1, 8)))
    value_weight = gaussian(seeds[7], (D, D), D ** -0.5, 0.1875, ((0, 4), (1, 8)))
    out_weight = gaussian(seeds[8], (D, D), (max(D // 128, 1)) ** -0.5, 2.0, ((0, 8), (1, 4)))
    up_weight = gaussian(seeds[9], (D, FF), D ** -0.5, 0.1875, ((0, 4), (1, 8)))
    down_weight = gaussian(seeds[10], (FF, D), FF ** -0.5, 0.09375, ((0, 8), (1, 4)))
    lengths = jax.vmap(lambda own: ragged(own, DOCS, TOK_GRP, TOK_GRP * 2 // 3, 2))(jax.random.split(seeds[11], MICRO * N_SEQ)).reshape((MICRO, N_SEQ, DOCS)).astype(jnp.int32)
    cotangent = noise_with(seeds[12], (MICRO, GROUP_ROWS, D), 1.0, 12.0, ((1, 32),), (1, 2, 32, 2.75))
    return {"tokens": tokens, "ln1_gain": ln1_gain, "ln1_bias": ln1_bias, "ln2_gain": ln2_gain, "ln2_bias": ln2_bias, "q_weight": q_weight, "k_weight": k_weight, "value_weight": value_weight, "out_weight": out_weight, "up_weight": up_weight, "down_weight": down_weight, "lengths": lengths, "cotangent": cotangent}


@jax.custom_vjp
def low(v):
    return lax.optimization_barrier(v.astype(jnp.bfloat16)).astype(jnp.float32)

@jax.custom_vjp
def low_back(v):
    return v

def lowpass_retained(v):
    return (low(v), None)

def low_pass(kept, grad):
    return (grad,)

def back_keep(v):
    return (v, None)

def back_low(kept, grad):
    return (low(grad),)
low.defvjp(lowpass_retained, low_pass)
low_back.defvjp(back_keep, back_low)

def prime_list(wanted):
    found_primes = []
    candidate = 2
    while len(found_primes) < wanted:
        if all((candidate % earlier != 0 for earlier in found_primes)):
            found_primes.append(candidate)
        candidate += 1
    return found_primes

def feature_maps(head_width, feature_count):
    primes_found = prime_list(head_width)
    uniform_rows = [[min(max((row_idx + 0.5) * math.sqrt(prime_val) % 1.0, 0.001), 0.999) for prime_val in primes_found] for row_idx in range(feature_count)]
    uniform_pts = jnp.asarray(uniform_rows, jnp.float32)
    points = math.sqrt(2.0) * lax.erf_inv(2.0 * uniform_pts - 1.0)
    cosine_rows = [[math.sqrt(2.0 / head_width) * math.cos(math.pi * (cell_idx + 0.5) * freq_idx / head_width) * (math.sqrt(0.5) if freq_idx == 0 else 1.0) for cell_idx in range(head_width)] for freq_idx in range(head_width)]
    cosine = jnp.asarray(cosine_rows, jnp.float32)
    project = jnp.dot(points, cosine, precision=lax.Precision.HIGHEST)
    project = jnp.transpose(project) * (1.0 / math.sqrt(head_width))
    weighting = 1.0 / (1.0 + lax.optimization_barrier(jnp.sum(points * points, axis=1)) / head_width)
    return (project, weighting)

def rotate(values, offset):
    half_dims = ROT // 2
    inverse = 10000.0 ** (-jnp.arange(half_dims, dtype=jnp.float32) * 2.0 / ROT)
    angles = offset[:, None] * inverse[None, :]
    cosine = jnp.cos(angles)[:, None, :]
    sine_part = jnp.sin(angles)[:, None, :]
    first_half = values[..., :half_dims]
    second = values[..., half_dims:ROT]
    return jnp.concatenate([first_half * cosine - second * sine_part, second * cosine + first_half * sine_part, values[..., ROT:]], axis=-1)

def layer_norm(values, gain_vec, bias_vec):
    centered = values - lax.optimization_barrier(jnp.mean(values, axis=-1, keepdims=True))
    variance = lax.optimization_barrier(jnp.mean(centered * centered, axis=-1, keepdims=True))
    return centered * lax.rsqrt(variance + 1e-05) * gain_vec + bias_vec

def doc_layout(doc_lengths, number_of_tokens):
    doc_ends = jnp.cumsum(doc_lengths).astype(jnp.int32)
    starts = (doc_ends - doc_lengths).astype(jnp.int32)
    places = jnp.arange(number_of_tokens, dtype=jnp.int32)
    segment = lax.optimization_barrier(jnp.sum((places[:, None] >= doc_ends[None, :]).astype(jnp.int32), axis=1)).astype(jnp.int32)
    member = segment[:, None] == jnp.arange(doc_lengths.shape[0], dtype=jnp.int32)[None, :]
    offset = places - lax.optimization_barrier(jnp.sum(jnp.where(member, starts[None, :], 0), axis=1)).astype(jnp.int32)
    return (segment, offset.astype(jnp.float32))

def head_attention(feat_query, feat_key, value_heads, segment):
    attention_scores = jnp.dot(feat_query, jnp.transpose(feat_key), precision=lax.Precision.HIGHEST)
    places = jnp.arange(segment.shape[0], dtype=jnp.int32)
    allowed = (places[:, None] >= places[None, :]) & (segment[:, None] == segment[None, :])
    attention_scores = jnp.where(allowed, attention_scores, 0.0)
    numerator = jnp.dot(attention_scores, value_heads, precision=lax.Precision.HIGHEST)
    denominator = lax.optimization_barrier(jnp.sum(attention_scores, axis=1, keepdims=True))
    return numerator / denominator

def block_forward(params, tokens_piece, doc_lengths, project, weighting):
    gain_one, bias_one, gain_two, bias_two, w_query, w_key, w_value, w_out, w_up, w_down = params
    maximal_precision_mode = lax.Precision.HIGHEST
    number_of_tokens = tokens_piece.shape[0]
    segment, offset = doc_layout(doc_lengths, number_of_tokens)
    normed_one = low(layer_norm(tokens_piece, gain_one, bias_one))
    normed_two = low(layer_norm(tokens_piece, gain_two, bias_two))
    plain_query_rows = low_back(jnp.dot(normed_one, w_query, precision=maximal_precision_mode))
    key_raw = low_back(jnp.dot(normed_one, w_key, precision=maximal_precision_mode))
    value_raw = low_back(jnp.dot(normed_one, w_value, precision=maximal_precision_mode))
    rot_query = rotate(plain_query_rows.reshape(number_of_tokens, HEADS, HEAD_DIM), offset)
    rot_key = rotate(key_raw.reshape(number_of_tokens, HEADS, HEAD_DIM), offset)
    value_heads = value_raw.reshape(number_of_tokens, HEADS, HEAD_DIM)
    feat_query = jnp.exp(jnp.einsum('thd,df->thf', rot_query, project, precision=maximal_precision_mode)) * weighting
    feat_key = jnp.exp(jnp.einsum('thd,df->thf', rot_key, project, precision=maximal_precision_mode))

    def one_head(pieces):
        return head_attention(pieces[0], pieces[1], pieces[2], segment)
    attended = lax.map(jax.checkpoint(one_head), (jnp.transpose(feat_query, (1, 0, 2)), jnp.transpose(feat_key, (1, 0, 2)), jnp.transpose(value_heads, (1, 0, 2))))
    context = low(jnp.transpose(attended, (1, 0, 2)).reshape(number_of_tokens, HEADS * HEAD_DIM))
    hidden = low_back(jnp.dot(normed_two, w_up, precision=maximal_precision_mode))
    activated = low(jax.nn.gelu(hidden, approximate=False))
    return tokens_piece + jnp.dot(context, w_out, precision=maximal_precision_mode) + jnp.dot(activated, w_down, precision=maximal_precision_mode)

def reference(tokens, ln1_gain, ln1_bias, ln2_gain, ln2_bias, q_weight, k_weight, value_weight, out_weight, up_weight, down_weight, lengths, cotangent):
    micro_count, group_rows, width = tokens.shape
    group_count = lengths.shape[1]
    number_of_tokens = group_rows // group_count
    pieces = tokens.astype(jnp.float32).reshape(micro_count * group_count, number_of_tokens, width)
    doc_table = lengths.reshape(micro_count * group_count, lengths.shape[2])
    params = (ln1_gain.astype(jnp.float32), ln1_bias.astype(jnp.float32), ln2_gain.astype(jnp.float32), ln2_bias.astype(jnp.float32), q_weight.astype(jnp.float32), k_weight.astype(jnp.float32), value_weight.astype(jnp.float32), out_weight.astype(jnp.float32), up_weight.astype(jnp.float32), down_weight.astype(jnp.float32))
    project, weighting = feature_maps(HEAD_DIM, FEATS)

    def forward(tokens_all, weight_set):

        def one_piece(carried):
            return block_forward(weight_set, carried[0], carried[1], project, weighting)
        return lax.map(jax.checkpoint(one_piece), (tokens_all, doc_table))
    outputs, pullback = jax.vjp(forward, pieces, params)
    grad_pieces, grad_params = pullback(cotangent.astype(jnp.float32).reshape(pieces.shape))
    return (outputs.reshape(tokens.shape).astype(jnp.bfloat16), grad_pieces.reshape(tokens.shape), grad_params[0], grad_params[1], grad_params[2], grad_params[3], grad_params[4], grad_params[5], grad_params[6], grad_params[7], grad_params[8], grad_params[9])
```

```python
import math

import jax
import jax.numpy as jnp
import numpy as np
from jax import lax
from jax.experimental import pallas as pl
from jax.experimental.pallas import tpu as pltpu
from jax.sharding import PartitionSpec as P

HEAD_DIM = 64
ROT = 16
FEATS = 64
STATE_ROWS = 80
AXES = ("seq", "mp")
BF16 = jnp.bfloat16
F32 = jnp.float32
HIGHEST = lax.Precision.HIGHEST
ROWS = (((0,), (0,)), ((), ()))
COLS = (((1,), (1,)), ((), ()))


def prime_list(wanted):
    found_primes = []
    candidate = 2
    while len(found_primes) < wanted:
        if all((candidate % earlier != 0 for earlier in found_primes)):
            found_primes.append(candidate)
        candidate += 1
    return found_primes


def feature_maps(head_width, feature_count):
    primes_found = prime_list(head_width)
    uniform_rows = [
        [
            min(max((row_idx + 0.5) * math.sqrt(prime_val) % 1.0, 0.001), 0.999)
            for prime_val in primes_found
        ]
        for row_idx in range(feature_count)
    ]
    uniform_pts = jnp.asarray(uniform_rows, F32)
    points = math.sqrt(2.0) * lax.erf_inv(2.0 * uniform_pts - 1.0)
    cosine_rows = [
        [
            math.sqrt(2.0 / head_width)
            * math.cos(math.pi * (cell_idx + 0.5) * freq_idx / head_width)
            * (math.sqrt(0.5) if freq_idx == 0 else 1.0)
            for cell_idx in range(head_width)
        ]
        for freq_idx in range(head_width)
    ]
    cosine = jnp.asarray(cosine_rows, F32)
    project = jnp.dot(points, cosine, precision=HIGHEST)
    project = jnp.transpose(project) * (1.0 / math.sqrt(head_width))
    weighting = 1.0 / (1.0 + jnp.sum(points * points, axis=1) / head_width)
    return (project, weighting)


def mm(left, right, dims=(((1,), (0,)), ((), ())), precision=None):
    return lax.dot_general(left, right, dims, precision=precision, preferred_element_type=F32)


def lane_head(shape):
    return lax.broadcasted_iota(jnp.int32, shape, len(shape) - 1) // HEAD_DIM


def block_diag(state):
    width = state.shape[1]
    tall = jnp.concatenate([state] * (width // HEAD_DIM), axis=0)
    rows = lax.broadcasted_iota(jnp.int32, tall.shape, 0) // HEAD_DIM
    return jnp.where(rows == lane_head(tall.shape), tall, 0.0)


def diag_blocks(full):
    width = full.shape[1]
    lanes = lane_head((HEAD_DIM, width))
    total = jnp.zeros((HEAD_DIM, width), F32)
    for head in range(width // HEAD_DIM):
        part = full[head * HEAD_DIM : (head + 1) * HEAD_DIM, :]
        total = total + jnp.where(lanes == head, part, 0.0)
    return total


def swap_halves(values):
    width = values.shape[1]
    half = ROT // 2
    lane = lax.broadcasted_iota(jnp.int32, values.shape, 1) % HEAD_DIM
    return jnp.where(
        lane < half, pltpu.roll(values, width - half, 1), pltpu.roll(values, half, 1)
    )


def wide(table, width):
    return jnp.concatenate([table] * (width // table.shape[1]), axis=1)


def causal(col, row):
    return (row >= col[:, 0:1]) & (row <= col[:, 1:2])


def state_of(keys, values, scores):
    width = values.shape[1]
    sums = diag_blocks(mm(keys.astype(BF16), values.astype(BF16), ROWS))
    totals = jnp.sum(keys * scores, axis=0, keepdims=True)
    tail = jnp.broadcast_to(totals, (STATE_ROWS - HEAD_DIM, width))
    return jnp.concatenate([sums, tail], axis=0)


def attend_body(
    normed, weight, cos, sin, col, row, proj, wts, fq_out, fk_out, v_out, num_out, den_out, st_out
):
    width = fq_out.shape[2]
    heads = width // HEAD_DIM
    qkv = mm(normed[0], weight[...])
    cosw, sinw = wide(cos[0], width), wide(sin[0], width)

    def feats(values):
        turned = values * cosw + swap_halves(values) * sinw
        return jnp.exp(mm(turned, proj[...], precision=HIGHEST))

    fq = feats(qkv[:, :width]) * wts[...]
    fk = feats(qkv[:, width : 2 * width])
    fqb, fkb = fq.astype(BF16), fk.astype(BF16)
    vb = qkv[:, 2 * width :].astype(BF16)
    fq_out[0] = fqb
    fk_out[0] = fkb
    v_out[0] = vb
    info = col[0]
    mask = causal(info, row[0, 0:1, :])
    lanes = lane_head(vb.shape)
    num = jnp.zeros(vb.shape, F32)
    den = jnp.zeros(vb.shape, F32)
    for head in range(heads):
        mine = lanes == head
        scores = mm(jnp.where(mine, fqb, 0), fkb, COLS)
        scores = jnp.where(mask, scores, 0.0).astype(BF16)
        both = mm(scores, jnp.where(mine, vb, 1))
        num = jnp.where(mine, both, num)
        den = jnp.where(mine, pltpu.roll(both, HEAD_DIM, 1), den)
    num_out[0] = num
    den_out[0] = den
    st_out[0] = state_of(jnp.where(info[:, 3:4] > 0.0, fk, 0.0), vb, 1.0)


def finish_body(num, den, fq, carry, col, ones, ctx_out, rden_out):
    fqb = fq[0]
    came = carry[0]
    more_num = mm(fqb, block_diag(came[:HEAD_DIM]).astype(BF16))
    more_den = mm(
        fqb.astype(F32) * came[HEAD_DIM : HEAD_DIM + 1], ones[...], precision=HIGHEST
    )
    carried = col[0][:, 2:3] > 0.0
    total_den = den[0] + jnp.where(carried, more_den, 0.0)
    total_num = num[0] + jnp.where(carried, more_num, 0.0)
    inverse = 1.0 / total_den
    ctx_out[0] = (total_num * inverse).astype(BF16)
    rden_out[0] = inverse


def back_body(
    grad, wout, fq, fk, vals, ctx, rden, carry, cos, sin, col, row, proj, ones,
    dq_out, dk_out, dv_out, st_out,
):
    width = fq.shape[2]
    heads = width // HEAD_DIM
    gctx = mm(grad[0], wout[...], COLS)
    inverse = rden[0]
    dnum = gctx * inverse
    dden = -mm(gctx * ctx[0].astype(F32), ones[...], precision=HIGHEST) * inverse
    fqb, fkb, vb = fq[0], fk[0], vals[0]
    info = col[0]
    mask = causal(info, row[0, 0:1, :])
    lanes = lane_head(vb.shape)
    lane = lax.broadcasted_iota(jnp.int32, vb.shape, 1)
    dnb = dnum.astype(BF16)
    rolled = pltpu.roll(dden, HEAD_DIM, 1).astype(BF16)
    dfq = jnp.zeros(vb.shape, F32)
    dfk = jnp.zeros(vb.shape, F32)
    dv = jnp.zeros(vb.shape, F32)
    for head in range(heads):
        mine = lanes == head
        extra = (head + 1) % heads * HEAD_DIM
        dn = jnp.where(mine, dnb, jnp.where(lane == extra, rolled, 0))
        dscores = mm(dn, jnp.where(mine, vb, 1), COLS)
        dscores = jnp.where(mask, dscores, 0.0).astype(BF16)
        scores = mm(jnp.where(mine, fqb, 0), fkb, COLS)
        scores = jnp.where(mask, scores, 0.0).astype(BF16)
        dfq = jnp.where(mine, mm(dscores, fkb), dfq)
        dfk = jnp.where(mine, mm(dscores, fqb, ROWS), dfk)
        dv = jnp.where(mine, mm(scores, dnb, ROWS), dv)
    came = carry[0]
    carried = info[:, 2:3] > 0.0
    more = mm(dnb, block_diag(came[:HEAD_DIM]).astype(BF16), COLS)
    more = more + dden * came[HEAD_DIM : HEAD_DIM + 1]
    dfq = dfq + jnp.where(carried, more, 0.0)
    fqf = fqb.astype(F32)
    st_out[0] = state_of(jnp.where(carried, fqf, 0.0), dnum, dden)
    cosw, sinw = wide(cos[0], width), wide(sin[0], width)
    turned = mm(dfq * fqf, proj[...], COLS, precision=HIGHEST)
    dq_out[0] = (turned * cosw - swap_halves(turned) * sinw).astype(BF16)
    dk_out[0] = dfk
    dv_out[0] = dv


def last_body(dfk, dv, fk, vals, carry, cos, sin, col, proj, dk_out, dv_out):
    width = fk.shape[2]
    fkb, vb = fk[0], vals[0]
    came = carry[0]
    state = block_diag(came[:HEAD_DIM]).astype(BF16)
    used = col[0][:, 3:4] > 0.0
    more_k = mm(vb, state, COLS) + came[HEAD_DIM : HEAD_DIM + 1]
    more_v = mm(fkb, state)
    total_k = dfk[0] + jnp.where(used, more_k, 0.0)
    dv_out[0] = (dv[0] + jnp.where(used, more_v, 0.0)).astype(BF16)
    cosw, sinw = wide(cos[0], width), wide(sin[0], width)
    turned = mm(total_k * fkb.astype(F32), proj[...], COLS, precision=HIGHEST)
    dk_out[0] = (turned * cosw - swap_halves(turned) * sinw).astype(BF16)


def per_sequence(body, args, outs):
    count = outs[0][0][0]

    def spec(shape):
        if len(shape) == 3:
            return pl.BlockSpec((1,) + tuple(shape[1:]), lambda i: (i, 0, 0))
        return pl.BlockSpec(tuple(shape), lambda i: (0, 0))

    return pl.pallas_call(
        body,
        grid=(count,),
        in_specs=[spec(arg.shape) for arg in args],
        out_specs=[spec(shape) for shape, _ in outs],
        out_shape=[jax.ShapeDtypeStruct(shape, kind) for shape, kind in outs],
        compiler_params=pltpu.CompilerParams(
            dimension_semantics=("arbitrary",), vmem_limit_bytes=56 * 1024 * 1024
        ),
    )(*args)


class Layout:
    def __init__(self):
        self.seqs, self.parts = lax.axis_size("seq"), lax.axis_size("mp")
        self.pairs, self.chunks = self.seqs // 2, self.parts // 2
        seq, part = lax.axis_index("seq"), lax.axis_index("mp")
        self.pair, self.core = seq // 2, seq % 2
        self.hi, self.lo = part // 2, part % 2

    def move(self, values, rule):
        links = []
        for seq in range(self.seqs):
            for part in range(self.parts):
                there = rule(seq // 2, seq % 2, part // 2, part % 2)
                if there is not None:
                    pair, core, hi, lo = there
                    goal = (pair * 2 + core) * self.parts + hi * 2 + lo
                    links.append((seq * self.parts + part, goal))
        return lax.ppermute(values, AXES, links)

    def core_swap(self, values):
        return self.move(values, lambda p, c, h, l: (p, 1 - c, h, l))

    def lo_swap(self, values):
        return self.move(values, lambda p, c, h, l: (p, c, h, 1 - l))

    def pair_step(self, values, way):
        return self.move(values, lambda p, c, h, l: ((p + way) % self.pairs, c, h, l))

    def hi_step(self, values, way):
        return self.move(values, lambda p, c, h, l: (p, c, (h + way) % self.chunks, l))


def both_orders(first, second, swapped, axis):
    return jnp.where(
        swapped,
        jnp.concatenate([second, first], axis),
        jnp.concatenate([first, second], axis),
    )


def reorder(stacked, here):
    count = stacked.shape[0]
    if count == 2:
        return jnp.where(here == 0, stacked, stacked[::-1])
    back = stacked[::-1]
    twice = jnp.concatenate([back, back], 0)
    return lax.dynamic_slice_in_dim(twice, (count - 1 - here) % count, count, 0)


def reorder_chunks(lay, parts):
    return jnp.swapaxes(reorder(jnp.swapaxes(parts, 0, 1), lay.hi), 0, 1)


def reorder_both(lay, parts):
    return reorder_chunks(lay, reorder(parts, lay.pair))


def gather_blocks(lay, block):
    ring = [block]
    for _ in range(lay.chunks - 1):
        ring.append(lay.hi_step(ring[-1], 1))
    half = (lay.chunks + 1) // 2
    groups = [jnp.stack(ring[:half]), jnp.stack(ring[half:])]
    rows = [jnp.concatenate(groups, 0)]
    for _ in range(lay.pairs - 1):
        groups = [lay.pair_step(group, 1) for group in groups]
        rows.append(jnp.concatenate(groups, 0))
    return jnp.stack(rows)


def scatter_blocks(lay, parts):
    total = parts[lay.pairs - 1]
    for step in range(lay.pairs - 2, -1, -1):
        total = lay.pair_step(total.astype(BF16), -1).astype(F32) + parts[step].astype(F32)
    out = total[lay.chunks - 1]
    for step in range(lay.chunks - 2, -1, -1):
        out = lay.hi_step(out.astype(BF16), -1).astype(F32) + total[step].astype(F32)
    return out


def combine_states(lay, local, straddles, size, backward):
    reach = local
    found = jnp.zeros_like(local)
    step = 1
    while step < lay.chunks:
        base = (lay.hi // (2 * step)) * (2 * step)
        upper = (lay.hi & step) > 0
        middle = (base + step) * size
        last = step * 2 >= lay.chunks

        def rule(p, c, h, l, step=step, last=last):
            sender = ((h & step) == 0) != backward
            return (p, c, h ^ step, l) if sender or not last else None

        got = lay.move(reach.astype(BF16), rule).astype(F32)
        scale = lambda edge: straddles(middle, edge)[:, None, None]
        if backward:
            here = (lay.hi + 1) * size
            keeps = jnp.where(upper, 0.0, scale(here))
            edge = base * size
        else:
            here = lay.hi * size
            keeps = jnp.where(upper, scale(here), 0.0)
            edge = (base + 2 * step) * size
        found = found + keeps * got
        if not last:
            far = scale(edge)
            mine_far = upper if backward else jnp.logical_not(upper)
            reach = jnp.where(mine_far, far * reach + got, reach + far * got)
        step *= 2
    return found


def local(
    tokens,
    ln1_gain,
    ln1_bias,
    ln2_gain,
    ln2_bias,
    q_weight,
    k_weight,
    value_weight,
    out_weight,
    up_weight,
    down_weight,
    lengths,
    cotangent,
):
    lay = Layout()
    micro, rows, dim = tokens.shape
    drows, units = q_weight.shape
    swapped = lay.core == 1
    split_heads = (units // HEAD_DIM) % 2 == 0

    def halves(values, axis):
        size = values.shape[axis] // 2
        low = lax.slice_in_dim(values, 0, size, axis=axis)
        high = lax.slice_in_dim(values, size, 2 * size, axis=axis)
        return jnp.where(swapped, high, low), jnp.where(swapped, low, high)

    if split_heads:
        keeps, sends = [], []
        for shard in (q_weight, k_weight, value_weight):
            keep, send = halves(shard, 1)
            keeps.append(keep)
            sends.append(send)
        keep, send = jnp.concatenate(keeps, 1), jnp.concatenate(sends, 1)
        got = lay.core_swap(send)
        block_a = both_orders(keep, got, swapped, 1)
        out_keep, out_send = halves(out_weight, 0)
    else:
        trade = lambda p, c, h, l: (p, c, h, l) if (h & 1) == c else (p, 1 - c, h ^ 1, l)
        block_a = lay.move(jnp.concatenate([q_weight, k_weight, value_weight], 1), trade)
        block_o = lay.move(out_weight, trade)

    def gather_rows(values):
        beside = lay.lo_swap(values)
        own = jnp.stack([values, beside], 1)
        other = jnp.stack([lay.core_swap(values), lay.core_swap(beside)], 1)
        return jnp.stack([own, other])

    group_tokens = gather_rows(tokens)
    gathered_a = gather_blocks(lay, block_a)
    half_units = units // 2
    width = lay.parts * units // 4
    if split_heads:
        parts = gathered_a.reshape(lay.pairs, lay.chunks, drows, 2, 3, half_units)
        parts = reorder_both(lay, parts)
        w_qkv = jnp.transpose(parts, (0, 3, 2, 4, 1, 5)).reshape(dim, 3 * width)
    else:
        parts = reorder_both(lay, gathered_a)
        parts = parts.reshape(lay.pairs, lay.chunks // 2, 2, drows, 3, units)
        w_qkv = jnp.transpose(parts, (0, 2, 3, 4, 1, 5)).reshape(dim, 3 * width)

    up_keep, up_send = halves(up_weight, 1)
    down_keep, down_send = halves(down_weight, 0)
    got = lay.core_swap(up_send)
    block_up = both_orders(up_keep, got, swapped, 0)
    if split_heads:
        keep = jnp.concatenate([down_keep, out_keep], 0)
        got = lay.core_swap(jnp.concatenate([down_send, out_send], 0))
        block_down = both_orders(keep, got, swapped, 1)
    else:
        block_down = both_orders(down_keep, lay.core_swap(down_send), swapped, 1)
    ff_half = up_keep.shape[1]
    ff = ff_half * lay.chunks
    w_up = jnp.transpose(
        reorder(gather_blocks(lay, block_up), lay.pair), (0, 2, 1, 3)
    ).reshape(dim, ff)
    gathered_down = reorder(gather_blocks(lay, block_down), lay.pair)
    w_down = jnp.transpose(gathered_down[:, :, :ff_half], (1, 2, 0, 3)).reshape(ff, dim)
    if split_heads:
        parts = reorder_chunks(lay, gathered_down[:, :, ff_half:])
        w_out = jnp.transpose(parts, (1, 2, 0, 3)).reshape(width, dim)
    else:
        parts = reorder_both(lay, gather_blocks(lay, block_o))
        parts = parts.reshape(lay.pairs, lay.chunks // 2, 2, units, drows)
        w_out = jnp.transpose(parts, (1, 3, 0, 2, 4)).reshape(width, dim)
    group_cot = gather_rows(cotangent)

    own_lengths = lengths[:, 0]
    table = jnp.stack([own_lengths, lay.core_swap(own_lengths)]).reshape(-1, lengths.shape[2])
    ends = jnp.cumsum(table, axis=1)
    starts = ends - table
    chunk = 2 * rows
    here = lay.hi * chunk
    count = jnp.arange(rows, dtype=jnp.int32)
    places = jnp.concatenate(
        [here + lay.lo * rows + count, here + (1 - lay.lo) * rows + count]
    )
    member = (places[None, :, None] >= starts[:, None, :]) & (
        places[None, :, None] < ends[:, None, :]
    )
    row_start = jnp.sum(jnp.where(member, starts[:, None, :], 0), axis=2)
    row_end = jnp.sum(jnp.where(member, ends[:, None, :], 0), axis=2)
    sequences = table.shape[0]
    place_rows = jnp.broadcast_to(places[None, :], row_start.shape)
    col = jnp.stack(
        [
            row_start.astype(F32),
            place_rows.astype(F32),
            (row_start < here).astype(F32),
            (row_end > here + chunk).astype(F32),
        ]
        + [jnp.zeros(row_start.shape, F32)] * 4,
        axis=2,
    )
    row = jnp.broadcast_to(place_rows[:, None, :].astype(F32), (sequences, 8, chunk))

    def straddles(first, second):
        lower, higher = jnp.minimum(first, second), jnp.maximum(first, second)
        return jnp.any((starts < lower) & (ends > higher), axis=1).astype(F32)

    offset = (place_rows - row_start).astype(F32)
    lane = np.arange(128) % HEAD_DIM
    turn = lane < ROT
    inverse = np.where(turn, 10000.0 ** (-(lane % (ROT // 2)) * 2.0 / ROT), 0.0)
    side = np.where(turn, np.where(lane < ROT // 2, -1.0, 1.0), 0.0)
    angles = offset[:, :, None] * jnp.asarray(inverse, F32)[None, None, :]
    cos = jnp.cos(angles)
    sin = jnp.sin(angles) * jnp.asarray(side, F32)[None, None, :]
    project, weighting = feature_maps(HEAD_DIM, FEATS)
    heads = width // HEAD_DIM
    proj = jnp.kron(jnp.eye(heads, dtype=F32), project)
    wts = jnp.tile(weighting, heads)[None, :]
    ones = jnp.asarray(np.kron(np.eye(heads), np.ones((HEAD_DIM, HEAD_DIM))), F32)

    total_rows = sequences * chunk
    x = group_tokens.reshape(total_rows, dim)

    def normalize(values):
        centered = values - jnp.mean(values, axis=-1, keepdims=True)
        variance = jnp.mean(centered * centered, axis=-1, keepdims=True)
        scale = lax.rsqrt(variance + 1e-05)
        return centered * scale, scale

    n_all, _ = normalize(x.astype(F32))
    n_one = (n_all * ln1_gain + ln1_bias).astype(BF16)
    n_two = (n_all * ln2_gain + ln2_bias).astype(BF16)
    by_seq = (sequences, chunk, width)
    fq, fk, vals, num, den, state = per_sequence(
        attend_body,
        (n_one.reshape(sequences, chunk, dim), w_qkv, cos, sin, col, row, proj, wts),
        [(by_seq, BF16)] * 3
        + [(by_seq, F32)] * 2
        + [((sequences, STATE_ROWS, width), F32)],
    )
    carry = combine_states(lay, state, straddles, chunk, False)

    hidden = mm(n_two, w_up)
    cdf = 0.5 * (1.0 + lax.erf(hidden * math.sqrt(0.5)))
    act = (hidden * cdf).astype(BF16)
    slope = (cdf + hidden * jnp.exp(-0.5 * hidden * hidden) * (0.5 / math.pi) ** 0.5).astype(BF16)

    ctx, rden = per_sequence(
        finish_body, (num, den, fq, carry, col, ones), [(by_seq, BF16), (by_seq, F32)]
    )
    ctx_rows = ctx.reshape(total_rows, width)
    half_rows = total_rows // 2

    def sum_rows(make):
        away = make(1).astype(BF16)
        mine = make(0) + lay.core_swap(away).astype(F32)
        mine = mine.reshape(micro, 2, rows, dim)
        return mine[:, 0] + lay.lo_swap(mine[:, 1].astype(BF16)).astype(F32)

    def branch(group):
        part = slice(group * half_rows, (group + 1) * half_rows)
        return mm(ctx_rows[part], w_out) + mm(act[part], w_down)

    mixed = (tokens.astype(F32) + sum_rows(branch)).astype(BF16)

    g = group_cot.reshape(total_rows, dim)
    grad_hidden = (mm(g, w_down, COLS) * slope.astype(F32)).astype(BF16)
    dq, dk_part, dv_part, dstate = per_sequence(
        back_body,
        (
            g.reshape(sequences, chunk, dim), w_out, fq, fk, vals, ctx, rden, carry,
            cos, sin, col, row, proj, ones,
        ),
        [(by_seq, BF16), (by_seq, F32), (by_seq, F32), ((sequences, STATE_ROWS, width), F32)],
    )
    dcarry = combine_states(lay, dstate, straddles, chunk, True)
    dw_down = mm(act, g, ROWS)
    dw_out = mm(ctx_rows, g, ROWS)
    dw_up = mm(n_two, grad_hidden, ROWS)
    dk, dv = per_sequence(
        last_body,
        (dk_part, dv_part, fk, vals, dcarry, cos, sin, col, proj),
        [(by_seq, BF16), (by_seq, BF16)],
    )
    dqkv = jnp.concatenate([dq, dk, dv], axis=2).reshape(total_rows, 3 * width)
    dw_qkv = mm(n_one, dqkv, ROWS)

    part_one = mm(dqkv, w_qkv, COLS)
    part_two = mm(grad_hidden, w_up, COLS)
    norm_sums = jnp.stack(
        [
            jnp.sum(part_one * n_all, axis=0),
            jnp.sum(part_one, axis=0),
            jnp.sum(part_two * n_all, axis=0),
            jnp.sum(part_two, axis=0),
        ]
    )
    mixed_grad = part_one * ln1_gain + part_two * ln2_gain
    e = sum_rows(lambda group: mixed_grad[group * half_rows : (group + 1) * half_rows])
    n_own, r_own = normalize(tokens.astype(F32))
    grad_tokens = cotangent.astype(F32) + r_own * (
        e
        - jnp.mean(e, axis=-1, keepdims=True)
        - n_own * jnp.mean(e * n_own, axis=-1, keepdims=True)
    )
    norm_sums = norm_sums + lay.core_swap(norm_sums)
    norm_sums = norm_sums + lay.lo_swap(norm_sums)
    step = 1
    while step < lay.pairs:
        norm_sums = norm_sums + lay.move(
            norm_sums, lambda p, c, h, l, step=step: (p ^ step, c, h, l)
        )
        step *= 2
    step = 1
    while step < lay.chunks:
        norm_sums = norm_sums + lay.move(
            norm_sums, lambda p, c, h, l, step=step: (p, c, h ^ step, l)
        )
        step *= 2

    def merge(block, axis_from, axis_to):
        keep, send = halves(block, axis_from)
        return both_orders(keep, lay.core_swap(send), swapped, axis_to)

    parts = dw_down.astype(BF16).reshape(lay.chunks, ff_half, lay.pairs, dim // lay.pairs)
    parts = reorder(jnp.transpose(parts, (2, 0, 1, 3)), lay.pair)
    if split_heads:
        outs = dw_out.astype(BF16).reshape(lay.chunks, half_units, lay.pairs, dim // lay.pairs)
        outs = reorder_both(lay, jnp.transpose(outs, (2, 0, 1, 3)))
        both = scatter_blocks(lay, jnp.concatenate([parts, outs], 2)).astype(BF16)
        keep, send = halves(both, 1)
        got = lay.core_swap(send)
        grad_down = both_orders(keep[:ff_half], got[:ff_half], swapped, 0)
        grad_out = both_orders(keep[ff_half:], got[ff_half:], swapped, 0)
    else:
        grad_down = merge(scatter_blocks(lay, parts).astype(BF16), 1, 0)
        outs = dw_out.astype(BF16).reshape(lay.chunks // 2, units, lay.pairs, 2, drows)
        outs = jnp.transpose(outs, (0, 3, 2, 1, 4)).reshape(
            lay.chunks, lay.pairs, units, drows
        )
        outs = reorder(jnp.swapaxes(reorder(outs, lay.hi), 0, 1), lay.pair)
        grad_out = lay.move(scatter_blocks(lay, outs).astype(BF16), trade)
    parts = dw_up.astype(BF16).reshape(lay.pairs, dim // lay.pairs, lay.chunks, ff_half)
    parts = reorder(jnp.transpose(parts, (0, 2, 1, 3)), lay.pair)
    grad_up = merge(scatter_blocks(lay, parts).astype(BF16), 0, 1)
    if split_heads:
        parts = dw_qkv.astype(BF16).reshape(
            lay.pairs, 2, drows, 3, lay.chunks, half_units
        )
        parts = jnp.transpose(parts, (0, 4, 2, 1, 3, 5))
        parts = parts.reshape(lay.pairs, lay.chunks, drows, 6 * half_units)
        both = scatter_blocks(lay, reorder_both(lay, parts)).astype(BF16)
        keep, send = halves(both, 1)
        got = lay.core_swap(send)
        grads = []
        for idx in range(3):
            cut = slice(idx * half_units, (idx + 1) * half_units)
            grads.append(both_orders(keep[:, cut], got[:, cut], swapped, 1))
    else:
        parts = dw_qkv.astype(BF16).reshape(
            lay.pairs, 2, drows, 3, lay.chunks // 2, units
        )
        parts = jnp.transpose(parts, (4, 1, 0, 2, 3, 5))
        parts = parts.reshape(lay.chunks, lay.pairs, drows, 3 * units)
        parts = reorder(jnp.swapaxes(reorder(parts, lay.hi), 0, 1), lay.pair)
        both = lay.move(scatter_blocks(lay, parts).astype(BF16), trade)
        grads = [both[:, idx * units : (idx + 1) * units] for idx in range(3)]

    return (
        mixed,
        grad_tokens,
        norm_sums[0],
        norm_sums[1],
        norm_sums[2],
        norm_sums[3],
        grads[0].astype(F32),
        grads[1].astype(F32),
        grads[2].astype(F32),
        grad_out.astype(F32),
        grad_up.astype(F32),
        grad_down.astype(F32),
    )


def solution(mesh):
    in_specs = (
        P(None, ("seq", "mp"), None),
        P(),
        P(),
        P(),
        P(),
        P("seq", "mp"),
        P("seq", "mp"),
        P("seq", "mp"),
        P("mp", "seq"),
        P("seq", "mp"),
        P("mp", "seq"),
        P(None, "seq", None),
        P(None, ("seq", "mp"), None),
    )
    out_specs = (
        P(None, ("seq", "mp"), None),
        P(None, ("seq", "mp"), None),
        P(),
        P(),
        P(),
        P(),
        P("seq", "mp"),
        P("seq", "mp"),
        P("seq", "mp"),
        P("mp", "seq"),
        P("seq", "mp"),
        P("mp", "seq"),
    )
    return jax.shard_map(local, mesh=mesh, in_specs=in_specs, out_specs=out_specs, check_vma=False)
```

```python
import functools
import math

import jax
import jax.numpy as jnp
import numpy as np
from jax import lax
from jax.experimental import pallas as pl
from jax.experimental.pallas import tpu as pltpu
from jax.sharding import PartitionSpec as P

HEAD_DIM = 64
ROT = 16
FEATS = 64
STATE_ROWS = 80
AXES = ("seq", "mp")
BF16 = jnp.bfloat16
F32 = jnp.float32
VMEM_LIMIT = 56 * 1024 * 1024
NN = (((1,), (0,)), ((), ()))
NT = (((1,), (1,)), ((), ()))
TN = (((0,), (0,)), ((), ()))


def prime_list(wanted):
    found_primes = []
    candidate = 2
    while len(found_primes) < wanted:
        if all((candidate % earlier != 0 for earlier in found_primes)):
            found_primes.append(candidate)
        candidate += 1
    return found_primes


def feature_maps(head_width, feature_count):
    primes_found = prime_list(head_width)
    uniform_rows = [
        [
            min(max((row_idx + 0.5) * math.sqrt(prime_val) % 1.0, 0.001), 0.999)
            for prime_val in primes_found
        ]
        for row_idx in range(feature_count)
    ]
    uniform_pts = jnp.asarray(uniform_rows, jnp.float32)
    points = math.sqrt(2.0) * lax.erf_inv(2.0 * uniform_pts - 1.0)
    cosine_rows = [
        [
            math.sqrt(2.0 / head_width)
            * math.cos(math.pi * (cell_idx + 0.5) * freq_idx / head_width)
            * (math.sqrt(0.5) if freq_idx == 0 else 1.0)
            for cell_idx in range(head_width)
        ]
        for freq_idx in range(head_width)
    ]
    cosine = jnp.asarray(cosine_rows, jnp.float32)
    project = jnp.dot(points, cosine, precision=lax.Precision.HIGHEST)
    project = jnp.transpose(project) * (1.0 / math.sqrt(head_width))
    weighting = 1.0 / (1.0 + jnp.sum(points * points, axis=1) / head_width)
    return (project, weighting)


def rotate_heads(values, offset):
    half_dims = ROT // 2
    inverse = 10000.0 ** (-jnp.arange(half_dims, dtype=jnp.float32) * 2.0 / ROT)
    angles = offset[:, None] * inverse[None, :]
    cosine = jnp.cos(angles)[None, :, :]
    sine_part = jnp.sin(angles)[None, :, :]
    first_half = values[..., :half_dims]
    second = values[..., half_dims:ROT]
    return jnp.concatenate(
        [
            first_half * cosine - second * sine_part,
            second * cosine + first_half * sine_part,
            values[..., ROT:],
        ],
        axis=-1,
    )


def layer_norm(values, gain_vec, bias_vec):
    centered = values - jnp.mean(values, axis=-1, keepdims=True)
    variance = jnp.mean(centered * centered, axis=-1, keepdims=True)
    return centered * lax.rsqrt(variance + 1e-05) * gain_vec + bias_vec


def exact_gelu(values):
    return jax.nn.gelu(values, approximate=False)


def doc_layout(doc_lengths, number_of_tokens):
    doc_ends = jnp.cumsum(doc_lengths).astype(jnp.int32)
    starts = (doc_ends - doc_lengths).astype(jnp.int32)
    places = jnp.arange(number_of_tokens, dtype=jnp.int32)
    segment = jnp.sum((places[:, None] >= doc_ends[None, :]).astype(jnp.int32), axis=1).astype(
        jnp.int32
    )
    member = segment[:, None] == jnp.arange(doc_lengths.shape[0], dtype=jnp.int32)[None, :]
    offset = places - jnp.sum(jnp.where(member, starts[None, :], 0), axis=1).astype(jnp.int32)
    return (segment, offset.astype(jnp.float32))


def contract_rows(left_side, right_side):
    return lax.dot_general(
        left_side, right_side, (((0,), (0,)), ((), ())), preferred_element_type=jnp.float32
    )


def contract_cols(left_side, right_side):
    return lax.dot_general(
        left_side, right_side, (((1,), (1,)), ((), ())), preferred_element_type=jnp.float32
    )


def local_attention(plain_query_rows, key_raw, value_raw, segment, offset, project, weighting):
    maximal_precision_mode = lax.Precision.HIGHEST
    number_of_tokens = plain_query_rows.shape[0]
    head_count = plain_query_rows.shape[1] // HEAD_DIM

    def heads_first(values):
        return jnp.transpose(values.reshape(number_of_tokens, head_count, HEAD_DIM), (1, 0, 2))

    rot_query = rotate_heads(heads_first(plain_query_rows), offset)
    rot_key = rotate_heads(heads_first(key_raw), offset)
    value_heads = heads_first(value_raw)
    feat_query = (
        jnp.exp(jnp.einsum("htd,df->htf", rot_query, project, precision=maximal_precision_mode))
        * weighting
    )
    feat_key = jnp.exp(
        jnp.einsum("htd,df->htf", rot_key, project, precision=maximal_precision_mode)
    )
    rows_per_block = min(512, number_of_tokens)
    block_count = number_of_tokens // rows_per_block

    def split_blocks(values):
        return jnp.transpose(
            values.reshape((head_count, block_count, rows_per_block, values.shape[2])), (1, 0, 2, 3)
        )

    def block_step(carry, pieces):
        kv_state, totals, previous = carry
        block_of_queries, block_of_keys, value_block, block_segment = pieces
        places = jnp.arange(block_segment.shape[0], dtype=jnp.int32)
        attention_scores = jnp.einsum(
            "ugy,uky->ugk", block_of_queries, block_of_keys, precision=maximal_precision_mode
        )
        allowed = (places[:, None] >= places[None, :]) & (
            block_segment[:, None] == block_segment[None, :]
        )
        attention_scores = jnp.where(allowed[None, :, :], attention_scores, 0.0)
        numerator = jnp.einsum(
            "hqk,hkd->hqd", attention_scores, value_block, precision=maximal_precision_mode
        )
        denominator = jnp.sum(attention_scores, axis=2)
        carried_in = (block_segment == previous)[None, :]
        numerator = numerator + jnp.where(
            carried_in[:, :, None],
            jnp.einsum(
                "hqf,hfd->hqd", block_of_queries, kv_state, precision=maximal_precision_mode
            ),
            0.0,
        )
        denominator = denominator + jnp.where(
            carried_in,
            jnp.einsum("hqf,hf->hq", block_of_queries, totals, precision=maximal_precision_mode),
            0.0,
        )
        final_output = block_segment[-1]
        carried_over = final_output == previous
        trailing_mask = (block_segment == final_output).astype(jnp.float32)
        new_state = jnp.where(carried_over, kv_state, 0.0) + jnp.einsum(
            "hrf,hrd,r->hfd",
            block_of_keys,
            value_block,
            trailing_mask,
            precision=maximal_precision_mode,
        )
        new_totals = jnp.where(carried_over, totals, 0.0) + jnp.einsum(
            "hrf,r->hf", block_of_keys, trailing_mask, precision=maximal_precision_mode
        )
        return ((new_state, new_totals, final_output), numerator / denominator[:, :, None])

    start_carry = (
        jnp.zeros((head_count, FEATS, HEAD_DIM), jnp.float32),
        jnp.zeros((head_count, FEATS), jnp.float32),
        jnp.array(-1, jnp.int32),
    )
    _, outputs = lax.scan(
        jax.checkpoint(block_step),
        start_carry,
        (
            split_blocks(feat_query),
            split_blocks(feat_key),
            split_blocks(value_heads),
            segment.reshape(block_count, rows_per_block),
        ),
    )
    joined = jnp.transpose(outputs, (1, 0, 2, 3)).reshape(head_count, number_of_tokens, HEAD_DIM)
    return jnp.transpose(joined, (1, 0, 2)).reshape(number_of_tokens, head_count * HEAD_DIM)


def plain_local(
    tokens,
    ln1_gain,
    ln1_bias,
    ln2_gain,
    ln2_bias,
    q_weight,
    k_weight,
    value_weight,
    out_weight,
    up_weight,
    down_weight,
    lengths,
    cotangent,
):
    micro_count = tokens.shape[0]
    local_rows = tokens.shape[1]
    group_rows = local_rows * lax.axis_size("mp")
    seq_count = lax.axis_size("seq")
    project, weighting = feature_maps(HEAD_DIM, FEATS)
    grad_sums = [
        jnp.zeros((q_weight.shape[0] * seq_count, q_weight.shape[1]), jnp.float32),
        jnp.zeros((k_weight.shape[0] * seq_count, k_weight.shape[1]), jnp.float32),
        jnp.zeros((value_weight.shape[0] * seq_count, value_weight.shape[1]), jnp.float32),
        jnp.zeros((out_weight.shape[0], out_weight.shape[1] * seq_count), jnp.float32),
        jnp.zeros((up_weight.shape[0] * seq_count, up_weight.shape[1]), jnp.float32),
        jnp.zeros((down_weight.shape[0], down_weight.shape[1] * seq_count), jnp.float32),
    ]
    norm_sums = [
        jnp.zeros_like(ln1_gain),
        jnp.zeros_like(ln1_bias),
        jnp.zeros_like(ln2_gain),
        jnp.zeros_like(ln2_bias),
    ]
    mixed_parts = []
    grad_parts = []
    for micro_step in range(micro_count):
        full_weights = (
            lax.all_gather(q_weight, "seq", axis=0, tiled=True),
            lax.all_gather(k_weight, "seq", axis=0, tiled=True),
            lax.all_gather(value_weight, "seq", axis=0, tiled=True),
            lax.all_gather(out_weight, "seq", axis=1, tiled=True),
            lax.all_gather(up_weight, "seq", axis=0, tiled=True),
            lax.all_gather(down_weight, "seq", axis=1, tiled=True),
        )
        w_query, w_key, w_value, w_out, w_up, w_down = full_weights
        rows_in = tokens[micro_step].astype(jnp.float32)
        normed_one, pull_one = jax.vjp(layer_norm, rows_in, ln1_gain, ln1_bias)
        normed_two, pull_two = jax.vjp(layer_norm, rows_in, ln2_gain, ln2_bias)
        group_one, group_two = (
            lax.all_gather(normed_one.astype(jnp.bfloat16), "mp", axis=0, tiled=True),
            lax.all_gather(normed_two.astype(jnp.bfloat16), "mp", axis=0, tiled=True),
        )
        plain_query_rows = jnp.dot(group_one, w_query, preferred_element_type=jnp.float32)
        key_raw = jnp.dot(group_one, w_key, preferred_element_type=jnp.float32)
        value_raw = jnp.dot(group_one, w_value, preferred_element_type=jnp.float32)
        segment, offset = doc_layout(lengths[micro_step, 0], group_rows)
        attend = functools.partial(
            local_attention, segment=segment, offset=offset, project=project, weighting=weighting
        )
        context, pull_attn = jax.vjp(attend, plain_query_rows, key_raw, value_raw)
        context_low = context.astype(jnp.bfloat16)
        hidden = jnp.dot(group_two, w_up, preferred_element_type=jnp.float32)
        activated, pull_gelu = jax.vjp(exact_gelu, hidden)
        activated_low = activated.astype(jnp.bfloat16)
        context_rows = lax.slice_in_dim(context_low, 0, lax.axis_size("mp") * local_rows, axis=0)
        active_rows = lax.slice_in_dim(activated_low, 0, lax.axis_size("mp") * local_rows, axis=0)
        branch_sum = lax.psum_scatter(
            jnp.dot(context_rows, w_out, preferred_element_type=jnp.float32)
            + jnp.dot(active_rows, w_down, preferred_element_type=jnp.float32),
            "mp",
            scatter_dimension=0,
            tiled=True,
        )
        mixed_parts.append((rows_in + branch_sum).astype(jnp.bfloat16))
        grad_group = lax.all_gather(cotangent[micro_step], "mp", axis=0, tiled=True)
        grad_context = contract_cols(grad_group, w_out)
        grad_activated = contract_cols(grad_group, w_down)
        grad_hidden = pull_gelu(grad_activated)[0].astype(jnp.bfloat16)
        grad_query_f, grad_key_f, grad_value_f = pull_attn(grad_context)
        grad_query = grad_query_f.astype(jnp.bfloat16)
        grad_key = grad_key_f.astype(jnp.bfloat16)
        grad_value = grad_value_f.astype(jnp.bfloat16)
        micro_grads = (
            contract_rows(group_one, grad_query),
            contract_rows(group_one, grad_key),
            contract_rows(group_one, grad_value),
            contract_rows(context_low, grad_group),
            contract_rows(group_two, grad_hidden),
            contract_rows(activated_low, grad_group),
        )
        grad_sums = [total + term for total, term in zip(grad_sums, micro_grads)]
        part_one = (
            contract_cols(grad_query, w_query)
            + contract_cols(grad_key, w_key)
            + contract_cols(grad_value, w_value)
        )
        part_two = contract_cols(grad_hidden, w_up)
        sum_one, sum_two = (
            lax.psum_scatter(
                part_one.astype(jnp.bfloat16), "mp", scatter_dimension=0, tiled=True
            ).astype(jnp.float32),
            lax.psum_scatter(
                part_two.astype(jnp.bfloat16), "mp", scatter_dimension=0, tiled=True
            ).astype(jnp.float32),
        )
        grad_in_one, grad_gain_one, grad_bias_one = pull_one(sum_one)
        grad_in_two, grad_gain_two, grad_bias_two = pull_two(sum_two)
        grad_parts.append(cotangent[micro_step].astype(jnp.float32) + grad_in_one + grad_in_two)
        norm_sums = [
            norm_sums[0] + grad_gain_one,
            norm_sums[1] + grad_bias_one,
            norm_sums[2] + grad_gain_two,
            norm_sums[3] + grad_bias_two,
        ]
    weight_grads = (
        lax.psum_scatter(
            grad_sums[0].astype(jnp.bfloat16), "seq", scatter_dimension=0, tiled=True
        ).astype(jnp.float32),
        lax.psum_scatter(
            grad_sums[1].astype(jnp.bfloat16), "seq", scatter_dimension=0, tiled=True
        ).astype(jnp.float32),
        lax.psum_scatter(
            grad_sums[2].astype(jnp.bfloat16), "seq", scatter_dimension=0, tiled=True
        ).astype(jnp.float32),
        lax.psum_scatter(
            grad_sums[3].astype(jnp.bfloat16), "seq", scatter_dimension=1, tiled=True
        ).astype(jnp.float32),
        lax.psum_scatter(
            grad_sums[4].astype(jnp.bfloat16), "seq", scatter_dimension=0, tiled=True
        ).astype(jnp.float32),
        lax.psum_scatter(
            grad_sums[5].astype(jnp.bfloat16), "seq", scatter_dimension=1, tiled=True
        ).astype(jnp.float32),
    )
    norm_grads = lax.psum((norm_sums[0], norm_sums[1], norm_sums[2], norm_sums[3]), ("seq", "mp"))
    return (
        jnp.stack(mixed_parts),
        jnp.stack(grad_parts),
        norm_grads[0],
        norm_grads[1],
        norm_grads[2],
        norm_grads[3],
        weight_grads[0],
        weight_grads[1],
        weight_grads[2],
        weight_grads[3],
        weight_grads[4],
        weight_grads[5],
    )


def mm(left, right, dims=NN):
    return lax.dot_general(left, right, dims, preferred_element_type=F32)


def split(values):
    high = values.astype(BF16)
    return high, (values - high.astype(F32)).astype(BF16)


def mm3(values, high, low, dims=NN):
    first, second = split(values)
    return mm(first, high, dims) + (mm(second, high, dims) + mm(first, low, dims))


def lane_head(shape):
    return lax.broadcasted_iota(jnp.int32, shape, len(shape) - 1) // HEAD_DIM


def block_diag(state):
    width = state.shape[1]
    tall = jnp.concatenate([state] * (width // HEAD_DIM), axis=0)
    rows = lax.broadcasted_iota(jnp.int32, tall.shape, 0) // HEAD_DIM
    return jnp.where(rows == lane_head(tall.shape), tall, 0.0)


def diag_blocks(full):
    width = full.shape[1]
    lanes = lane_head((HEAD_DIM, width))
    total = jnp.zeros((HEAD_DIM, width), F32)
    for head in range(width // HEAD_DIM):
        part = full[head * HEAD_DIM : (head + 1) * HEAD_DIM, :]
        total = total + jnp.where(lanes == head, part, 0.0)
    return total


def head_sums(values):
    width = values.shape[1]
    rows = lax.broadcasted_iota(jnp.int32, (width, width), 0) // HEAD_DIM
    ones = jnp.where(rows == lane_head((width, width)), 1.0, 0.0).astype(BF16)
    high, low = split(values)
    return mm(high, ones) + mm(low, ones)


def swap_halves(values):
    width = values.shape[1]
    half = ROT // 2
    lane = lax.broadcasted_iota(jnp.int32, values.shape, 1) % HEAD_DIM
    return jnp.where(
        lane < half, pltpu.roll(values, width - half, 1), pltpu.roll(values, half, 1)
    )


def turn(values, cos, sin):
    reps = values.shape[1] // cos.shape[1]
    cosw = jnp.concatenate([cos] * reps, axis=1)
    sinw = jnp.concatenate([sin] * reps, axis=1)
    return values * cosw + swap_halves(values) * sinw


def normalize(values):
    centered = values - jnp.mean(values, axis=-1, keepdims=True)
    variance = jnp.mean(centered * centered, axis=-1, keepdims=True)
    scale = lax.rsqrt(variance + 1e-05)
    return centered * scale, scale


class Rows:
    def __init__(self, scal, seq, chunk, docs):
        rows = chunk // 2
        self.here = scal[1] * chunk
        low = self.here + scal[2] * rows
        high = self.here + (1 - scal[2]) * rows - rows

        def places(shape, axis):
            count = lax.broadcasted_iota(jnp.int32, shape, axis)
            return jnp.where(count < rows, count + low, count + high)

        self.place = places((chunk, 1), 0)
        self.across = places((1, chunk), 1)
        self.start = jnp.zeros((chunk, 1), jnp.int32)
        end = jnp.zeros((chunk, 1), jnp.int32)
        base = 4 + seq * 2 * docs
        for doc in range(docs):
            first, last = scal[base + doc], scal[base + docs + doc]
            inside = (self.place >= first) & (self.place < last)
            self.start = jnp.where(inside, first, self.start)
            end = jnp.where(inside, last, end)
        self.came = self.start < self.here
        self.goes = end > self.here + chunk

    def mask(self):
        return (self.across >= self.start) & (self.across <= self.place)


def whole(array):
    zeros = (0,) * array.ndim
    return (array, tuple(array.shape), lambda *_: zeros)


def by_seq(array):
    rest = (0,) * (array.ndim - 1)
    return (array, (1,) + tuple(array.shape[1:]), lambda i, s: (i,) + rest)


def own_seq(array):
    rest, most = (0,) * (array.ndim - 1), array.shape[0] - 1
    return (array, (1,) + tuple(array.shape[1:]), lambda i, s: (jnp.minimum(i, most),) + rest)


def away_seq(array):
    rest, count = (0,) * (array.ndim - 1), array.shape[0]
    return (
        array, (1,) + tuple(array.shape[1:]), lambda i, s: (jnp.maximum(i - count, 0),) + rest
    )


def new(shape, kind):
    return jax.ShapeDtypeStruct(shape, kind)


def call(name, body, scal, grid, ins, outs, scratch=()):
    return pl.pallas_call(
        body,
        name=name,
        grid_spec=pltpu.PrefetchScalarGridSpec(
            num_scalar_prefetch=1,
            grid=grid or (1,),
            in_specs=[pl.BlockSpec(block, index) for _, block, index in ins],
            out_specs=[pl.BlockSpec(block, index) for _, block, index in outs],
            scratch_shapes=list(scratch),
        ),
        out_shape=[array for array, _, _ in outs],
        compiler_params=pltpu.CompilerParams(
            dimension_semantics=("arbitrary",) * max(len(grid), 1), vmem_limit_bytes=VMEM_LIMIT
        ),
    )(scal, *[array for array, _, _ in ins])


class Shape:
    def __init__(self, pairs, chunks, dim, half_units, half_ff, chunk, docs):
        self.pairs, self.chunks, self.dim = pairs, chunks, dim
        self.hu, self.hf, self.chunk, self.docs = half_units, half_ff, chunk, docs
        self.dp = dim // pairs
        self.width, self.ff = chunks * half_units, chunks * half_ff

    def cols(self, scal, slot):
        start = ((scal[0] + slot) % self.pairs) * self.dp
        return pl.ds(pl.multiple_of(start, 128), self.dp)


def fill_rows(sh, target, blocks, first, size, at):
    for slot in range(sh.pairs):
        for j in range(sh.chunks):
            part = blocks[slot * sh.chunks + j][first : first + size, :]
            target[slot, at + j * size : at + (j + 1) * size, :] = part


def pack_body(scal, q, k, v, out, up, down, keep_a, send_a, send_u, send_d):
    low = scal[3] == 0
    parts_keep, parts_send = [], []
    for ref in (q, k, v):
        flat = jnp.transpose(ref[...].astype(F32))
        half = flat.shape[0] // 2
        parts_keep.append(jnp.where(low, flat[:half], flat[half:]))
        parts_send.append(jnp.where(low, flat[half:], flat[:half]))
    flat = out[...].astype(F32)
    half = flat.shape[0] // 2
    parts_keep.append(jnp.where(low, flat[:half], flat[half:]))
    parts_send.append(jnp.where(low, flat[half:], flat[:half]))
    keep_a[...] = jnp.concatenate(parts_keep, 0).astype(BF16)
    send_a[...] = jnp.concatenate(parts_send, 0).astype(BF16)
    half = up.shape[1] // 2
    send_u[...] = jnp.where(low, up[:, half:], up[:, :half])
    half = down.shape[0] // 2
    send_d[...] = jnp.where(low, down[half:, :], down[:half, :])


def join_a_body(scal, keep, got, block):
    low = scal[3] == 0
    size = keep.shape[1]
    block[:, :size] = jnp.where(low, keep[...], got[...])
    block[:, size:] = jnp.where(low, got[...], keep[...])


def join_u_body(scal, up, got, block):
    low = scal[3] == 0
    rows, half = up.shape[0], up.shape[1] // 2
    keep = jnp.where(low, up[:, :half], up[:, half:])
    block[:rows, :] = jnp.where(low, keep, got[...])
    block[rows:, :] = jnp.where(low, got[...], keep)


def join_d_body(scal, down, got, block):
    low = scal[3] == 0
    cols, half = down.shape[1], down.shape[0] // 2
    keep = jnp.where(low, down[:half, :], down[half:, :])
    block[:, :cols] = jnp.where(low, keep, got[...])
    block[:, cols:] = jnp.where(low, got[...], keep)


def norm_body(scal, own, away, g1, b1, g2, b2, one, two):
    own_turn = pl.program_id(0) < pl.num_programs(0) // 2
    x = jnp.where(own_turn, own[0], away[0]).astype(F32)
    n, _ = normalize(x)
    one[0] = (n * g1[...] + b1[...]).astype(BF16)
    two[0] = (n * g2[...] + b2[...]).astype(BF16)


def attend_body(sh, scal, normed, cos, sin, ph, pw, wts, *refs):
    blocks = refs[: sh.pairs * sh.chunks]
    fq_out, fk_out, v_out, num_out, den_out, st_out, wt = refs[sh.pairs * sh.chunks :]
    width, seq = sh.width, pl.program_id(0)

    @pl.when(seq == 0)
    def _():
        for kind in range(3):
            fill_rows(sh, wt, blocks, kind * sh.hu, sh.hu, kind * width)

    qkv = mm(normed[0, :, sh.cols(scal, 0)], wt[0], NT)
    for slot in range(1, sh.pairs):
        qkv = qkv + mm(normed[0, :, sh.cols(scal, slot)], wt[slot], NT)

    def feats(values):
        return jnp.exp(mm3(turn(values, cos[0], sin[0]), ph[...], pw[...]))

    fqb = (feats(qkv[:, :width]) * wts[...]).astype(BF16)
    fk = feats(qkv[:, width : 2 * width])
    fkb = fk.astype(BF16)
    v = qkv[:, 2 * width :]
    vb = v.astype(BF16)
    fq_out[0] = fqb
    fk_out[0] = fkb
    v_out[0] = v
    rows = Rows(scal, seq, sh.chunk, sh.docs)
    mask = rows.mask()
    lanes = lane_head(vb.shape)
    num = jnp.zeros(vb.shape, F32)
    den = jnp.zeros(vb.shape, F32)
    for head in range(width // HEAD_DIM):
        mine = lanes == head
        scores = mm(jnp.where(mine, fqb, 0), fkb, NT)
        scores = jnp.where(mask, scores, 0.0).astype(BF16)
        both = mm(scores, jnp.where(mine, vb, 1))
        num = jnp.where(mine, both, num)
        den = jnp.where(mine, pltpu.roll(both, HEAD_DIM, 1), den)
    num_out[0] = num
    den_out[0] = den
    kept = jnp.where(rows.goes, fk, 0.0)
    store_state(sh, scal, st_out, mm(kept.astype(BF16), vb, TN), kept)


def store_state(sh, scal, st_out, sums, totals):
    tail = jnp.broadcast_to(
        jnp.sum(totals, axis=0, keepdims=True), (STATE_ROWS - HEAD_DIM, sh.width)
    )
    state = jnp.concatenate([diag_blocks(sums), tail], axis=0)
    st_out[0] = pltpu.roll(state, scal[1] * sh.hu, 1)


def load_state(sh, scal, carry):
    state = pltpu.roll(carry[0], (sh.width - scal[1] * sh.hu) % sh.width, 1)
    return state[:HEAD_DIM], state[HEAD_DIM : HEAD_DIM + 1]


def up_body(sh, scal, normed, *refs):
    blocks = refs[: sh.pairs * sh.chunks]
    act_out, slope_out, wu = refs[sh.pairs * sh.chunks :]

    @pl.when(pl.program_id(0) == 0)
    def _():
        for slot in range(sh.pairs):
            for j in range(sh.chunks):
                wu[slot, :, j * sh.hf : (j + 1) * sh.hf] = blocks[slot * sh.chunks + j][...]

    hidden = mm(normed[0, :, sh.cols(scal, 0)], wu[0])
    for slot in range(1, sh.pairs):
        hidden = hidden + mm(normed[0, :, sh.cols(scal, slot)], wu[slot])
    cdf = 0.5 + 0.5 * lax.erf(hidden * math.sqrt(0.5))
    act_out[0] = (hidden * cdf).astype(BF16)
    bell = jnp.exp(-0.5 * hidden * hidden) * math.sqrt(0.5 / math.pi)
    slope_out[0] = (cdf + hidden * bell).astype(BF16)


def fill_out(sh, blocks_a, blocks_d, wo, wd):
    fill_rows(sh, wo, blocks_a, 3 * sh.hu, sh.hu, 0)
    fill_rows(sh, wd, blocks_d, 0, sh.hf, 0)


def branch_body(sh, scal, num, den, fq, carry, act, *refs):
    count = sh.pairs * sh.chunks
    blocks_a, blocks_d = refs[:count], refs[count : 2 * count]
    ctx_out, rden_out, own_out, away_out, wo, wd = refs[2 * count :]
    seq = pl.program_id(0)

    @pl.when(seq == 0)
    def _():
        fill_out(sh, blocks_a, blocks_d, wo, wd)

    fqb = fq[0]
    sums, totals = load_state(sh, scal, carry)
    more_num = mm(fqb, block_diag(sums).astype(BF16))
    more_den = head_sums(fqb.astype(F32) * totals)
    came = Rows(scal, seq, sh.chunk, sh.docs).came
    inverse = 1.0 / (den[0] + jnp.where(came, more_den, 0.0))
    ctx = (num[0] + jnp.where(came, more_num, 0.0)) * inverse
    ctx_out[0] = ctx
    rden_out[0] = inverse
    ctxb = ctx.astype(BF16)
    half = pl.num_programs(0) // 2
    for slot in range(sh.pairs):
        part = (mm(act[0], wd[slot]) + mm(ctxb, wo[slot])).astype(BF16)

        @pl.when(seq < half)
        def _():
            own_out[0, :, sh.cols(scal, slot)] = part

        @pl.when(seq >= half)
        def _():
            away_out[0, :, sh.cols(scal, slot)] = part


def pick(own, away, scal, sh, slot):
    first = pl.program_id(0) < pl.num_programs(0) // 2
    cols = sh.cols(scal, slot)
    return jnp.where(first, own[0, :, cols], away[0, :, cols])


def hidden_body(sh, scal, own, away, slope, *refs):
    blocks = refs[: sh.pairs * sh.chunks]
    out, wd = refs[sh.pairs * sh.chunks :]

    @pl.when(pl.program_id(0) == 0)
    def _():
        fill_rows(sh, wd, blocks, 0, sh.hf, 0)

    grad = mm(pick(own, away, scal, sh, 0), wd[0], NT)
    for slot in range(1, sh.pairs):
        grad = grad + mm(pick(own, away, scal, sh, slot), wd[slot], NT)
    out[0] = (grad * slope[0].astype(F32)).astype(BF16)


def back_body(sh, scal, own, away, fq, fk, vals, ctx, rden, carry, cos, sin, ph, pw, *refs):
    blocks = refs[: sh.pairs * sh.chunks]
    dq_out, dk_out, dv_out, st_out, wo = refs[sh.pairs * sh.chunks :]
    width, seq = sh.width, pl.program_id(0)

    @pl.when(seq == 0)
    def _():
        fill_rows(sh, wo, blocks, 3 * sh.hu, sh.hu, 0)

    gctx = mm(pick(own, away, scal, sh, 0), wo[0], NT)
    for slot in range(1, sh.pairs):
        gctx = gctx + mm(pick(own, away, scal, sh, slot), wo[slot], NT)
    inverse = rden[0]
    dnum = gctx * inverse
    dden = -head_sums(gctx * ctx[0]) * inverse
    fqb, fkb, v = fq[0], fk[0], vals[0]
    rows = Rows(scal, seq, sh.chunk, sh.docs)
    mask = rows.mask()
    lanes = lane_head(v.shape)
    lane = lax.broadcasted_iota(jnp.int32, v.shape, 1) % HEAD_DIM
    dn_high, dn_low = split(dnum)
    v_high, v_low = split(v)
    dd_high = dden.astype(BF16).astype(F32)
    roll = lambda values, steps: pltpu.roll(values, steps * HEAD_DIM, 1)
    den_part = jnp.where(lane == 0, dd_high, jnp.where(lane == 1, dden - dd_high, 0.0))
    left = [
        dn_high,
        roll(dn_low.astype(F32), 1).astype(BF16),
        roll(den_part, 2).astype(BF16),
        roll(dn_high.astype(F32), 3).astype(BF16),
    ]
    right = [
        v_high,
        roll(v_high.astype(F32), 1).astype(BF16),
        jnp.ones(v.shape, BF16),
        roll(v_low.astype(F32), 3).astype(BF16),
    ]

    def lay_out(parts, head):
        group = (lanes - head) & 3
        low = jnp.where(group == 0, parts[0], parts[1])
        high = jnp.where(group == 2, parts[2], parts[3])
        return jnp.where(group < 2, low, high)

    dfq = jnp.zeros(v.shape, F32)
    dfk = jnp.zeros(v.shape, F32)
    dv = jnp.zeros(v.shape, F32)
    for head in range(width // HEAD_DIM):
        mine = lanes == head
        dscores = mm(lay_out(left, head), lay_out(right, head), NT)
        dscores = jnp.where(mask, dscores, 0.0).astype(BF16)
        scores = mm(jnp.where(mine, fqb, 0), fkb, NT)
        scores = jnp.where(mask, scores, 0.0).astype(BF16)
        dfq = jnp.where(mine, mm(dscores, fkb), dfq)
        dfk = jnp.where(mine, mm(dscores, fqb, TN), dfk)
        dv = jnp.where(mine, mm(scores, dn_high, TN), dv)
    sums, totals = load_state(sh, scal, carry)
    more = mm(dn_high, block_diag(sums).astype(BF16), NT) + dden * totals
    dfq = dfq + jnp.where(rows.came, more, 0.0)
    fqf = fqb.astype(F32)
    used = jnp.where(rows.came, fqf, 0.0)
    store_state(sh, scal, st_out, mm(used.astype(BF16), dn_high, TN), used * dden)
    turned = mm3(dfq * fqf, ph[...], pw[...], NT)
    dq_out[0] = turn(turned, cos[0], -sin[0]).astype(BF16)
    dk_out[0] = dfk
    dv_out[0] = dv


def last_body(sh, scal, dfk, dv, fk, vals, carry, cos, sin, ph, pw, dk_out, dv_out):
    fkb = fk[0]
    sums, totals = load_state(sh, scal, carry)
    state = block_diag(sums).astype(BF16)
    goes = Rows(scal, pl.program_id(0), sh.chunk, sh.docs).goes
    more_k = mm(vals[0].astype(BF16), state, NT) + totals
    total_k = dfk[0] + jnp.where(goes, more_k, 0.0)
    dv_out[0] = (dv[0] + jnp.where(goes, mm(fkb, state), 0.0)).astype(BF16)
    turned = mm3(total_k * fkb.astype(F32), ph[...], pw[...], NT)
    dk_out[0] = turn(turned, cos[0], -sin[0]).astype(BF16)


def down_grad_body(sh, with_got, scal, act, ctx, own, away, *refs):
    half = own.shape[0]
    scratch = refs[-1]
    j = pl.program_id(0)

    @pl.when(j == 0)
    def _():
        scratch[...] = mm(ctx[:half, :].astype(BF16), own[...], TN) + mm(
            ctx[half:, :].astype(BF16), away[...], TN
        )

    grad = mm(act[:half, :], own[...], TN) + mm(act[half:, :], away[...], TN)
    low = scratch[pl.ds(pl.multiple_of(j * sh.hu, 8), sh.hu), :]
    store_block(with_got, refs[:-1], (grad, low), j)


def store_block(with_got, refs, parts, j):
    at = 0
    for part in parts:
        rows = slice(at, at + part.shape[0])
        at += part.shape[0]
        if not with_got:
            refs[0][0, rows, :] = part.astype(BF16)
            continue
        value = (part + refs[0][0, rows, :].astype(F32)).astype(BF16)
        for step, out in enumerate(refs[1:]):

            @pl.when(j == step)
            def _():
                out[rows, :] = value


def up_grad_body(sh, with_got, scal, normed, grad, *refs):
    store_block(with_got, refs, (mm(normed[...], grad[...], TN),), pl.program_id(0))


def qkv_grad_body(sh, with_got, scal, dq, dk, dv, normed, *refs):
    for kind, ref in enumerate((dq, dk, dv)):
        refs[-1][kind] = mm(ref[...], normed[...], TN)
    for j in range(sh.chunks):
        rows = slice(j * sh.hu, (j + 1) * sh.hu)
        value = jnp.concatenate([refs[-1][kind, rows, :] for kind in range(3)], axis=0)
        if with_got:
            refs[1 + j][...] = (value + refs[0][j].astype(F32)).astype(BF16)
        else:
            refs[0][j] = value.astype(BF16)


def rows_grad_body(sh, scal, dq, dk, dv, gh, own, away, g1, g2, *refs):
    count = sh.pairs * sh.chunks
    blocks_a, blocks_u = refs[:count], refs[count : 2 * count]
    own_out, away_out, sums, wt, wu, n_ref = refs[2 * count :]
    seq = pl.program_id(0)
    half = pl.num_programs(0) // 2

    @pl.when(seq == 0)
    def _():
        for kind in range(3):
            fill_rows(sh, wt, blocks_a, kind * sh.hu, sh.hu, kind * sh.width)
        for slot in range(sh.pairs):
            for j in range(sh.chunks):
                wu[slot, :, j * sh.hf : (j + 1) * sh.hf] = blocks_u[slot * sh.chunks + j][...]
        sums[...] = jnp.zeros(sums.shape, F32)

    x = jnp.where(seq < half, own[0], away[0]).astype(F32)
    n_ref[...] = normalize(x)[0]
    for slot in range(sh.pairs):
        cols = sh.cols(scal, slot)
        one = mm(dq[0], wt[slot, : sh.width, :])
        one = one + mm(dk[0], wt[slot, sh.width : 2 * sh.width, :])
        one = one + mm(dv[0], wt[slot, 2 * sh.width :, :])
        two = mm(gh[0], wu[slot], NT)
        n = n_ref[:, cols]
        for at, value in enumerate((one * n, one, two * n, two)):
            line = slice(at, at + 1)
            sums[line, cols] = sums[line, cols] + jnp.sum(value, axis=0, keepdims=True)
        e = (one * g1[:, cols] + two * g2[:, cols]).astype(BF16)

        @pl.when(seq < half)
        def _():
            own_out[0, :, cols] = e

        @pl.when(seq >= half)
        def _():
            away_out[0, :, cols] = e


def tokens_grad_body(scal, mine, got, tokens, cot, out):
    e = mine[0].astype(F32) + got[0].astype(F32)
    n, scale = normalize(tokens[0].astype(F32))
    shift = jnp.mean(e, axis=-1, keepdims=True) + n * jnp.mean(e * n, axis=-1, keepdims=True)
    out[0] = cot[0].astype(F32) + scale * (e - shift)


def cut_cols_body(scal, first, second, keep, send):
    total = (first[...].astype(F32) + second[...].astype(F32)).astype(BF16)
    half = total.shape[1] // 2
    low = scal[3] == 0
    keep[...] = jnp.where(low, total[:, :half], total[:, half:])
    send[...] = jnp.where(low, total[:, half:], total[:, :half])


def cut_rows_body(scal, first, second, keep, send):
    total = (first[...].astype(F32) + second[...].astype(F32)).astype(BF16)
    half = total.shape[0] // 2
    low = scal[3] == 0
    keep[...] = jnp.where(low, total[:half], total[half:])
    send[...] = jnp.where(low, total[half:], total[:half])


def end_down_body(sh, scal, keep, got, down, out):
    low = scal[3] == 0
    mine, other = keep[...].astype(F32), got[...].astype(F32)
    first, second = jnp.where(low, mine, other), jnp.where(low, other, mine)
    down[: sh.hf, :] = first[: sh.hf]
    down[sh.hf :, :] = second[: sh.hf]
    out[: sh.hu, :] = first[sh.hf :]
    out[sh.hu :, :] = second[sh.hf :]


def end_up_body(sh, scal, keep, got, up):
    low = scal[3] == 0
    mine, other = keep[...].astype(F32), got[...].astype(F32)
    up[:, : sh.hf] = jnp.where(low, mine, other)
    up[:, sh.hf :] = jnp.where(low, other, mine)


def end_qkv_body(sh, scal, keep, got, *outs):
    low = scal[3] == 0
    mine, other = keep[...].astype(F32), got[...].astype(F32)
    first, second = jnp.where(low, mine, other), jnp.where(low, other, mine)
    for kind, out in enumerate(outs):
        rows = slice(kind * sh.hu, (kind + 1) * sh.hu)
        out[...] = jnp.transpose(jnp.concatenate([first[rows], second[rows]], axis=0))


class Layout:
    def __init__(self):
        self.seqs, self.parts = lax.axis_size("seq"), lax.axis_size("mp")
        self.pairs, self.chunks = self.seqs // 2, self.parts // 2
        seq, part = lax.axis_index("seq"), lax.axis_index("mp")
        self.pair, self.core = seq // 2, seq % 2
        self.hi, self.lo = part // 2, part % 2

    def move(self, values, rule):
        links = []
        for seq in range(self.seqs):
            for part in range(self.parts):
                there = rule(seq // 2, seq % 2, part // 2, part % 2)
                if there is not None:
                    pair, core, hi, lo = there
                    goal = (pair * 2 + core) * self.parts + hi * 2 + lo
                    links.append((seq * self.parts + part, goal))
        return lax.ppermute(values, AXES, links)

    def core_swap(self, values):
        return self.move(values, lambda p, c, h, l: (p, 1 - c, h, l))

    def lo_swap(self, values):
        return self.move(values, lambda p, c, h, l: (p, c, h, 1 - l))

    def pair_step(self, values, way):
        return self.move(values, lambda p, c, h, l: ((p + way) % self.pairs, c, h, l))

    def hi_step(self, values, way):
        return self.move(values, lambda p, c, h, l: (p, c, (h + way) % self.chunks, l))


def gather_blocks(lay, block):
    ring = [block]
    for _ in range(lay.chunks - 1):
        ring.append(lay.hi_step(ring[-1], -1))
    blocks = list(ring)
    for _ in range(lay.pairs - 1):
        ring = [lay.pair_step(part, -1) for part in ring]
        blocks += ring
    return blocks


def combine_states(lay, local, straddles, size, backward):
    reach = local
    found = jnp.zeros_like(local)
    step = 1
    while step < lay.chunks:
        base = (lay.hi // (2 * step)) * (2 * step)
        upper = (lay.hi & step) > 0
        middle = (base + step) * size
        last = step * 2 >= lay.chunks

        def rule(p, c, h, l, step=step, last=last):
            sender = ((h & step) == 0) != backward
            return (p, c, h ^ step, l) if sender or not last else None

        got = lay.move(reach.astype(BF16), rule).astype(F32)
        scale = lambda edge: straddles(middle, edge)[:, None, None]
        if backward:
            here = (lay.hi + 1) * size
            keeps = jnp.where(upper, 0.0, scale(here))
            edge = base * size
        else:
            here = lay.hi * size
            keeps = jnp.where(upper, scale(here), 0.0)
            edge = (base + 2 * step) * size
        found = found + keeps * got
        if not last:
            far = scale(edge)
            mine_far = upper if backward else jnp.logical_not(upper)
            reach = jnp.where(mine_far, far * reach + got, reach + far * got)
        step *= 2
    return found


def erf_inverse(target):
    low, high = -6.0, 6.0
    for _ in range(60):
        middle = 0.5 * (low + high)
        low, high = (middle, high) if math.erf(middle) < target else (low, middle)
    guess = 0.5 * (low + high)
    for _ in range(3):
        gap = math.erf(guess) - target
        guess -= gap * math.exp(guess * guess) * math.sqrt(math.pi) / 2.0
    return guess


@functools.lru_cache(None)
def tables(heads):
    primes = prime_list(HEAD_DIM)
    points = np.zeros((FEATS, HEAD_DIM))
    for row in range(FEATS):
        for col in range(HEAD_DIM):
            share = min(max((row + 0.5) * math.sqrt(primes[col]) % 1.0, 0.001), 0.999)
            points[row, col] = math.sqrt(2.0) * erf_inverse(2.0 * float(np.float32(share)) - 1.0)
    cells = np.arange(HEAD_DIM)
    cosine = np.cos(np.pi * (cells[None, :] + 0.5) * cells[:, None] / HEAD_DIM)
    cosine = cosine * math.sqrt(2.0 / HEAD_DIM)
    cosine[0] *= math.sqrt(0.5)
    project = np.kron(np.eye(heads), (points @ cosine).T / math.sqrt(HEAD_DIM))
    project = project.astype(np.float32)
    high = project.astype(BF16)
    low = (project - high.astype(np.float32)).astype(BF16)
    weighting = 1.0 / (1.0 + np.sum(points * points, axis=1) / HEAD_DIM)
    return high, low, np.tile(weighting, heads)[None, :].astype(np.float32)


def team_local(
    tokens,
    ln1_gain,
    ln1_bias,
    ln2_gain,
    ln2_bias,
    q_weight,
    k_weight,
    value_weight,
    out_weight,
    up_weight,
    down_weight,
    lengths,
    cotangent,
):
    lay = Layout()
    micro, rows, dim = tokens.shape
    drows, units = q_weight.shape
    docs = lengths.shape[2]
    chunk = 2 * rows
    half_units, half_ff = units // 2, up_weight.shape[1] // 2
    sh = Shape(lay.pairs, lay.chunks, dim, half_units, half_ff, chunk, docs)
    width, ff, dp = sh.width, sh.ff, sh.dp
    count = 2 * micro
    total = count * chunk
    whole_rows = lambda array: array.reshape(total, array.shape[-1])
    bind = lambda body, *first: functools.partial(body, *first)
    gains = [vec.reshape(1, dim) for vec in (ln1_gain, ln1_bias, ln2_gain, ln2_bias)]

    own_lengths = lengths[:, 0]
    table = jnp.stack([own_lengths, lay.core_swap(own_lengths)]).reshape(count, docs)
    ends = jnp.cumsum(table, axis=1)
    starts = ends - table
    scal = jnp.concatenate(
        [
            jnp.stack([lay.pair, lay.hi, lay.lo, lay.core]).astype(jnp.int32),
            jnp.concatenate([starts, ends], axis=1).reshape(-1).astype(jnp.int32),
        ]
    )
    places = jnp.stack([lay.core, lay.core, lay.core, lay.core]).astype(jnp.int32)
    core_only = places

    block_shape = [(4 * half_units, drows), (drows, half_ff), (half_ff, drows)]
    keep_a, send_a, send_u, send_d = call(
        "pack", pack_body, core_only, (),
        [whole(w) for w in (q_weight, k_weight, value_weight, out_weight, up_weight, down_weight)],
        [whole(new(shape, BF16)) for shape in [block_shape[0]] + block_shape],
    )
    got_a = lay.core_swap(send_a)
    tokens_beside = lay.lo_swap(tokens)
    (block,) = call(
        "join_a", join_a_body, core_only, (), [whole(keep_a), whole(got_a)],
        [whole(new((4 * half_units, 2 * drows), BF16))],
    )
    blocks_a = gather_blocks(lay, block)
    got_u = lay.core_swap(send_u)
    (block,) = call(
        "join_u", join_u_body, core_only, (), [whole(up_weight), whole(got_u)],
        [whole(new((2 * drows, half_ff), BF16))],
    )
    blocks_u = gather_blocks(lay, block)
    got_d = lay.core_swap(send_d)
    (block,) = call(
        "join_d", join_d_body, core_only, (), [whole(down_weight), whole(got_d)],
        [whole(new((half_ff, 2 * drows), BF16))],
    )
    blocks_d = gather_blocks(lay, block)
    in_a, in_u, in_d = ([whole(b) for b in blocks] for blocks in (blocks_a, blocks_u, blocks_d))

    def pair_rows(values, beside):
        own = jnp.stack([values, beside], 1).reshape(micro, chunk, dim)
        return own, lay.core_swap(own)

    x_own, x_away = pair_rows(tokens, tokens_beside)
    g_own, g_away = pair_rows(cotangent, lay.lo_swap(cotangent))

    here = lay.hi * chunk
    step = jnp.arange(rows, dtype=jnp.int32)
    places = jnp.concatenate([here + lay.lo * rows + step, here + (1 - lay.lo) * rows + step])
    start = jnp.zeros((count, chunk), jnp.int32)
    for doc in range(docs):
        first = starts[:, doc : doc + 1]
        start = jnp.where(places[None, :] >= first, first, start)
    offset = (places[None, :] - start).astype(F32)
    lane = np.arange(128) % HEAD_DIM
    turned = lane < ROT
    inverse = np.where(turned, 10000.0 ** (-(lane % (ROT // 2)) * 2.0 / ROT), 0.0)
    side = np.where(turned, np.where(lane < ROT // 2, -1.0, 1.0), 0.0)
    angles = offset[:, :, None] * jnp.asarray(inverse, F32)[None, None, :]
    cos = jnp.cos(angles)
    sin = jnp.sin(angles) * jnp.asarray(side, F32)[None, None, :]
    high, low, weighting = tables(width // HEAD_DIM)
    maps = [whole(jnp.asarray(high)), whole(jnp.asarray(low))]
    turns = [by_seq(cos), by_seq(sin)]

    def straddles(first, second):
        lower, higher = jnp.minimum(first, second), jnp.maximum(first, second)
        return jnp.any((starts < lower) & (ends > higher), axis=1).astype(F32)

    rows_new = lambda size, kind: by_seq(new((count, chunk, size), kind))
    state_new = by_seq(new((count, STATE_ROWS, width), F32))
    n_one, n_two = call(
        "norms", norm_body, scal, (count,),
        [own_seq(x_own), away_seq(x_away)] + [whole(vec) for vec in gains],
        [rows_new(dim, BF16), rows_new(dim, BF16)],
    )
    fq, fk, vals, num, den, state = call(
        "attend", bind(attend_body, sh), scal, (count,),
        [by_seq(n_one)] + turns + maps + [whole(jnp.asarray(weighting))] + in_a,
        [rows_new(width, BF16)] * 2 + [rows_new(width, F32)] * 3 + [state_new],
        [pltpu.VMEM((sh.pairs, 3 * width, dp), BF16)],
    )
    carry = combine_states(lay, state, straddles, chunk, False)
    act, slope = call(
        "up", bind(up_body, sh), scal, (count,), [by_seq(n_two)] + in_u,
        [rows_new(ff, BF16)] * 2, [pltpu.VMEM((sh.pairs, dp, ff), BF16)],
    )
    out_scratch = [
        pltpu.VMEM((sh.pairs, width, dp), BF16), pltpu.VMEM((sh.pairs, ff, dp), BF16)
    ]
    halves_new = [
        own_seq(new((micro, chunk, dim), BF16)), away_seq(new((micro, chunk, dim), BF16))
    ]
    ctx, rden, own, away = call(
        "branch", bind(branch_body, sh), scal, (count,),
        [by_seq(a) for a in (num, den, fq, carry, act)] + in_a + in_d,
        [rows_new(width, F32)] * 2 + halves_new, out_scratch,
    )

    def team_sum(own, away):
        got = lay.core_swap(away)
        both = own.astype(F32) + got.astype(F32)
        return both[:, :rows], lay.lo_swap(both[:, rows:].astype(BF16))

    mine, got = team_sum(own, away)
    mixed = (tokens.astype(F32) + mine + got.astype(F32)).astype(BF16)

    (grad_hidden,) = call(
        "hidden_grad", bind(hidden_body, sh), scal, (count,),
        [own_seq(g_own), away_seq(g_away), by_seq(slope)] + in_d,
        [rows_new(ff, BF16)], [pltpu.VMEM((sh.pairs, ff, dp), BF16)],
    )
    dq, dk_part, dv_part, dstate = call(
        "attend_back", bind(back_body, sh), scal, (count,),
        [own_seq(g_own), away_seq(g_away)]
        + [by_seq(a) for a in (fq, fk, vals, ctx, rden, carry)] + turns + maps + in_a,
        [rows_new(width, BF16), rows_new(width, F32), rows_new(width, F32), state_new],
        [pltpu.VMEM((sh.pairs, width, dp), BF16)],
    )
    dcarry = combine_states(lay, dstate, straddles, chunk, True)
    dk, dv = call(
        "keys_back", bind(last_body, sh), scal, (count,),
        [by_seq(a) for a in (dk_part, dv_part, fk, vals, dcarry)] + turns + maps,
        [rows_new(width, BF16)] * 2,
    )

    def cols_of(array, slot):
        pairs = sh.pairs
        index = lambda *ids: (0, (ids[-1][0] + slot) % pairs)
        return (array, (array.shape[0], dp), index)

    def lanes_of(array, size):
        return (array, (array.shape[0], size), lambda j, s: (0, j))

    def block_of(array):
        rest = tuple(array.shape[1:])
        return (array, (1,) + rest, lambda j, s: (j,) + (0,) * len(rest))

    def scatter(name, body, shape, ins, scratch, grid):
        got = None
        for slot in range(sh.pairs - 1, -1, -1):
            stacked = new((sh.chunks,) + shape, BF16)
            take = block_of if grid else whole
            extra = [] if got is None else [take(got)]
            final = slot == 0
            outs = [whole(new(shape, BF16))] * sh.chunks if final else [take(stacked)]
            parts = call(
                name + str(slot), bind(body, sh, got is not None), scal, grid,
                ins(slot) + extra, outs, scratch,
            )
            if not final:
                got = lay.pair_step(parts[0], 1)
        term = parts[sh.chunks - 1]
        for j in range(sh.chunks - 2, -1, -1):
            term = lay.hi_step(term, 1)
            if j:
                term = (term.astype(F32) + parts[j].astype(F32)).astype(BF16)
        return term, parts[0]

    g_rows = [g.reshape(total // 2, dim) for g in (g_own, g_away)]
    grid = (sh.chunks,)
    down_ends = scatter(
        "down_grad", down_grad_body, (half_ff + half_units, dp),
        lambda slot: [lanes_of(whole_rows(act), half_ff), whole(whole_rows(ctx))]
        + [cols_of(g, slot) for g in g_rows],
        [pltpu.VMEM((width, dp), F32)], grid,
    )
    up_ends = scatter(
        "up_grad", up_grad_body, (dp, half_ff),
        lambda slot: [cols_of(whole_rows(n_two), slot), lanes_of(whole_rows(grad_hidden), half_ff)],
        [], grid,
    )
    qkv_ends = scatter(
        "qkv_grad", qkv_grad_body, (3 * half_units, dp),
        lambda slot: [whole(whole_rows(a)) for a in (dq, dk, dv)]
        + [cols_of(whole_rows(n_one), slot)],
        [pltpu.VMEM((3, width, dp), F32)], (),
    )

    own, away, sums = call(
        "rows_grad", bind(rows_grad_body, sh), scal, (count,),
        [by_seq(a) for a in (dq, dk, dv, grad_hidden)] + [own_seq(x_own), away_seq(x_away)]
        + [whole(gains[0]), whole(gains[2])] + in_a + in_u,
        halves_new + [whole(new((8, dim), F32))],
        [
            pltpu.VMEM((sh.pairs, 3 * width, dp), BF16),
            pltpu.VMEM((sh.pairs, dp, ff), BF16),
            pltpu.VMEM((chunk, dim), F32),
        ],
    )
    mine, got = team_sum(own, away)
    (grad_tokens,) = call(
        "tokens_grad", tokens_grad_body, scal, (micro,),
        [by_seq(a) for a in (mine, got, tokens, cotangent)],
        [by_seq(new((micro, rows, dim), F32))],
    )
    sums = sums[:4]
    sums = sums + lay.core_swap(sums)
    sums = sums + lay.lo_swap(sums)
    step = 1
    while step < lay.pairs:
        sums = sums + lay.move(sums, lambda p, c, h, l, step=step: (p ^ step, c, h, l))
        step *= 2
    step = 1
    while step < lay.chunks:
        sums = sums + lay.move(sums, lambda p, c, h, l, step=step: (p, c, h ^ step, l))
        step *= 2

    def trade(name, body, ends, shape):
        keep, send = call(
            name, body, core_only, (), [whole(part) for part in ends],
            [whole(new(shape, BF16))] * 2,
        )
        return [whole(keep), whole(lay.core_swap(send))]

    grad_down, grad_out = call(
        "end_down", bind(end_down_body, sh), core_only, (),
        trade("cut_down", cut_cols_body, down_ends, (half_ff + half_units, drows)),
        [whole(new(down_weight.shape, F32)), whole(new(out_weight.shape, F32))],
    )
    (grad_up,) = call(
        "end_up", bind(end_up_body, sh), core_only, (),
        trade("cut_up", cut_rows_body, up_ends, (drows, half_ff)),
        [whole(new(up_weight.shape, F32))],
    )
    grads = call(
        "end_qkv", bind(end_qkv_body, sh), core_only, (),
        trade("cut_qkv", cut_cols_body, qkv_ends, (3 * half_units, drows)),
        [whole(new(q_weight.shape, F32))] * 3,
    )
    return (
        mixed,
        grad_tokens,
        sums[0],
        sums[1],
        sums[2],
        sums[3],
        grads[0],
        grads[1],
        grads[2],
        grad_out,
        grad_up,
        grad_down,
    )


def solution(mesh):
    seqs, parts = mesh.shape["seq"], mesh.shape["mp"]

    def body(*args):
        units = args[5].shape[1]
        teams = seqs % 2 == 0 and parts % 2 == 0 and (units // HEAD_DIM) % 2 == 0
        chunks = parts // 2
        if teams and chunks & (chunks - 1) == 0 and parts * units == 16 * HEAD_DIM:
            return team_local(*args)
        return plain_local(*args)

    in_specs = (
        P(None, ("seq", "mp"), None),
        P(),
        P(),
        P(),
        P(),
        P("seq", "mp"),
        P("seq", "mp"),
        P("seq", "mp"),
        P("mp", "seq"),
        P("seq", "mp"),
        P("mp", "seq"),
        P(None, "seq", None),
        P(None, ("seq", "mp"), None),
    )
    out_specs = (
        P(None, ("seq", "mp"), None),
        P(None, ("seq", "mp"), None),
        P(),
        P(),
        P(),
        P(),
        P("seq", "mp"),
        P("seq", "mp"),
        P("seq", "mp"),
        P("mp", "seq"),
        P("seq", "mp"),
        P("mp", "seq"),
    )
    return jax.shard_map(body, mesh=mesh, in_specs=in_specs, out_specs=out_specs, check_vma=False)
```

```python
import functools
import math

import jax
import jax.numpy as jnp
import numpy as np
from jax import lax
from jax.experimental import pallas as pl
from jax.experimental.pallas import tpu as pltpu
from jax.sharding import PartitionSpec as P

HEAD_DIM = 64
ROT = 16
FEATS = 64
STATE_ROWS = 80
AXES = ("seq", "mp")
BF16 = jnp.bfloat16
F32 = jnp.float32
VMEM_LIMIT = 56 * 1024 * 1024
NN = (((1,), (0,)), ((), ()))
NT = (((1,), (1,)), ((), ()))
TN = (((0,), (0,)), ((), ()))


def prime_list(wanted):
    found_primes = []
    candidate = 2
    while len(found_primes) < wanted:
        if all((candidate % earlier != 0 for earlier in found_primes)):
            found_primes.append(candidate)
        candidate += 1
    return found_primes


def feature_maps(head_width, feature_count):
    primes_found = prime_list(head_width)
    uniform_rows = [
        [
            min(max((row_idx + 0.5) * math.sqrt(prime_val) % 1.0, 0.001), 0.999)
            for prime_val in primes_found
        ]
        for row_idx in range(feature_count)
    ]
    uniform_pts = jnp.asarray(uniform_rows, jnp.float32)
    points = math.sqrt(2.0) * lax.erf_inv(2.0 * uniform_pts - 1.0)
    cosine_rows = [
        [
            math.sqrt(2.0 / head_width)
            * math.cos(math.pi * (cell_idx + 0.5) * freq_idx / head_width)
            * (math.sqrt(0.5) if freq_idx == 0 else 1.0)
            for cell_idx in range(head_width)
        ]
        for freq_idx in range(head_width)
    ]
    cosine = jnp.asarray(cosine_rows, jnp.float32)
    project = jnp.dot(points, cosine, precision=lax.Precision.HIGHEST)
    project = jnp.transpose(project) * (1.0 / math.sqrt(head_width))
    weighting = 1.0 / (1.0 + jnp.sum(points * points, axis=1) / head_width)
    return (project, weighting)


def rotate_heads(values, offset):
    half_dims = ROT // 2
    inverse = 10000.0 ** (-jnp.arange(half_dims, dtype=jnp.float32) * 2.0 / ROT)
    angles = offset[:, None] * inverse[None, :]
    cosine = jnp.cos(angles)[None, :, :]
    sine_part = jnp.sin(angles)[None, :, :]
    first_half = values[..., :half_dims]
    second = values[..., half_dims:ROT]
    return jnp.concatenate(
        [
            first_half * cosine - second * sine_part,
            second * cosine + first_half * sine_part,
            values[..., ROT:],
        ],
        axis=-1,
    )


def layer_norm(values, gain_vec, bias_vec):
    centered = values - jnp.mean(values, axis=-1, keepdims=True)
    variance = jnp.mean(centered * centered, axis=-1, keepdims=True)
    return centered * lax.rsqrt(variance + 1e-05) * gain_vec + bias_vec


def exact_gelu(values):
    return jax.nn.gelu(values, approximate=False)


def doc_layout(doc_lengths, number_of_tokens):
    doc_ends = jnp.cumsum(doc_lengths).astype(jnp.int32)
    starts = (doc_ends - doc_lengths).astype(jnp.int32)
    places = jnp.arange(number_of_tokens, dtype=jnp.int32)
    segment = jnp.sum((places[:, None] >= doc_ends[None, :]).astype(jnp.int32), axis=1).astype(
        jnp.int32
    )
    member = segment[:, None] == jnp.arange(doc_lengths.shape[0], dtype=jnp.int32)[None, :]
    offset = places - jnp.sum(jnp.where(member, starts[None, :], 0), axis=1).astype(jnp.int32)
    return (segment, offset.astype(jnp.float32))


def contract_rows(left_side, right_side):
    return lax.dot_general(
        left_side, right_side, (((0,), (0,)), ((), ())), preferred_element_type=jnp.float32
    )


def contract_cols(left_side, right_side):
    return lax.dot_general(
        left_side, right_side, (((1,), (1,)), ((), ())), preferred_element_type=jnp.float32
    )


def local_attention(plain_query_rows, key_raw, value_raw, segment, offset, project, weighting):
    maximal_precision_mode = lax.Precision.HIGHEST
    number_of_tokens = plain_query_rows.shape[0]
    head_count = plain_query_rows.shape[1] // HEAD_DIM

    def heads_first(values):
        return jnp.transpose(values.reshape(number_of_tokens, head_count, HEAD_DIM), (1, 0, 2))

    rot_query = rotate_heads(heads_first(plain_query_rows), offset)
    rot_key = rotate_heads(heads_first(key_raw), offset)
    value_heads = heads_first(value_raw)
    feat_query = (
        jnp.exp(jnp.einsum("htd,df->htf", rot_query, project, precision=maximal_precision_mode))
        * weighting
    )
    feat_key = jnp.exp(
        jnp.einsum("htd,df->htf", rot_key, project, precision=maximal_precision_mode)
    )
    rows_per_block = min(512, number_of_tokens)
    block_count = number_of_tokens // rows_per_block

    def split_blocks(values):
        return jnp.transpose(
            values.reshape((head_count, block_count, rows_per_block, values.shape[2])), (1, 0, 2, 3)
        )

    def block_step(carry, pieces):
        kv_state, totals, previous = carry
        block_of_queries, block_of_keys, value_block, block_segment = pieces
        places = jnp.arange(block_segment.shape[0], dtype=jnp.int32)
        attention_scores = jnp.einsum(
            "ugy,uky->ugk", block_of_queries, block_of_keys, precision=maximal_precision_mode
        )
        allowed = (places[:, None] >= places[None, :]) & (
            block_segment[:, None] == block_segment[None, :]
        )
        attention_scores = jnp.where(allowed[None, :, :], attention_scores, 0.0)
        numerator = jnp.einsum(
            "hqk,hkd->hqd", attention_scores, value_block, precision=maximal_precision_mode
        )
        denominator = jnp.sum(attention_scores, axis=2)
        carried_in = (block_segment == previous)[None, :]
        numerator = numerator + jnp.where(
            carried_in[:, :, None],
            jnp.einsum(
                "hqf,hfd->hqd", block_of_queries, kv_state, precision=maximal_precision_mode
            ),
            0.0,
        )
        denominator = denominator + jnp.where(
            carried_in,
            jnp.einsum("hqf,hf->hq", block_of_queries, totals, precision=maximal_precision_mode),
            0.0,
        )
        final_output = block_segment[-1]
        carried_over = final_output == previous
        trailing_mask = (block_segment == final_output).astype(jnp.float32)
        new_state = jnp.where(carried_over, kv_state, 0.0) + jnp.einsum(
            "hrf,hrd,r->hfd",
            block_of_keys,
            value_block,
            trailing_mask,
            precision=maximal_precision_mode,
        )
        new_totals = jnp.where(carried_over, totals, 0.0) + jnp.einsum(
            "hrf,r->hf", block_of_keys, trailing_mask, precision=maximal_precision_mode
        )
        return ((new_state, new_totals, final_output), numerator / denominator[:, :, None])

    start_carry = (
        jnp.zeros((head_count, FEATS, HEAD_DIM), jnp.float32),
        jnp.zeros((head_count, FEATS), jnp.float32),
        jnp.array(-1, jnp.int32),
    )
    _, outputs = lax.scan(
        jax.checkpoint(block_step),
        start_carry,
        (
            split_blocks(feat_query),
            split_blocks(feat_key),
            split_blocks(value_heads),
            segment.reshape(block_count, rows_per_block),
        ),
    )
    joined = jnp.transpose(outputs, (1, 0, 2, 3)).reshape(head_count, number_of_tokens, HEAD_DIM)
    return jnp.transpose(joined, (1, 0, 2)).reshape(number_of_tokens, head_count * HEAD_DIM)


def plain_local(
    tokens,
    ln1_gain,
    ln1_bias,
    ln2_gain,
    ln2_bias,
    q_weight,
    k_weight,
    value_weight,
    out_weight,
    up_weight,
    down_weight,
    lengths,
    cotangent,
):
    micro_count = tokens.shape[0]
    local_rows = tokens.shape[1]
    group_rows = local_rows * lax.axis_size("mp")
    seq_count = lax.axis_size("seq")
    project, weighting = feature_maps(HEAD_DIM, FEATS)
    grad_sums = [
        jnp.zeros((q_weight.shape[0] * seq_count, q_weight.shape[1]), jnp.float32),
        jnp.zeros((k_weight.shape[0] * seq_count, k_weight.shape[1]), jnp.float32),
        jnp.zeros((value_weight.shape[0] * seq_count, value_weight.shape[1]), jnp.float32),
        jnp.zeros((out_weight.shape[0], out_weight.shape[1] * seq_count), jnp.float32),
        jnp.zeros((up_weight.shape[0] * seq_count, up_weight.shape[1]), jnp.float32),
        jnp.zeros((down_weight.shape[0], down_weight.shape[1] * seq_count), jnp.float32),
    ]
    norm_sums = [
        jnp.zeros_like(ln1_gain),
        jnp.zeros_like(ln1_bias),
        jnp.zeros_like(ln2_gain),
        jnp.zeros_like(ln2_bias),
    ]
    mixed_parts = []
    grad_parts = []
    for micro_step in range(micro_count):
        full_weights = (
            lax.all_gather(q_weight, "seq", axis=0, tiled=True),
            lax.all_gather(k_weight, "seq", axis=0, tiled=True),
            lax.all_gather(value_weight, "seq", axis=0, tiled=True),
            lax.all_gather(out_weight, "seq", axis=1, tiled=True),
            lax.all_gather(up_weight, "seq", axis=0, tiled=True),
            lax.all_gather(down_weight, "seq", axis=1, tiled=True),
        )
        w_query, w_key, w_value, w_out, w_up, w_down = full_weights
        rows_in = tokens[micro_step].astype(jnp.float32)
        normed_one, pull_one = jax.vjp(layer_norm, rows_in, ln1_gain, ln1_bias)
        normed_two, pull_two = jax.vjp(layer_norm, rows_in, ln2_gain, ln2_bias)
        group_one, group_two = (
            lax.all_gather(normed_one.astype(jnp.bfloat16), "mp", axis=0, tiled=True),
            lax.all_gather(normed_two.astype(jnp.bfloat16), "mp", axis=0, tiled=True),
        )
        plain_query_rows = jnp.dot(group_one, w_query, preferred_element_type=jnp.float32)
        key_raw = jnp.dot(group_one, w_key, preferred_element_type=jnp.float32)
        value_raw = jnp.dot(group_one, w_value, preferred_element_type=jnp.float32)
        segment, offset = doc_layout(lengths[micro_step, 0], group_rows)
        attend = functools.partial(
            local_attention, segment=segment, offset=offset, project=project, weighting=weighting
        )
        context, pull_attn = jax.vjp(attend, plain_query_rows, key_raw, value_raw)
        context_low = context.astype(jnp.bfloat16)
        hidden = jnp.dot(group_two, w_up, preferred_element_type=jnp.float32)
        activated, pull_gelu = jax.vjp(exact_gelu, hidden)
        activated_low = activated.astype(jnp.bfloat16)
        context_rows = lax.slice_in_dim(context_low, 0, lax.axis_size("mp") * local_rows, axis=0)
        active_rows = lax.slice_in_dim(activated_low, 0, lax.axis_size("mp") * local_rows, axis=0)
        branch_sum = lax.psum_scatter(
            jnp.dot(context_rows, w_out, preferred_element_type=jnp.float32)
            + jnp.dot(active_rows, w_down, preferred_element_type=jnp.float32),
            "mp",
            scatter_dimension=0,
            tiled=True,
        )
        mixed_parts.append((rows_in + branch_sum).astype(jnp.bfloat16))
        grad_group = lax.all_gather(cotangent[micro_step], "mp", axis=0, tiled=True)
        grad_context = contract_cols(grad_group, w_out)
        grad_activated = contract_cols(grad_group, w_down)
        grad_hidden = pull_gelu(grad_activated)[0].astype(jnp.bfloat16)
        grad_query_f, grad_key_f, grad_value_f = pull_attn(grad_context)
        grad_query = grad_query_f.astype(jnp.bfloat16)
        grad_key = grad_key_f.astype(jnp.bfloat16)
        grad_value = grad_value_f.astype(jnp.bfloat16)
        micro_grads = (
            contract_rows(group_one, grad_query),
            contract_rows(group_one, grad_key),
            contract_rows(group_one, grad_value),
            contract_rows(context_low, grad_group),
            contract_rows(group_two, grad_hidden),
            contract_rows(activated_low, grad_group),
        )
        grad_sums = [total + term for total, term in zip(grad_sums, micro_grads)]
        part_one = (
            contract_cols(grad_query, w_query)
            + contract_cols(grad_key, w_key)
            + contract_cols(grad_value, w_value)
        )
        part_two = contract_cols(grad_hidden, w_up)
        sum_one, sum_two = (
            lax.psum_scatter(
                part_one.astype(jnp.bfloat16), "mp", scatter_dimension=0, tiled=True
            ).astype(jnp.float32),
            lax.psum_scatter(
                part_two.astype(jnp.bfloat16), "mp", scatter_dimension=0, tiled=True
            ).astype(jnp.float32),
        )
        grad_in_one, grad_gain_one, grad_bias_one = pull_one(sum_one)
        grad_in_two, grad_gain_two, grad_bias_two = pull_two(sum_two)
        grad_parts.append(cotangent[micro_step].astype(jnp.float32) + grad_in_one + grad_in_two)
        norm_sums = [
            norm_sums[0] + grad_gain_one,
            norm_sums[1] + grad_bias_one,
            norm_sums[2] + grad_gain_two,
            norm_sums[3] + grad_bias_two,
        ]
    weight_grads = (
        lax.psum_scatter(
            grad_sums[0].astype(jnp.bfloat16), "seq", scatter_dimension=0, tiled=True
        ).astype(jnp.float32),
        lax.psum_scatter(
            grad_sums[1].astype(jnp.bfloat16), "seq", scatter_dimension=0, tiled=True
        ).astype(jnp.float32),
        lax.psum_scatter(
            grad_sums[2].astype(jnp.bfloat16), "seq", scatter_dimension=0, tiled=True
        ).astype(jnp.float32),
        lax.psum_scatter(
            grad_sums[3].astype(jnp.bfloat16), "seq", scatter_dimension=1, tiled=True
        ).astype(jnp.float32),
        lax.psum_scatter(
            grad_sums[4].astype(jnp.bfloat16), "seq", scatter_dimension=0, tiled=True
        ).astype(jnp.float32),
        lax.psum_scatter(
            grad_sums[5].astype(jnp.bfloat16), "seq", scatter_dimension=1, tiled=True
        ).astype(jnp.float32),
    )
    norm_grads = lax.psum((norm_sums[0], norm_sums[1], norm_sums[2], norm_sums[3]), ("seq", "mp"))
    return (
        jnp.stack(mixed_parts),
        jnp.stack(grad_parts),
        norm_grads[0],
        norm_grads[1],
        norm_grads[2],
        norm_grads[3],
        weight_grads[0],
        weight_grads[1],
        weight_grads[2],
        weight_grads[3],
        weight_grads[4],
        weight_grads[5],
    )


def mm(left, right, dims=NN):
    return lax.dot_general(left, right, dims, preferred_element_type=F32)


def split(values):
    high = values.astype(BF16)
    return high, (values - high.astype(F32)).astype(BF16)


def mm3(values, high, low, dims=NN):
    first, second = split(values)
    return mm(first, high, dims) + (mm(second, high, dims) + mm(first, low, dims))


def lane_head(shape):
    return lax.broadcasted_iota(jnp.int32, shape, len(shape) - 1) // HEAD_DIM


def block_diag(state):
    width = state.shape[1]
    tall = jnp.concatenate([state] * (width // HEAD_DIM), axis=0)
    rows = lax.broadcasted_iota(jnp.int32, tall.shape, 0) // HEAD_DIM
    return jnp.where(rows == lane_head(tall.shape), tall, 0.0)


def diag_blocks(full):
    width = full.shape[1]
    lanes = lane_head((HEAD_DIM, width))
    total = jnp.zeros((HEAD_DIM, width), F32)
    for head in range(width // HEAD_DIM):
        part = full[head * HEAD_DIM : (head + 1) * HEAD_DIM, :]
        total = total + jnp.where(lanes == head, part, 0.0)
    return total


def head_sums(values):
    width = values.shape[1]
    rows = lax.broadcasted_iota(jnp.int32, (width, width), 0) // HEAD_DIM
    ones = jnp.where(rows == lane_head((width, width)), 1.0, 0.0).astype(BF16)
    high, low = split(values)
    return mm(high, ones) + mm(low, ones)


def swap_halves(values):
    width = values.shape[1]
    half = ROT // 2
    lane = lax.broadcasted_iota(jnp.int32, values.shape, 1) % HEAD_DIM
    return jnp.where(
        lane < half, pltpu.roll(values, width - half, 1), pltpu.roll(values, half, 1)
    )


def turn(values, cos, sin):
    reps = values.shape[1] // cos.shape[1]
    cosw = jnp.concatenate([cos] * reps, axis=1)
    sinw = jnp.concatenate([sin] * reps, axis=1)
    return values * cosw + swap_halves(values) * sinw


def normalize(values):
    centered = values - jnp.mean(values, axis=-1, keepdims=True)
    variance = jnp.mean(centered * centered, axis=-1, keepdims=True)
    scale = lax.rsqrt(variance + 1e-05)
    return centered * scale, scale


class Rows:
    def __init__(self, scal, seq, chunk, docs):
        rows = chunk // 2
        self.here = (scal[1] * 2 + (scal[2] // 2 + seq) % 2) * chunk
        side = scal[2] % 2
        low = self.here + side * rows
        high = self.here + (1 - side) * rows - rows

        def places(shape, axis):
            count = lax.broadcasted_iota(jnp.int32, shape, axis)
            return jnp.where(count < rows, count + low, count + high)

        self.place = places((chunk, 1), 0)
        self.across = places((1, chunk), 1)
        self.start = jnp.zeros((chunk, 1), jnp.int32)
        end = jnp.zeros((chunk, 1), jnp.int32)
        base = 4 + seq * 2 * docs
        for doc in range(docs):
            first, last = scal[base + doc], scal[base + docs + doc]
            inside = (self.place >= first) & (self.place < last)
            self.start = jnp.where(inside, first, self.start)
            end = jnp.where(inside, last, end)
        self.came = self.start < self.here
        self.goes = end > self.here + chunk

    def mask(self):
        return (self.across >= self.start) & (self.across <= self.place)


def whole(array):
    zeros = (0,) * array.ndim
    return (array, tuple(array.shape), lambda *_: zeros)


def by_seq(array):
    rest = (0,) * (array.ndim - 1)
    return (array, (1,) + tuple(array.shape[1:]), lambda i, s: (i,) + rest)


def own_seq(array):
    rest, most = (0,) * (array.ndim - 1), array.shape[0] - 1
    return (array, (1,) + tuple(array.shape[1:]), lambda i, s: (jnp.minimum(i, most),) + rest)


def away_seq(array):
    rest, count = (0,) * (array.ndim - 1), array.shape[0]
    return (
        array, (1,) + tuple(array.shape[1:]), lambda i, s: (jnp.maximum(i - count, 0),) + rest
    )


def new(shape, kind):
    return jax.ShapeDtypeStruct(shape, kind)


def call(name, body, scal, grid, ins, outs, scratch=(), aliases=None):
    return pl.pallas_call(
        body,
        name=name,
        grid_spec=pltpu.PrefetchScalarGridSpec(
            num_scalar_prefetch=1,
            grid=grid or (1,),
            in_specs=[
                pl.BlockSpec(block, index) if index else pl.BlockSpec(memory_space=pl.ANY)
                for _, block, index in ins
            ],
            out_specs=[pl.BlockSpec(block, index) for _, block, index in outs],
            scratch_shapes=list(scratch),
        ),
        out_shape=[array for array, _, _ in outs],
        input_output_aliases=aliases or {},
        compiler_params=pltpu.CompilerParams(
            dimension_semantics=("arbitrary",) * max(len(grid), 1), vmem_limit_bytes=VMEM_LIMIT
        ),
    )(scal, *[array for array, _, _ in ins])


class Shape:
    def __init__(self, pairs, chunks, dim, half_units, half_ff, chunk, docs):
        self.pairs, self.chunks, self.dim = pairs, chunks, dim
        self.hu, self.hf, self.chunk, self.docs = half_units, half_ff, chunk, docs
        self.dp = dim // pairs
        self.width, self.ff = chunks * half_units, chunks * half_ff

    def cols(self, scal, slot):
        start = ((scal[0] + slot) % self.pairs) * self.dp
        return pl.ds(pl.multiple_of(start, 128), self.dp)


def fill_rows(sh, target, blocks, first, size, at):
    for slot in range(sh.pairs):
        for j in range(sh.chunks):
            part = blocks[slot * sh.chunks + j][first : first + size, :]
            target[slot, at + j * size : at + (j + 1) * size, :] = part


def pack_body(scal, q, k, v, out, up, down, keep_a, send_a, send_u, send_d):
    low = scal[3] == 0
    parts_keep, parts_send = [], []
    for ref in (q, k, v):
        flat = jnp.transpose(ref[...].astype(F32))
        half = flat.shape[0] // 2
        parts_keep.append(jnp.where(low, flat[:half], flat[half:]))
        parts_send.append(jnp.where(low, flat[half:], flat[:half]))
    flat = out[...].astype(F32)
    half = flat.shape[0] // 2
    parts_keep.append(jnp.where(low, flat[:half], flat[half:]))
    parts_send.append(jnp.where(low, flat[half:], flat[:half]))
    keep_a[...] = jnp.concatenate(parts_keep, 0).astype(BF16)
    send_a[...] = jnp.concatenate(parts_send, 0).astype(BF16)
    half = up.shape[1] // 2
    send_u[...] = jnp.where(low, up[:, half:], up[:, :half])
    half = down.shape[0] // 2
    send_d[...] = jnp.where(low, down[half:, :], down[:half, :])


def norm_body(scal, rows, g1, b1, g2, b2, *refs):
    one, two = refs[-2:]
    n, _ = normalize(rows[0].astype(F32))
    one[0] = (n * g1[...] + b1[...]).astype(BF16)
    two[0] = (n * g2[...] + b2[...]).astype(BF16)


def attend_body(sh, scal, normed, cos, sin, ph, pw, wts, *refs):
    blocks = refs[: sh.pairs * sh.chunks]
    fq_out, fk_out, v_out, num_out, den_out, st_out, wt = refs[sh.pairs * sh.chunks :]
    width, seq = sh.width, pl.program_id(0)

    @pl.when(seq == 0)
    def _():
        for kind in range(3):
            fill_rows(sh, wt, blocks, kind * sh.hu, sh.hu, kind * width)

    qkv = mm(normed[0, :, sh.cols(scal, 0)], wt[0], NT)
    for slot in range(1, sh.pairs):
        qkv = qkv + mm(normed[0, :, sh.cols(scal, slot)], wt[slot], NT)

    def feats(values):
        return jnp.exp(mm3(turn(values, cos[0], sin[0]), ph[...], pw[...]))

    fqb = (feats(qkv[:, :width]) * wts[...]).astype(BF16)
    fk = feats(qkv[:, width : 2 * width])
    fkb = fk.astype(BF16)
    v = qkv[:, 2 * width :]
    vb = v.astype(BF16)
    fq_out[0] = fqb
    fk_out[0] = fkb
    v_out[0] = v
    rows = Rows(scal, seq, sh.chunk, sh.docs)
    mask = rows.mask()
    lanes = lane_head(vb.shape)
    num = jnp.zeros(vb.shape, F32)
    den = jnp.zeros(vb.shape, F32)
    for head in range(width // HEAD_DIM):
        mine = lanes == head
        scores = mm(jnp.where(mine, fqb, 0), fkb, NT)
        scores = jnp.where(mask, scores, 0.0).astype(BF16)
        both = mm(scores, jnp.where(mine, vb, 1))
        num = jnp.where(mine, both, num)
        den = jnp.where(mine, pltpu.roll(both, HEAD_DIM, 1), den)
    num_out[0] = num
    den_out[0] = den
    kept = jnp.where(rows.goes, fk, 0.0)
    store_state(sh, scal, st_out, mm(kept.astype(BF16), vb, TN), kept)


def store_state(sh, scal, st_out, sums, totals):
    tail = jnp.broadcast_to(
        jnp.sum(totals, axis=0, keepdims=True), (STATE_ROWS - HEAD_DIM, sh.width)
    )
    state = jnp.concatenate([diag_blocks(sums), tail], axis=0)
    st_out[0] = pltpu.roll(state, scal[1] * sh.hu, 1).astype(BF16)


def load_state(sh, scal, carry):
    state = pltpu.roll(carry[0], (sh.width - scal[1] * sh.hu) % sh.width, 1)
    return state[:HEAD_DIM], state[HEAD_DIM : HEAD_DIM + 1]


def up_body(sh, scal, normed, *refs):
    blocks = refs[: sh.pairs * sh.chunks]
    act_out, slope_out, wu = refs[sh.pairs * sh.chunks :]

    @pl.when(pl.program_id(0) == 0)
    def _():
        for slot in range(sh.pairs):
            for j in range(sh.chunks):
                wu[slot, :, j * sh.hf : (j + 1) * sh.hf] = blocks[slot * sh.chunks + j][...]

    hidden = mm(normed[0, :, sh.cols(scal, 0)], wu[0])
    for slot in range(1, sh.pairs):
        hidden = hidden + mm(normed[0, :, sh.cols(scal, slot)], wu[slot])
    cdf = 0.5 + 0.5 * lax.erf(hidden * math.sqrt(0.5))
    act_out[0] = (hidden * cdf).astype(BF16)
    bell = jnp.exp(-0.5 * hidden * hidden) * math.sqrt(0.5 / math.pi)
    slope_out[0] = (cdf + hidden * bell).astype(BF16)


def finish_body(sh, scal, num, den, fq, carry, ctx_out, rden_out):
    fqb = fq[0]
    sums, totals = load_state(sh, scal, carry)
    more_num = mm(fqb, block_diag(sums).astype(BF16))
    more_den = head_sums(fqb.astype(F32) * totals)
    came = Rows(scal, pl.program_id(0), sh.chunk, sh.docs).came
    inverse = 1.0 / (den[0] + jnp.where(came, more_den, 0.0))
    ctx_out[0] = (num[0] + jnp.where(came, more_num, 0.0)) * inverse
    rden_out[0] = inverse


def branch_body(sh, scal, ctx, act, *refs):
    count = sh.pairs * sh.chunks
    blocks_a, blocks_d = refs[:count], refs[count : 2 * count]
    own_out, away_out, wo, wd = refs[2 * count :]
    seq = pl.program_id(0)

    @pl.when(seq == 0)
    def _():
        fill_rows(sh, wo, blocks_a, 3 * sh.hu, sh.hu, 0)
        fill_rows(sh, wd, blocks_d, 0, sh.hf, 0)

    ctxb = ctx[0].astype(BF16)
    half = pl.num_programs(0) // 2
    for slot in range(sh.pairs):
        part = (mm(act[0], wd[slot]) + mm(ctxb, wo[slot])).astype(BF16)

        @pl.when(seq < half)
        def _():
            own_out[0, :, sh.cols(scal, slot)] = part

        @pl.when(seq >= half)
        def _():
            away_out[0, :, sh.cols(scal, slot)] = part


def pick(own, away, scal, sh, slot):
    first = pl.program_id(0) < pl.num_programs(0) // 2
    cols = sh.cols(scal, slot)
    return jnp.where(first, own[0, :, cols], away[0, :, cols])


def hidden_body(sh, scal, own, away, slope, *refs):
    blocks = refs[: sh.pairs * sh.chunks]
    out, wd = refs[sh.pairs * sh.chunks :]

    @pl.when(pl.program_id(0) == 0)
    def _():
        fill_rows(sh, wd, blocks, 0, sh.hf, 0)

    grad = mm(pick(own, away, scal, sh, 0), wd[0], NT)
    for slot in range(1, sh.pairs):
        grad = grad + mm(pick(own, away, scal, sh, slot), wd[slot], NT)
    out[0] = (grad * slope[0].astype(F32)).astype(BF16)


def back_body(sh, scal, own, away, fq, fk, vals, ctx, rden, carry, cos, sin, ph, pw, *refs):
    blocks = refs[: sh.pairs * sh.chunks]
    dq_out, dk_out, dv_out, st_out, wo = refs[sh.pairs * sh.chunks :]
    width, seq = sh.width, pl.program_id(0)

    @pl.when(seq == 0)
    def _():
        fill_rows(sh, wo, blocks, 3 * sh.hu, sh.hu, 0)

    gctx = mm(pick(own, away, scal, sh, 0), wo[0], NT)
    for slot in range(1, sh.pairs):
        gctx = gctx + mm(pick(own, away, scal, sh, slot), wo[slot], NT)
    inverse = rden[0]
    dnum = gctx * inverse
    dden = -head_sums(gctx * ctx[0]) * inverse
    fqb, fkb, v = fq[0], fk[0], vals[0]
    rows = Rows(scal, seq, sh.chunk, sh.docs)
    mask = rows.mask()
    lanes = lane_head(v.shape)
    lane = lax.broadcasted_iota(jnp.int32, v.shape, 1) % HEAD_DIM
    dn_high, dn_low = split(dnum)
    v_high, v_low = split(v)
    dd_high = dden.astype(BF16).astype(F32)
    roll = lambda values: pltpu.roll(values.astype(F32), HEAD_DIM, 1).astype(BF16)
    den_part = jnp.where(lane == 0, dd_high, jnp.where(lane == 1, dden - dd_high, 0.0))
    den_part = den_part.astype(BF16)
    dn_high_beside, dn_low_beside = roll(dn_high), roll(dn_low)
    v_high_beside, v_low_beside = roll(v_high), roll(v_low)

    dfq = jnp.zeros(v.shape, F32)
    dfk = jnp.zeros(v.shape, F32)
    dv = jnp.zeros(v.shape, F32)
    for head in range(width // HEAD_DIM):
        mine = lanes == head
        left = [jnp.where(mine, dn_high, dn_low_beside), jnp.where(mine, den_part, dn_high_beside)]
        right = [jnp.where(mine, v_high, v_high_beside), jnp.where(mine, 1, v_low_beside)]
        dscores = mm(jnp.concatenate(left, axis=1), jnp.concatenate(right, axis=1), NT)
        dscores = jnp.where(mask, dscores, 0.0).astype(BF16)
        scores = mm(jnp.where(mine, fqb, 0), fkb, NT)
        scores = jnp.where(mask, scores, 0.0).astype(BF16)
        dfq = jnp.where(mine, mm(dscores, fkb), dfq)
        dfk = jnp.where(mine, mm(dscores, fqb, TN), dfk)
        dv = jnp.where(mine, mm(scores, dn_high, TN), dv)
    sums, totals = load_state(sh, scal, carry)
    more = mm(dn_high, block_diag(sums).astype(BF16), NT) + dden * totals
    dfq = dfq + jnp.where(rows.came, more, 0.0)
    fqf = fqb.astype(F32)
    used = jnp.where(rows.came, fqf, 0.0)
    store_state(sh, scal, st_out, mm(used.astype(BF16), dn_high, TN), used * dden)
    turned = mm3(dfq * fqf, ph[...], pw[...], NT)
    dq_out[0] = turn(turned, cos[0], -sin[0]).astype(BF16)
    dk_out[0] = dfk
    dv_out[0] = dv


def last_body(sh, scal, dfk, dv, fk, vals, carry, cos, sin, ph, pw, dk_out, dv_out):
    fkb = fk[0]
    sums, totals = load_state(sh, scal, carry)
    state = block_diag(sums).astype(BF16)
    goes = Rows(scal, pl.program_id(0), sh.chunk, sh.docs).goes
    more_k = mm(vals[0].astype(BF16), state, NT) + totals
    total_k = dfk[0] + jnp.where(goes, more_k, 0.0)
    dv_out[0] = (dv[0] + jnp.where(goes, mm(fkb, state), 0.0)).astype(BF16)
    turned = mm3(total_k * fkb.astype(F32), ph[...], pw[...], NT)
    dk_out[0] = turn(turned, cos[0], -sin[0]).astype(BF16)


def unit_grad_body(with_got, scal, left, *refs):
    many, with_got = with_got
    rights, refs = refs[:many], refs[many:]
    at, grad = 0, None
    for right in rights:
        part = mm(left[at : at + right.shape[0], :], right[...], TN)
        at += right.shape[0]
        grad = part if grad is None else grad + part
    if not with_got:
        refs[0][0] = grad.astype(BF16)
        return
    value = (grad + refs[0][0].astype(F32)).astype(BF16)
    j = pl.program_id(0)
    for step, out in enumerate(refs[1:]):

        @pl.when(j == step)
        def _():
            out[...] = value


def head_grad_body(sh, with_got, scal, dq, dk, dv, ctx, normed, own, away, *refs):
    scratch = refs[-1]
    for kind, ref in enumerate((dq, dk, dv)):
        scratch[kind] = mm(ref[...], normed[...], TN)
    half = own.shape[0]
    scratch[3] = mm(ctx[:half, :].astype(BF16), own[...], TN) + mm(
        ctx[half:, :].astype(BF16), away[...], TN
    )
    for j in range(sh.chunks):
        rows = slice(j * sh.hu, (j + 1) * sh.hu)
        value = jnp.concatenate([scratch[kind, rows, :] for kind in range(4)], axis=0)
        if with_got:
            refs[1 + j][...] = (value + refs[0][j].astype(F32)).astype(BF16)
        else:
            refs[0][j] = value.astype(BF16)


def rows_grad_body(sh, scal, dq, dk, dv, gh, own, away, g1, g2, *refs):
    count = sh.pairs * sh.chunks
    blocks_a, blocks_u = refs[:count], refs[count : 2 * count]
    own_out, away_out, sums, wt, wu, n_ref = refs[2 * count :]
    seq = pl.program_id(0)
    half = pl.num_programs(0) // 2

    @pl.when(seq == 0)
    def _():
        for kind in range(3):
            fill_rows(sh, wt, blocks_a, kind * sh.hu, sh.hu, kind * sh.width)
        for slot in range(sh.pairs):
            for j in range(sh.chunks):
                wu[slot, :, j * sh.hf : (j + 1) * sh.hf] = blocks_u[slot * sh.chunks + j][...]
        sums[...] = jnp.zeros(sums.shape, F32)

    x = jnp.where(seq < half, own[0], away[0]).astype(F32)
    n_ref[...] = normalize(x)[0]
    for slot in range(sh.pairs):
        cols = sh.cols(scal, slot)
        one = mm(dq[0], wt[slot, : sh.width, :])
        one = one + mm(dk[0], wt[slot, sh.width : 2 * sh.width, :])
        one = one + mm(dv[0], wt[slot, 2 * sh.width :, :])
        two = mm(gh[0], wu[slot], NT)
        n = n_ref[:, cols]
        for at, value in enumerate((one * n, one, two * n, two)):
            line = slice(at, at + 1)
            sums[line, cols] = sums[line, cols] + jnp.sum(value, axis=0, keepdims=True)
        e = (one * g1[:, cols] + two * g2[:, cols]).astype(BF16)

        @pl.when(seq < half)
        def _():
            own_out[0, :, cols] = e

        @pl.when(seq >= half)
        def _():
            away_out[0, :, cols] = e


def tokens_grad_body(scal, mine, got, tokens, cot, out):
    e = mine[0].astype(F32) + got[0].astype(F32)
    n, scale = normalize(tokens[0].astype(F32))
    shift = jnp.mean(e, axis=-1, keepdims=True) + n * jnp.mean(e * n, axis=-1, keepdims=True)
    out[0] = cot[0].astype(F32) + scale * (e - shift)


def join_units(scal, keep, got):
    low = scal[3] == 0
    mine, other = keep[...].astype(F32), got[...].astype(F32)
    return jnp.where(low, mine, other), jnp.where(low, other, mine)


def end_units_body(sh, scal, keep_u, got_u, keep_d, got_d, up, down):
    first, second = join_units(scal, keep_u, got_u)
    up[:, : sh.hf] = jnp.transpose(first)
    up[:, sh.hf :] = jnp.transpose(second)
    first, second = join_units(scal, keep_d, got_d)
    down[: sh.hf, :] = first
    down[sh.hf :, :] = second


def end_heads_body(sh, scal, keep, got, *outs):
    first, second = join_units(scal, keep, got)
    for kind in range(4):
        rows = slice(kind * sh.hu, (kind + 1) * sh.hu)
        both = jnp.concatenate([first[rows], second[rows]], axis=0)
        outs[kind][...] = both if kind == 3 else jnp.transpose(both)


class Layout:
    def __init__(self):
        self.seqs, self.parts = lax.axis_size("seq"), lax.axis_size("mp")
        self.pairs, self.chunks = self.seqs // 2, self.parts // 4
        seq, part = lax.axis_index("seq"), lax.axis_index("mp")
        self.pair, self.core = seq // 2, seq % 2
        self.hi, self.lo = part // 4, part % 4

    def move(self, values, rule):
        links = []
        for seq in range(self.seqs):
            for part in range(self.parts):
                there = rule(seq // 2, seq % 2, part // 4, part % 4)
                if there is not None:
                    pair, core, hi, lo = there
                    goal = (pair * 2 + core) * self.parts + hi * 4 + lo
                    links.append((seq * self.parts + part, goal))
        return lax.ppermute(values, AXES, links)

    def core_swap(self, values):
        return self.move(values, lambda p, c, h, l: (p, 1 - c, h, l))

    def lo_swap(self, values, bit):
        return self.move(values, lambda p, c, h, l: (p, c, h, l ^ bit))

    def pair_step(self, values, way):
        return self.move(values, lambda p, c, h, l: ((p + way) % self.pairs, c, h, l))

    def hi_step(self, values, way):
        return self.move(values, lambda p, c, h, l: (p, c, (h + way) % self.chunks, l))


def after(value, *others):
    return lax.optimization_barrier((value,) + others)[0]


def hold(values, *others):
    return lax.optimization_barrier(tuple(values) + others)[: len(values)]


def in_order(lay, one, two):
    flip = lay.lo >= 2
    return jnp.where(flip, two, one), jnp.where(flip, one, two)


def send_states(lay, local, scale, backward):
    states = local.astype(F32).reshape((-1, 2) + local.shape[1:])
    first, second = in_order(lay, states[:, 0], states[:, 1])
    if backward:
        out, goal = first + second * scale(0, 1), 0
    else:
        out, goal = second + first * scale(1, 2), 1
    return lay.move(
        out.astype(BF16), lambda p, c, h, l: (p, c, goal, l) if h != goal else None
    )


def combine_states(lay, local, got, scale, backward):
    states = local.astype(F32).reshape((-1, 2) + local.shape[1:])
    first, second = in_order(lay, states[:, 0], states[:, 1])
    got = got.astype(F32)
    if backward:
        first, second = second + got * scale(1, 2), got
    else:
        first, second = got, first + got * scale(0, 1)
    return jnp.stack(in_order(lay, first, second), 1).reshape(local.shape)


def erf_inverse(target):
    low, high = -6.0, 6.0
    for _ in range(60):
        middle = 0.5 * (low + high)
        low, high = (middle, high) if math.erf(middle) < target else (low, middle)
    guess = 0.5 * (low + high)
    for _ in range(3):
        gap = math.erf(guess) - target
        guess -= gap * math.exp(guess * guess) * math.sqrt(math.pi) / 2.0
    return guess


@functools.lru_cache(None)
def tables(heads):
    primes = prime_list(HEAD_DIM)
    points = np.zeros((FEATS, HEAD_DIM))
    for row in range(FEATS):
        for col in range(HEAD_DIM):
            share = min(max((row + 0.5) * math.sqrt(primes[col]) % 1.0, 0.001), 0.999)
            points[row, col] = math.sqrt(2.0) * erf_inverse(2.0 * float(np.float32(share)) - 1.0)
    cells = np.arange(HEAD_DIM)
    cosine = np.cos(np.pi * (cells[None, :] + 0.5) * cells[:, None] / HEAD_DIM)
    cosine = cosine * math.sqrt(2.0 / HEAD_DIM)
    cosine[0] *= math.sqrt(0.5)
    project = np.kron(np.eye(heads), (points @ cosine).T / math.sqrt(HEAD_DIM))
    project = project.astype(np.float32)
    high = project.astype(BF16)
    low = (project - high.astype(np.float32)).astype(BF16)
    weighting = 1.0 / (1.0 + np.sum(points * points, axis=1) / HEAD_DIM)
    return high, low, np.tile(weighting, heads)[None, :].astype(np.float32)


def team_local(
    tokens,
    ln1_gain,
    ln1_bias,
    ln2_gain,
    ln2_bias,
    q_weight,
    k_weight,
    value_weight,
    out_weight,
    up_weight,
    down_weight,
    lengths,
    cotangent,
):
    lay = Layout()
    micro, rows, dim = tokens.shape
    drows, units = q_weight.shape
    docs = lengths.shape[2]
    chunk = 2 * rows
    half_units, half_ff = units // 2, up_weight.shape[1] // 2
    sh = Shape(lay.pairs, lay.chunks, dim, half_units, half_ff, chunk, docs)
    width, ff, dp = sh.width, sh.ff, sh.dp
    half = 2 * micro
    count = 2 * half
    total = count * chunk
    whole_rows = lambda array: array.reshape(total, array.shape[-1])
    bind = lambda body, *first: functools.partial(body, *first)
    gains = [vec.reshape(1, dim) for vec in (ln1_gain, ln1_bias, ln2_gain, ln2_bias)]

    own_lengths = lengths[:, 0]
    table = jnp.stack([own_lengths, lay.core_swap(own_lengths)]).reshape(half, docs)
    seq_ends = jnp.cumsum(table, axis=1)
    seq_starts = seq_ends - table
    starts, ends = jnp.repeat(seq_starts, 2, axis=0), jnp.repeat(seq_ends, 2, axis=0)
    scal = jnp.concatenate(
        [
            jnp.stack([lay.pair, lay.hi, lay.lo, lay.core]).astype(jnp.int32),
            jnp.concatenate([starts, ends], axis=1).reshape(-1).astype(jnp.int32),
        ]
    )
    places = jnp.stack([lay.core, lay.core, lay.core, lay.core]).astype(jnp.int32)
    core_only = places

    block_shape = [(4 * half_units, drows), (drows, half_ff), (half_ff, drows)]
    keep_a, send_a, send_u, send_d = call(
        "pack", pack_body, core_only, (),
        [whole(w) for w in (q_weight, k_weight, value_weight, out_weight, up_weight, down_weight)],
        [whole(new(shape, BF16)) for shape in [block_shape[0]] + block_shape],
    )
    first_core = lay.core == 0

    def join(keep, got, axis):
        return jnp.where(
            first_core, jnp.concatenate([keep, got], axis), jnp.concatenate([got, keep], axis)
        )

    got_a, got_u, got_d = lax.optimization_barrier(
        tuple(lay.core_swap(send) for send in (send_a, send_u, send_d))
    )
    block_a = join(keep_a, got_a, 1)
    split_at = micro // 2

    def first_swaps(values):
        return lay.lo_swap(values, 1), lay.lo_swap(values, 2)

    def second_swaps(by_y, by_z):
        return lay.lo_swap(by_z[:split_at], 1), lay.lo_swap(by_y[split_at:], 2)

    def team_rows(values, by_y, by_z, both):
        both = jnp.concatenate(both, 0)
        own = jnp.stack([jnp.stack([values, by_y], 1), jnp.stack([by_z, both], 1)], 1)
        own = own.reshape(half, chunk, dim)
        return own, lay.core_swap(own)

    def cross(values):
        return lay.pair_step(values, -1)

    def beside(values):
        return lay.hi_step(values, -1)

    block_a, own_tokens = hold((block_a, tokens), got_a)
    by_y, by_z = first_swaps(own_tokens)
    beside_a, cross_a = beside(block_a), cross(block_a)
    late_up, late_down = hold((up_weight, down_weight), block_a)
    keep_u = jnp.where(first_core, late_up[:, :half_ff], late_up[:, half_ff:])
    keep_d = jnp.where(first_core, late_down[:half_ff], late_down[half_ff:])
    block_u, block_d = join(keep_u, got_u, 0), join(keep_d, got_d, 1)
    cross_u = cross(block_u)

    here = (2 * lay.hi + (lay.lo // 2 + jnp.arange(count, dtype=jnp.int32)) % 2) * chunk
    step = jnp.arange(rows, dtype=jnp.int32)
    side = (lay.lo % 2) * rows
    places = here[:, None] + jnp.concatenate([side + step, rows - side + step])[None, :]
    start = jnp.zeros((count, chunk), jnp.int32)
    for doc in range(docs):
        first = starts[:, doc : doc + 1]
        start = jnp.where(places >= first, first, start)
    offset = after((places - start).astype(F32), block_a)
    lane = np.arange(128) % HEAD_DIM
    turned = lane < ROT
    inverse = np.where(turned, 10000.0 ** (-(lane % (ROT // 2)) * 2.0 / ROT), 0.0)
    side = np.where(turned, np.where(lane < ROT // 2, -1.0, 1.0), 0.0)
    angles = offset[:, :, None] * jnp.asarray(inverse, F32)[None, None, :]
    cos = jnp.cos(angles)
    sin = jnp.sin(angles) * jnp.asarray(side, F32)[None, None, :]
    cos, sin = lax.optimization_barrier((cos, sin))

    by_y, by_z, beside_a, cross_a, cross_u, block_d, cos, sin = hold(
        (by_y, by_z, beside_a, cross_a, cross_u, block_d, cos, sin)
    )
    both = second_swaps(by_y, by_z)
    across_a, cross_d = cross(beside_a), cross(block_d)
    both = hold(both, across_a)
    x_own, x_away = team_rows(tokens, by_y, by_z, both)

    high, low, weighting = tables(width // HEAD_DIM)
    maps = [whole(jnp.asarray(high)), whole(jnp.asarray(low))]
    turns = [by_seq(cos), by_seq(sin)]

    def straddles(first, second):
        lower, higher = jnp.minimum(first, second), jnp.maximum(first, second)
        return jnp.any((seq_starts < lower) & (seq_ends > higher), axis=1).astype(F32)

    edges = [(2 * lay.hi + step) * chunk for step in range(3)]
    scale = lambda a, b: straddles(edges[a], edges[b])[:, None, None]

    rows_new = lambda size, kind: by_seq(new((count, chunk, size), kind))
    state_new = by_seq(new((count, STATE_ROWS, width), BF16))
    norm_ins = [whole(vec) for vec in gains]
    norm_outs = [rows_new(dim, BF16), rows_new(dim, BF16)]
    n_one, n_two = call(
        "norms_own", norm_body, core_only, (half,), [by_seq(x_own)] + norm_ins, norm_outs
    )
    n_one, n_two, x_away, block_u, cross_u, block_d, cross_d, cot = hold(
        (n_one, n_two, x_away, block_u, cross_u, block_d, cross_d, cotangent)
    )
    beside_u, across_u = beside(block_u), beside(cross_u)
    cot_y, cot_z = first_swaps(cot)
    beside_d = beside(block_d)
    rest = lambda i, s: (i + half, 0, 0)
    n_one, n_two = call(
        "norms_away", norm_body, core_only, (half,),
        [by_seq(x_away)] + norm_ins + [(n_one, None, None), (n_two, None, None)],
        [(array, block, rest) for array, block, _ in norm_outs], aliases={6: 0, 7: 1},
    )
    in_a = [whole(block) for block in (block_a, beside_a, cross_a, across_a)]
    fq, fk, vals, num, den, state = call(
        "attend", bind(attend_body, sh), scal, (count,),
        [by_seq(n_one)] + turns + maps + [whole(jnp.asarray(weighting))] + in_a,
        [rows_new(width, BF16)] * 2 + [rows_new(width, F32)] * 3 + [state_new],
        [pltpu.VMEM((sh.pairs, 3 * width, dp), BF16)],
    )
    n_two, fq, state, beside_u, across_u, cot_y, cot_z = hold(
        (n_two, fq, state, beside_u, across_u, cot_y, cot_z)
    )
    in_u = [whole(block) for block in (block_u, beside_u, cross_u, across_u)]
    state_got = send_states(lay, state, scale, False)
    cot_both = second_swaps(cot_y, cot_z)
    act, slope = call(
        "up", bind(up_body, sh), scal, (count,), [by_seq(n_two)] + in_u,
        [rows_new(ff, BF16)] * 2, [pltpu.VMEM((sh.pairs, dp, ff), BF16)],
    )
    act, num, state_got, beside_d, cot_both0, cot_both1 = hold(
        (act, num, state_got, beside_d) + cot_both
    )
    across_d = cross(beside_d)
    g_own, g_away = team_rows(cotangent, cot_y, cot_z, (cot_both0, cot_both1))
    carry = combine_states(lay, state, state_got, scale, False)
    ctx, rden = call(
        "finish", bind(finish_body, sh), scal, (count,),
        [by_seq(a) for a in (after(num, g_own), den, fq, carry)], [rows_new(width, F32)] * 2,
    )
    g_own, g_away, ctx, across_d = hold((g_own, g_away, ctx, across_d))
    in_d = [whole(block) for block in (block_d, beside_d, cross_d, across_d)]

    def cols_of(array, slot):
        pairs = sh.pairs
        index = lambda *ids: (0, (ids[-1][0] + slot) % pairs)
        return (array, (array.shape[0], dp), index)

    def lanes_of(array, size):
        return (array, (array.shape[0], size), lambda j, s: (0, j))

    def block_of(array):
        rest = tuple(array.shape[1:])
        return (array, (1,) + rest, lambda j, s: (j,) + (0,) * len(rest))

    g_rows = [g.reshape(total // 2, dim) for g in (g_own, g_away)]
    unit_shape, head_shape = (half_ff, dp), (4 * half_units, dp)

    def unit_grads(name, left, rights, slot, got=None):
        final = slot == 0
        outs = [whole(new(unit_shape, BF16))] * sh.chunks
        if not final:
            outs = [block_of(new((sh.chunks,) + unit_shape, BF16))]
        return call(
            name + str(slot), bind(unit_grad_body, (len(rights), got is not None)), scal,
            (sh.chunks,),
            [lanes_of(left, half_ff)] + [cols_of(right, slot) for right in rights]
            + ([] if got is None else [block_of(got)]),
            outs,
        )

    def head_grads(parts, slot, got=None):
        final = slot == 0
        outs = [whole(new(head_shape, BF16))] * sh.chunks
        if not final:
            outs = [whole(new((sh.chunks,) + head_shape, BF16))]
        return call(
            "head_grad" + str(slot), bind(head_grad_body, sh, got is not None), scal, (),
            [whole(whole_rows(a)) for a in parts] + [cols_of(whole_rows(n_one), slot)]
            + [cols_of(g, slot) for g in g_rows] + ([] if got is None else [whole(got)]),
            outs, [pltpu.VMEM((4, width, dp), F32)],
        )

    def pair_sums(make):
        got = None
        for slot in range(sh.pairs - 1, 0, -1):
            part = make(slot, got)[0]
            got = lay.pair_step(part, 1)
        return part, got

    def hi_sums(parts):
        term = parts[sh.chunks - 1]
        for j in range(sh.chunks - 2, -1, -1):
            term = lay.hi_step(term, 1)
            if j:
                term = (term.astype(F32) + parts[j].astype(F32)).astype(BF16)
        return term, parts[0]

    def trade(ends, *others):
        sums = (ends[0].astype(F32) + ends[1].astype(F32)).astype(BF16)
        first, second = sums[:, :drows], sums[:, drows:]
        keep = jnp.where(first_core, first, second)
        send = jnp.where(first_core, second, first)
        return [whole(keep), whole(lay.core_swap(send))]

    down_make = lambda slot, got: unit_grads("down_grad", whole_rows(act), g_rows, slot, got)
    down_part, down_got = pair_sums(down_make)

    ctx = after(ctx, down_part)
    halves_new = [
        own_seq(new((half, chunk, dim), BF16)), away_seq(new((half, chunk, dim), BF16))
    ]
    branch_own, branch_away = call(
        "branch", bind(branch_body, sh), scal, (count,),
        [by_seq(ctx), by_seq(act)] + in_a + in_d, halves_new,
        [pltpu.VMEM((sh.pairs, width, dp), BF16), pltpu.VMEM((sh.pairs, ff, dp), BF16)],
    )

    def first_sums(own, away_got):
        both = (own.astype(F32) + away_got.astype(F32)).reshape(micro, 2, 2, rows, dim)
        by_z, by_y = both[:split_at], both[split_at:]
        sends = by_z[:, 1].astype(BF16), by_y[:, :, 1].astype(BF16)
        return (by_z[:, 0].astype(BF16), by_y[:, :, 0].astype(BF16)), sends

    def second_sums(keeps, gots):
        by_z = keeps[0].astype(F32) + gots[0].astype(F32)
        by_y = keeps[1].astype(F32) + gots[1].astype(F32)
        sends = by_z[:, 1].astype(BF16), by_y[:, 1].astype(BF16)
        return (by_z[:, 0].astype(BF16), by_y[:, 0].astype(BF16)), sends

    def round_one(sends):
        return lay.lo_swap(sends[0], 2), lay.lo_swap(sends[1], 1)

    def round_two(sends):
        return lay.lo_swap(sends[0], 1), lay.lo_swap(sends[1], 2)

    join_micro = lambda parts: jnp.concatenate(parts, 0)
    down_got, branch_own, branch_away, ctx = hold((down_got, branch_own, branch_away, ctx))
    m_got = lay.core_swap(branch_away)

    dq, dk_part, dv_part, dstate = call(
        "attend_back", bind(back_body, sh), scal, (count,),
        [own_seq(g_own), away_seq(g_away)]
        + [by_seq(a) for a in (fq, fk, vals, ctx, rden, carry)]
        + turns + maps + in_a,
        [rows_new(width, BF16), rows_new(width, F32), rows_new(width, F32), state_new],
        [pltpu.VMEM((sh.pairs, width, dp), BF16)],
    )
    branch_own, m_got, dq, dstate = hold((branch_own, m_got, dq, dstate))
    m_keeps, m_sends = first_sums(branch_own, m_got)
    m_gots = round_one(m_sends)
    state_got = send_states(lay, dstate, scale, True)
    (grad_hidden,) = call(
        "hidden_grad", bind(hidden_body, sh), scal, (count,),
        [own_seq(g_own), away_seq(g_away), by_seq(after(slope, *m_sends))] + in_d,
        [rows_new(ff, BF16)], [pltpu.VMEM((sh.pairs, ff, dp), BF16)],
    )
    grad_hidden, state_got = hold((grad_hidden, state_got))
    dcarry = combine_states(lay, dstate, state_got, scale, True)
    up_make = lambda slot, got: unit_grads(
        "up_grad", whole_rows(grad_hidden), [whole_rows(n_two)], slot, got
    )
    up_part, up_got = pair_sums(up_make)
    dk_part, *m_parts = hold((dk_part,) + m_keeps + m_gots, up_part)
    m_keeps, m_sends = second_sums(m_parts[:2], m_parts[2:])
    m_gots = round_two(m_sends)
    dk, dv = call(
        "keys_back", bind(last_body, sh), scal, (count,),
        [by_seq(a) for a in (after(dk_part, *m_sends), dv_part, fk, vals, dcarry)]
        + turns + maps,
        [rows_new(width, BF16)] * 2,
    )
    dk, up_got, *m_parts = hold((dk, up_got) + m_keeps + m_gots)
    up_parts = up_make(0, up_got)
    dk, *up_parts = hold((dk,) + tuple(up_parts))
    up_ends = hi_sums(up_parts)
    mixed = tokens.astype(F32) + join_micro(m_parts[:2]).astype(F32)
    mixed = (mixed + join_micro(m_parts[2:]).astype(F32)).astype(BF16)
    own, away, sums = call(
        "rows_grad", bind(rows_grad_body, sh), scal, (count,),
        [by_seq(a) for a in (after(dq, mixed), dk, dv, grad_hidden)]
        + [own_seq(x_own), away_seq(x_away)]
        + [whole(gains[0]), whole(gains[2])] + in_a + in_u,
        halves_new + [whole(new((8, dim), F32))],
        [
            pltpu.VMEM((sh.pairs, 3 * width, dp), BF16),
            pltpu.VMEM((sh.pairs, dp, ff), BF16),
            pltpu.VMEM((chunk, dim), F32),
        ],
    )
    own, away, sums, dq, up_ends = hold((own, away, sums, dq, up_ends))
    e_got = lay.core_swap(away)
    sums = sums[:4]
    sums_got = lay.lo_swap(sums, 1)
    head_make = lambda slot, got: head_grads((dq, dk, dv, ctx), slot, got)
    head_part, head_got = pair_sums(head_make)
    own, e_got, sums_got = hold((own, e_got, sums_got), head_part)
    sums = sums + sums_got
    sums_got = lay.core_swap(sums)
    e_keeps, e_sends = first_sums(own, e_got)
    e_gots = round_one(e_sends)
    down_parts = down_make(0, after(down_got, *e_sends))
    head_got, sums_got, *down_parts = hold((head_got, sums_got) + tuple(down_parts))
    down_ends = hi_sums(down_parts)
    sums = sums + sums_got
    sums_got = lay.move(sums, lambda p, c, h, l: (1 - p, c, h, l))
    head_parts = head_make(0, after(head_got, sums))
    e_keep0, e_keep1, e_got0, e_got1, sums_got, down_end0, down_end1, *head_parts = hold(
        e_keeps + e_gots + (sums_got,) + down_ends + tuple(head_parts)
    )
    down_ends = (down_end0, down_end1)
    sums = sums + sums_got
    sums_got = lay.lo_swap(sums, 2)
    head_ends = hi_sums(head_parts)
    e_keeps, e_sends = second_sums((e_keep0, e_keep1), (e_got0, e_got1))
    sums_got, *e_sends = hold((sums_got,) + e_sends)
    e_gots = round_two(e_sends)
    sums = sums + sums_got
    units_ends = trade(hold(up_ends, *e_sends)) + trade(hold(down_ends, *e_sends))
    grads_units = call(
        "end_units", bind(end_units_body, sh), core_only, (), units_ends,
        [whole(new(w.shape, F32)) for w in (up_weight, down_weight)],
    )
    e_gots = hold(e_gots, grads_units[0])
    mine, got = join_micro(e_keeps), join_micro(e_gots)
    (grad_tokens,) = call(
        "tokens_grad", tokens_grad_body, scal, (micro,),
        [by_seq(a) for a in (mine, got, tokens, cotangent)],
        [by_seq(new((micro, rows, dim), F32))],
    )
    sums = sums + lay.move(sums, lambda p, c, h, l: (p, c, 1 - h, l))
    grads = call(
        "end_heads", bind(end_heads_body, sh), core_only, (), trade(head_ends),
        [whole(new(w.shape, F32)) for w in (q_weight, k_weight, value_weight, out_weight)],
    )
    return (
        mixed,
        grad_tokens,
        sums[0],
        sums[1],
        sums[2],
        sums[3],
        grads[0],
        grads[1],
        grads[2],
        grads[3],
        grads_units[0],
        grads_units[1],
    )


def solution(mesh):
    seqs, parts = mesh.shape["seq"], mesh.shape["mp"]

    def body(*args):
        units = args[5].shape[1]
        if parts == 8 and seqs == 4 and units == 2 * HEAD_DIM and args[0].shape[0] % 2 == 0:
            return team_local(*args)
        return plain_local(*args)

    in_specs = (
        P(None, ("seq", "mp"), None),
        P(),
        P(),
        P(),
        P(),
        P("seq", "mp"),
        P("seq", "mp"),
        P("seq", "mp"),
        P("mp", "seq"),
        P("seq", "mp"),
        P("mp", "seq"),
        P(None, "seq", None),
        P(None, ("seq", "mp"), None),
    )
    out_specs = (
        P(None, ("seq", "mp"), None),
        P(None, ("seq", "mp"), None),
        P(),
        P(),
        P(),
        P(),
        P("seq", "mp"),
        P("seq", "mp"),
        P("seq", "mp"),
        P("mp", "seq"),
        P("seq", "mp"),
        P("mp", "seq"),
    )
    return jax.shard_map(body, mesh=mesh, in_specs=in_specs, out_specs=out_specs, check_vma=False)
```

```python
import functools
import math

import jax
import jax.numpy as jnp
import numpy as np
from jax import lax
from jax.experimental import pallas as pl
from jax.experimental.pallas import tpu as pltpu
from jax.sharding import PartitionSpec as P

HEAD_DIM = 64
ROT = 16
FEATS = 64
STATE_ROWS = 80
AXES = ("seq", "mp")
BF16 = jnp.bfloat16
F32 = jnp.float32
VMEM_LIMIT = 56 * 1024 * 1024
PER = 2
NN = (((1,), (0,)), ((), ()))
NT = (((1,), (1,)), ((), ()))
TN = (((0,), (0,)), ((), ()))


def prime_list(wanted):
    found_primes = []
    candidate = 2
    while len(found_primes) < wanted:
        if all((candidate % earlier != 0 for earlier in found_primes)):
            found_primes.append(candidate)
        candidate += 1
    return found_primes


def feature_maps(head_width, feature_count):
    primes_found = prime_list(head_width)
    uniform_rows = [
        [
            min(max((row_idx + 0.5) * math.sqrt(prime_val) % 1.0, 0.001), 0.999)
            for prime_val in primes_found
        ]
        for row_idx in range(feature_count)
    ]
    uniform_pts = jnp.asarray(uniform_rows, jnp.float32)
    points = math.sqrt(2.0) * lax.erf_inv(2.0 * uniform_pts - 1.0)
    cosine_rows = [
        [
            math.sqrt(2.0 / head_width)
            * math.cos(math.pi * (cell_idx + 0.5) * freq_idx / head_width)
            * (math.sqrt(0.5) if freq_idx == 0 else 1.0)
            for cell_idx in range(head_width)
        ]
        for freq_idx in range(head_width)
    ]
    cosine = jnp.asarray(cosine_rows, jnp.float32)
    project = jnp.dot(points, cosine, precision=lax.Precision.HIGHEST)
    project = jnp.transpose(project) * (1.0 / math.sqrt(head_width))
    weighting = 1.0 / (1.0 + jnp.sum(points * points, axis=1) / head_width)
    return (project, weighting)


def rotate_heads(values, offset):
    half_dims = ROT // 2
    inverse = 10000.0 ** (-jnp.arange(half_dims, dtype=jnp.float32) * 2.0 / ROT)
    angles = offset[:, None] * inverse[None, :]
    cosine = jnp.cos(angles)[None, :, :]
    sine_part = jnp.sin(angles)[None, :, :]
    first_half = values[..., :half_dims]
    second = values[..., half_dims:ROT]
    return jnp.concatenate(
        [
            first_half * cosine - second * sine_part,
            second * cosine + first_half * sine_part,
            values[..., ROT:],
        ],
        axis=-1,
    )


def layer_norm(values, gain_vec, bias_vec):
    centered = values - jnp.mean(values, axis=-1, keepdims=True)
    variance = jnp.mean(centered * centered, axis=-1, keepdims=True)
    return centered * lax.rsqrt(variance + 1e-05) * gain_vec + bias_vec


def exact_gelu(values):
    return jax.nn.gelu(values, approximate=False)


def doc_layout(doc_lengths, number_of_tokens):
    doc_ends = jnp.cumsum(doc_lengths).astype(jnp.int32)
    starts = (doc_ends - doc_lengths).astype(jnp.int32)
    places = jnp.arange(number_of_tokens, dtype=jnp.int32)
    segment = jnp.sum((places[:, None] >= doc_ends[None, :]).astype(jnp.int32), axis=1).astype(
        jnp.int32
    )
    member = segment[:, None] == jnp.arange(doc_lengths.shape[0], dtype=jnp.int32)[None, :]
    offset = places - jnp.sum(jnp.where(member, starts[None, :], 0), axis=1).astype(jnp.int32)
    return (segment, offset.astype(jnp.float32))


def contract_rows(left_side, right_side):
    return lax.dot_general(
        left_side, right_side, (((0,), (0,)), ((), ())), preferred_element_type=jnp.float32
    )


def contract_cols(left_side, right_side):
    return lax.dot_general(
        left_side, right_side, (((1,), (1,)), ((), ())), preferred_element_type=jnp.float32
    )


def local_attention(plain_query_rows, key_raw, value_raw, segment, offset, project, weighting):
    maximal_precision_mode = lax.Precision.HIGHEST
    number_of_tokens = plain_query_rows.shape[0]
    head_count = plain_query_rows.shape[1] // HEAD_DIM

    def heads_first(values):
        return jnp.transpose(values.reshape(number_of_tokens, head_count, HEAD_DIM), (1, 0, 2))

    rot_query = rotate_heads(heads_first(plain_query_rows), offset)
    rot_key = rotate_heads(heads_first(key_raw), offset)
    value_heads = heads_first(value_raw)
    feat_query = (
        jnp.exp(jnp.einsum("htd,df->htf", rot_query, project, precision=maximal_precision_mode))
        * weighting
    )
    feat_key = jnp.exp(
        jnp.einsum("htd,df->htf", rot_key, project, precision=maximal_precision_mode)
    )
    rows_per_block = min(512, number_of_tokens)
    block_count = number_of_tokens // rows_per_block

    def split_blocks(values):
        return jnp.transpose(
            values.reshape((head_count, block_count, rows_per_block, values.shape[2])), (1, 0, 2, 3)
        )

    def block_step(carry, pieces):
        kv_state, totals, previous = carry
        block_of_queries, block_of_keys, value_block, block_segment = pieces
        places = jnp.arange(block_segment.shape[0], dtype=jnp.int32)
        attention_scores = jnp.einsum(
            "ugy,uky->ugk", block_of_queries, block_of_keys, precision=maximal_precision_mode
        )
        allowed = (places[:, None] >= places[None, :]) & (
            block_segment[:, None] == block_segment[None, :]
        )
        attention_scores = jnp.where(allowed[None, :, :], attention_scores, 0.0)
        numerator = jnp.einsum(
            "hqk,hkd->hqd", attention_scores, value_block, precision=maximal_precision_mode
        )
        denominator = jnp.sum(attention_scores, axis=2)
        carried_in = (block_segment == previous)[None, :]
        numerator = numerator + jnp.where(
            carried_in[:, :, None],
            jnp.einsum(
                "hqf,hfd->hqd", block_of_queries, kv_state, precision=maximal_precision_mode
            ),
            0.0,
        )
        denominator = denominator + jnp.where(
            carried_in,
            jnp.einsum("hqf,hf->hq", block_of_queries, totals, precision=maximal_precision_mode),
            0.0,
        )
        final_output = block_segment[-1]
        carried_over = final_output == previous
        trailing_mask = (block_segment == final_output).astype(jnp.float32)
        new_state = jnp.where(carried_over, kv_state, 0.0) + jnp.einsum(
            "hrf,hrd,r->hfd",
            block_of_keys,
            value_block,
            trailing_mask,
            precision=maximal_precision_mode,
        )
        new_totals = jnp.where(carried_over, totals, 0.0) + jnp.einsum(
            "hrf,r->hf", block_of_keys, trailing_mask, precision=maximal_precision_mode
        )
        return ((new_state, new_totals, final_output), numerator / denominator[:, :, None])

    start_carry = (
        jnp.zeros((head_count, FEATS, HEAD_DIM), jnp.float32),
        jnp.zeros((head_count, FEATS), jnp.float32),
        jnp.array(-1, jnp.int32),
    )
    _, outputs = lax.scan(
        jax.checkpoint(block_step),
        start_carry,
        (
            split_blocks(feat_query),
            split_blocks(feat_key),
            split_blocks(value_heads),
            segment.reshape(block_count, rows_per_block),
        ),
    )
    joined = jnp.transpose(outputs, (1, 0, 2, 3)).reshape(head_count, number_of_tokens, HEAD_DIM)
    return jnp.transpose(joined, (1, 0, 2)).reshape(number_of_tokens, head_count * HEAD_DIM)


def plain_local(
    tokens,
    ln1_gain,
    ln1_bias,
    ln2_gain,
    ln2_bias,
    q_weight,
    k_weight,
    value_weight,
    out_weight,
    up_weight,
    down_weight,
    lengths,
    cotangent,
):
    micro_count = tokens.shape[0]
    local_rows = tokens.shape[1]
    group_rows = local_rows * lax.axis_size("mp")
    seq_count = lax.axis_size("seq")
    project, weighting = feature_maps(HEAD_DIM, FEATS)
    grad_sums = [
        jnp.zeros((q_weight.shape[0] * seq_count, q_weight.shape[1]), jnp.float32),
        jnp.zeros((k_weight.shape[0] * seq_count, k_weight.shape[1]), jnp.float32),
        jnp.zeros((value_weight.shape[0] * seq_count, value_weight.shape[1]), jnp.float32),
        jnp.zeros((out_weight.shape[0], out_weight.shape[1] * seq_count), jnp.float32),
        jnp.zeros((up_weight.shape[0] * seq_count, up_weight.shape[1]), jnp.float32),
        jnp.zeros((down_weight.shape[0], down_weight.shape[1] * seq_count), jnp.float32),
    ]
    norm_sums = [
        jnp.zeros_like(ln1_gain),
        jnp.zeros_like(ln1_bias),
        jnp.zeros_like(ln2_gain),
        jnp.zeros_like(ln2_bias),
    ]
    mixed_parts = []
    grad_parts = []
    for micro_step in range(micro_count):
        full_weights = (
            lax.all_gather(q_weight, "seq", axis=0, tiled=True),
            lax.all_gather(k_weight, "seq", axis=0, tiled=True),
            lax.all_gather(value_weight, "seq", axis=0, tiled=True),
            lax.all_gather(out_weight, "seq", axis=1, tiled=True),
            lax.all_gather(up_weight, "seq", axis=0, tiled=True),
            lax.all_gather(down_weight, "seq", axis=1, tiled=True),
        )
        w_query, w_key, w_value, w_out, w_up, w_down = full_weights
        rows_in = tokens[micro_step].astype(jnp.float32)
        normed_one, pull_one = jax.vjp(layer_norm, rows_in, ln1_gain, ln1_bias)
        normed_two, pull_two = jax.vjp(layer_norm, rows_in, ln2_gain, ln2_bias)
        group_one, group_two = (
            lax.all_gather(normed_one.astype(jnp.bfloat16), "mp", axis=0, tiled=True),
            lax.all_gather(normed_two.astype(jnp.bfloat16), "mp", axis=0, tiled=True),
        )
        plain_query_rows = jnp.dot(group_one, w_query, preferred_element_type=jnp.float32)
        key_raw = jnp.dot(group_one, w_key, preferred_element_type=jnp.float32)
        value_raw = jnp.dot(group_one, w_value, preferred_element_type=jnp.float32)
        segment, offset = doc_layout(lengths[micro_step, 0], group_rows)
        attend = functools.partial(
            local_attention, segment=segment, offset=offset, project=project, weighting=weighting
        )
        context, pull_attn = jax.vjp(attend, plain_query_rows, key_raw, value_raw)
        context_low = context.astype(jnp.bfloat16)
        hidden = jnp.dot(group_two, w_up, preferred_element_type=jnp.float32)
        activated, pull_gelu = jax.vjp(exact_gelu, hidden)
        activated_low = activated.astype(jnp.bfloat16)
        context_rows = lax.slice_in_dim(context_low, 0, lax.axis_size("mp") * local_rows, axis=0)
        active_rows = lax.slice_in_dim(activated_low, 0, lax.axis_size("mp") * local_rows, axis=0)
        branch_sum = lax.psum_scatter(
            jnp.dot(context_rows, w_out, preferred_element_type=jnp.float32)
            + jnp.dot(active_rows, w_down, preferred_element_type=jnp.float32),
            "mp",
            scatter_dimension=0,
            tiled=True,
        )
        mixed_parts.append((rows_in + branch_sum).astype(jnp.bfloat16))
        grad_group = lax.all_gather(cotangent[micro_step], "mp", axis=0, tiled=True)
        grad_context = contract_cols(grad_group, w_out)
        grad_activated = contract_cols(grad_group, w_down)
        grad_hidden = pull_gelu(grad_activated)[0].astype(jnp.bfloat16)
        grad_query_f, grad_key_f, grad_value_f = pull_attn(grad_context)
        grad_query = grad_query_f.astype(jnp.bfloat16)
        grad_key = grad_key_f.astype(jnp.bfloat16)
        grad_value = grad_value_f.astype(jnp.bfloat16)
        micro_grads = (
            contract_rows(group_one, grad_query),
            contract_rows(group_one, grad_key),
            contract_rows(group_one, grad_value),
            contract_rows(context_low, grad_group),
            contract_rows(group_two, grad_hidden),
            contract_rows(activated_low, grad_group),
        )
        grad_sums = [total + term for total, term in zip(grad_sums, micro_grads)]
        part_one = (
            contract_cols(grad_query, w_query)
            + contract_cols(grad_key, w_key)
            + contract_cols(grad_value, w_value)
        )
        part_two = contract_cols(grad_hidden, w_up)
        sum_one, sum_two = (
            lax.psum_scatter(
                part_one.astype(jnp.bfloat16), "mp", scatter_dimension=0, tiled=True
            ).astype(jnp.float32),
            lax.psum_scatter(
                part_two.astype(jnp.bfloat16), "mp", scatter_dimension=0, tiled=True
            ).astype(jnp.float32),
        )
        grad_in_one, grad_gain_one, grad_bias_one = pull_one(sum_one)
        grad_in_two, grad_gain_two, grad_bias_two = pull_two(sum_two)
        grad_parts.append(cotangent[micro_step].astype(jnp.float32) + grad_in_one + grad_in_two)
        norm_sums = [
            norm_sums[0] + grad_gain_one,
            norm_sums[1] + grad_bias_one,
            norm_sums[2] + grad_gain_two,
            norm_sums[3] + grad_bias_two,
        ]
    weight_grads = (
        lax.psum_scatter(
            grad_sums[0].astype(jnp.bfloat16), "seq", scatter_dimension=0, tiled=True
        ).astype(jnp.float32),
        lax.psum_scatter(
            grad_sums[1].astype(jnp.bfloat16), "seq", scatter_dimension=0, tiled=True
        ).astype(jnp.float32),
        lax.psum_scatter(
            grad_sums[2].astype(jnp.bfloat16), "seq", scatter_dimension=0, tiled=True
        ).astype(jnp.float32),
        lax.psum_scatter(
            grad_sums[3].astype(jnp.bfloat16), "seq", scatter_dimension=1, tiled=True
        ).astype(jnp.float32),
        lax.psum_scatter(
            grad_sums[4].astype(jnp.bfloat16), "seq", scatter_dimension=0, tiled=True
        ).astype(jnp.float32),
        lax.psum_scatter(
            grad_sums[5].astype(jnp.bfloat16), "seq", scatter_dimension=1, tiled=True
        ).astype(jnp.float32),
    )
    norm_grads = lax.psum((norm_sums[0], norm_sums[1], norm_sums[2], norm_sums[3]), ("seq", "mp"))
    return (
        jnp.stack(mixed_parts),
        jnp.stack(grad_parts),
        norm_grads[0],
        norm_grads[1],
        norm_grads[2],
        norm_grads[3],
        weight_grads[0],
        weight_grads[1],
        weight_grads[2],
        weight_grads[3],
        weight_grads[4],
        weight_grads[5],
    )


def mm(left, right, dims=NN):
    return lax.dot_general(left, right, dims, preferred_element_type=F32)


def split(values):
    high = values.astype(BF16)
    return high, (values - high.astype(F32)).astype(BF16)


def mm3(values, high, low, dims=NN):
    first, second = split(values)
    return mm(first, high, dims) + (mm(second, high, dims) + mm(first, low, dims))


def lane_head(shape):
    return lax.broadcasted_iota(jnp.int32, shape, len(shape) - 1) // HEAD_DIM


def block_diag(state):
    width = state.shape[1]
    tall = jnp.concatenate([state] * (width // HEAD_DIM), axis=0)
    rows = lax.broadcasted_iota(jnp.int32, tall.shape, 0) // HEAD_DIM
    return jnp.where(rows == lane_head(tall.shape), tall, 0.0)


def diag_blocks(full):
    width = full.shape[1]
    lanes = lane_head((HEAD_DIM, width))
    total = jnp.zeros((HEAD_DIM, width), F32)
    for head in range(width // HEAD_DIM):
        part = full[head * HEAD_DIM : (head + 1) * HEAD_DIM, :]
        total = total + jnp.where(lanes == head, part, 0.0)
    return total


def head_sums(values):
    width = values.shape[1]
    rows = lax.broadcasted_iota(jnp.int32, (width, width), 0) // HEAD_DIM
    ones = jnp.where(rows == lane_head((width, width)), 1.0, 0.0).astype(BF16)
    high, low = split(values)
    return mm(high, ones) + mm(low, ones)


def swap_halves(values):
    width = values.shape[1]
    half = ROT // 2
    lane = lax.broadcasted_iota(jnp.int32, values.shape, 1) % HEAD_DIM
    return jnp.where(
        lane < half, pltpu.roll(values, width - half, 1), pltpu.roll(values, half, 1)
    )


def turn(values, cos, sin):
    reps = values.shape[1] // cos.shape[1]
    cosw = jnp.concatenate([cos] * reps, axis=1)
    sinw = jnp.concatenate([sin] * reps, axis=1)
    return values * cosw + swap_halves(values) * sinw


def normalize(values):
    centered = values - jnp.mean(values, axis=-1, keepdims=True)
    variance = jnp.mean(centered * centered, axis=-1, keepdims=True)
    scale = lax.rsqrt(variance + 1e-05)
    return centered * scale, scale


class Rows:
    def __init__(self, scal, seq, chunk, docs):
        rows = chunk // 2
        self.here = (scal[1] * 2 + (scal[2] // 2 + seq) % 2) * chunk
        side = scal[2] % 2
        low = self.here + side * rows
        high = self.here + (1 - side) * rows - rows

        def places(shape, axis):
            count = lax.broadcasted_iota(jnp.int32, shape, axis)
            return jnp.where(count < rows, count + low, count + high)

        self.place = places((chunk, 1), 0)
        self.across = places((1, chunk), 1)
        self.start = jnp.zeros((chunk, 1), jnp.int32)
        end = jnp.zeros((chunk, 1), jnp.int32)
        base = 4 + seq * 2 * docs
        for doc in range(docs):
            first, last = scal[base + doc], scal[base + docs + doc]
            inside = (self.place >= first) & (self.place < last)
            self.start = jnp.where(inside, first, self.start)
            end = jnp.where(inside, last, end)
        self.came = self.start < self.here
        self.goes = end > self.here + chunk

    def mask(self):
        return (self.across >= self.start) & (self.across <= self.place)


def whole(array):
    zeros = (0,) * array.ndim
    return (array, tuple(array.shape), lambda *_: zeros)


class Seq(tuple):
    pass


def by_seq(array, per=1):
    rest = (0,) * (array.ndim - 1)
    return Seq((array, (per,) + tuple(array.shape[1:]), lambda i, s: (i,) + rest))


def own_seq(array, per=1):
    rest, most = (0,) * (array.ndim - 1), array.shape[0] // per - 1
    return Seq(
        (array, (per,) + tuple(array.shape[1:]), lambda i, s: (jnp.minimum(i, most),) + rest)
    )


def away_seq(array, per=1):
    rest, count = (0,) * (array.ndim - 1), array.shape[0] // per
    return Seq(
        (array, (per,) + tuple(array.shape[1:]), lambda i, s: (jnp.maximum(i - count, 0),) + rest)
    )


def new(shape, kind):
    return jax.ShapeDtypeStruct(shape, kind)


def call(name, body, scal, grid, ins, outs, scratch=(), aliases=None):
    return pl.pallas_call(
        body,
        name=name,
        grid_spec=pltpu.PrefetchScalarGridSpec(
            num_scalar_prefetch=1,
            grid=grid or (1,),
            in_specs=[
                pl.BlockSpec(block, index) if index else pl.BlockSpec(memory_space=pl.ANY)
                for _, block, index in ins
            ],
            out_specs=[pl.BlockSpec(block, index) for _, block, index in outs],
            scratch_shapes=list(scratch),
        ),
        out_shape=[array for array, _, _ in outs],
        input_output_aliases=aliases or {},
        compiler_params=pltpu.CompilerParams(
            dimension_semantics=("arbitrary",) * max(len(grid), 1), vmem_limit_bytes=VMEM_LIMIT
        ),
    )(scal, *[array for array, _, _ in ins])


def seq_call(name, body, scal, count, ins, outs, scratch=(), per=PER):
    marks = [isinstance(part, Seq) for part in list(ins) + list(outs)]

    def step(scal, *refs):
        for k in range(per):
            views = [ref.at[pl.ds(k, 1)] if mark else ref for ref, mark in zip(refs, marks)]
            body(k, pl.program_id(0) * per + k, scal, *views, *refs[len(marks) :])

    return call(name, step, scal, (count // per,), ins, outs, scratch)


class Shape:
    def __init__(self, pairs, chunks, dim, half_units, half_ff, chunk, docs):
        self.pairs, self.chunks, self.dim = pairs, chunks, dim
        self.hu, self.hf, self.chunk, self.docs = half_units, half_ff, chunk, docs
        self.dp = dim // pairs
        self.width, self.ff = chunks * half_units, chunks * half_ff
        self.half = 0

    def cols(self, scal, slot):
        start = ((scal[0] + slot) % self.pairs) * self.dp
        return pl.ds(pl.multiple_of(start, 128), self.dp)


def fill_rows(sh, target, blocks, first, size, at):
    for slot in range(sh.pairs):
        for j in range(sh.chunks):
            part = blocks[slot * sh.chunks + j][first : first + size, :]
            target[slot, at + j * size : at + (j + 1) * size, :] = part


def pack_body(scal, q, k, v, out, up, down, keep_a, send_a, send_u, send_d):
    low = scal[3] == 0
    parts_keep, parts_send = [], []
    for ref in (q, k, v):
        flat = jnp.transpose(ref[...].astype(F32))
        half = flat.shape[0] // 2
        parts_keep.append(jnp.where(low, flat[:half], flat[half:]))
        parts_send.append(jnp.where(low, flat[half:], flat[:half]))
    flat = out[...].astype(F32)
    half = flat.shape[0] // 2
    parts_keep.append(jnp.where(low, flat[:half], flat[half:]))
    parts_send.append(jnp.where(low, flat[half:], flat[:half]))
    keep_a[...] = jnp.concatenate(parts_keep, 0).astype(BF16)
    send_a[...] = jnp.concatenate(parts_send, 0).astype(BF16)
    half = up.shape[1] // 2
    send_u[...] = jnp.where(low, up[:, half:], up[:, :half])
    half = down.shape[0] // 2
    send_d[...] = jnp.where(low, down[half:, :], down[:half, :])


def norm_body(scal, rows, g1, b1, g2, b2, *refs):
    one, two = refs[-2:]
    n, _ = normalize(rows[0].astype(F32))
    one[0] = (n * g1[...] + b1[...]).astype(BF16)
    two[0] = (n * g2[...] + b2[...]).astype(BF16)


def attend_body(sh, k, seq, scal, normed, cos, sin, ph, pw, wts, *refs):
    blocks = refs[: sh.pairs * sh.chunks]
    fq_out, fk_out, v_out, num_out, den_out, st_out, wt = refs[sh.pairs * sh.chunks :]
    width = sh.width

    if k == 0:

        @pl.when(seq == 0)
        def _():
            for kind in range(3):
                fill_rows(sh, wt, blocks, kind * sh.hu, sh.hu, kind * width)

    qkv = mm(normed[0, :, sh.cols(scal, 0)], wt[0], NT)
    for slot in range(1, sh.pairs):
        qkv = qkv + mm(normed[0, :, sh.cols(scal, slot)], wt[slot], NT)

    def feats(values):
        return jnp.exp(mm3(turn(values, cos[0], sin[0]), ph[...], pw[...]))

    fqb = (feats(qkv[:, :width]) * wts[...]).astype(BF16)
    fk = feats(qkv[:, width : 2 * width])
    fkb = fk.astype(BF16)
    v = qkv[:, 2 * width :]
    vb = v.astype(BF16)
    fq_out[0] = fqb
    fk_out[0] = fkb
    v_out[0] = v
    rows = Rows(scal, seq, sh.chunk, sh.docs)
    mask = rows.mask()
    lanes = lane_head(vb.shape)
    num = jnp.zeros(vb.shape, F32)
    den = jnp.zeros(vb.shape, F32)
    for head in range(width // HEAD_DIM):
        mine = lanes == head
        scores = mm(jnp.where(mine, fqb, 0), fkb, NT)
        scores = jnp.where(mask, scores, 0.0).astype(BF16)
        both = mm(scores, jnp.where(mine, vb, 1))
        num = jnp.where(mine, both, num)
        den = jnp.where(mine, pltpu.roll(both, HEAD_DIM, 1), den)
    num_out[0] = num
    den_out[0] = den
    kept = jnp.where(rows.goes, fk, 0.0)
    store_state(sh, scal, st_out, mm(kept.astype(BF16), vb, TN), kept)


def store_state(sh, scal, st_out, sums, totals):
    tail = jnp.broadcast_to(
        jnp.sum(totals, axis=0, keepdims=True), (STATE_ROWS - HEAD_DIM, sh.width)
    )
    state = jnp.concatenate([diag_blocks(sums), tail], axis=0)
    st_out[0] = pltpu.roll(state, scal[1] * sh.hu, 1).astype(BF16)


def load_state(sh, scal, carry):
    state = pltpu.roll(carry[0], (sh.width - scal[1] * sh.hu) % sh.width, 1)
    return state[:HEAD_DIM], state[HEAD_DIM : HEAD_DIM + 1]


def up_body(sh, k, seq, scal, normed, *refs):
    blocks = refs[: sh.pairs * sh.chunks]
    act_out, slope_out, wu = refs[sh.pairs * sh.chunks :]

    if k == 0:

        @pl.when(seq == 0)
        def _():
            for slot in range(sh.pairs):
                for j in range(sh.chunks):
                    wu[slot, :, j * sh.hf : (j + 1) * sh.hf] = blocks[slot * sh.chunks + j][...]

    hidden = mm(normed[0, :, sh.cols(scal, 0)], wu[0])
    for slot in range(1, sh.pairs):
        hidden = hidden + mm(normed[0, :, sh.cols(scal, slot)], wu[slot])
    cdf = 0.5 + 0.5 * lax.erf(hidden * math.sqrt(0.5))
    act_out[0] = (hidden * cdf).astype(BF16)
    bell = jnp.exp(-0.5 * hidden * hidden) * math.sqrt(0.5 / math.pi)
    slope_out[0] = (cdf + hidden * bell).astype(BF16)


def finish_body(sh, k, seq, scal, num, den, fq, carry, ctx_out, rden_out):
    fqb = fq[0]
    sums, totals = load_state(sh, scal, carry)
    more_num = mm(fqb, block_diag(sums).astype(BF16))
    more_den = head_sums(fqb.astype(F32) * totals)
    came = Rows(scal, seq, sh.chunk, sh.docs).came
    inverse = 1.0 / (den[0] + jnp.where(came, more_den, 0.0))
    ctx_out[0] = (num[0] + jnp.where(came, more_num, 0.0)) * inverse
    rden_out[0] = inverse


def store_half(sh, seq, cols, part, own_out, away_out):
    own_out[0, :, cols] = jnp.where(seq < sh.half, part, own_out[0, :, cols])
    away_out[0, :, cols] = part


def branch_body(sh, k, seq, scal, ctx, act, *refs):
    count = sh.pairs * sh.chunks
    blocks_a, blocks_d = refs[:count], refs[count : 2 * count]
    own_out, away_out, wo, wd = refs[2 * count :]

    if k == 0:

        @pl.when(seq == 0)
        def _():
            fill_rows(sh, wo, blocks_a, 3 * sh.hu, sh.hu, 0)
            fill_rows(sh, wd, blocks_d, 0, sh.hf, 0)

    ctxb = ctx[0].astype(BF16)
    for slot in range(sh.pairs):
        part = (mm(act[0], wd[slot]) + mm(ctxb, wo[slot])).astype(BF16)
        store_half(sh, seq, sh.cols(scal, slot), part, own_out, away_out)


def pick(own, away, seq, scal, sh, slot):
    first = seq < sh.half
    cols = sh.cols(scal, slot)
    return jnp.where(first, own[0, :, cols], away[0, :, cols])


def hidden_body(sh, k, seq, scal, own, away, slope, *refs):
    blocks = refs[: sh.pairs * sh.chunks]
    out, wd = refs[sh.pairs * sh.chunks :]

    if k == 0:

        @pl.when(seq == 0)
        def _():
            fill_rows(sh, wd, blocks, 0, sh.hf, 0)

    grad = mm(pick(own, away, seq, scal, sh, 0), wd[0], NT)
    for slot in range(1, sh.pairs):
        grad = grad + mm(pick(own, away, seq, scal, sh, slot), wd[slot], NT)
    out[0] = (grad * slope[0].astype(F32)).astype(BF16)


def back_body(sh, k, seq, scal, own, away, fq, fk, vals, ctx, rden, carry, cos, sin, ph, pw, *refs):
    blocks = refs[: sh.pairs * sh.chunks]
    dq_out, dk_out, dv_out, st_out, wo = refs[sh.pairs * sh.chunks :]
    width = sh.width

    if k == 0:

        @pl.when(seq == 0)
        def _():
            fill_rows(sh, wo, blocks, 3 * sh.hu, sh.hu, 0)

    gctx = mm(pick(own, away, seq, scal, sh, 0), wo[0], NT)
    for slot in range(1, sh.pairs):
        gctx = gctx + mm(pick(own, away, seq, scal, sh, slot), wo[slot], NT)
    inverse = rden[0]
    dnum = gctx * inverse
    dden = -head_sums(gctx * ctx[0]) * inverse
    fqb, fkb, v = fq[0], fk[0], vals[0]
    rows = Rows(scal, seq, sh.chunk, sh.docs)
    mask = rows.mask()
    lanes = lane_head(v.shape)
    lane = lax.broadcasted_iota(jnp.int32, v.shape, 1) % HEAD_DIM
    dn_high, dn_low = split(dnum)
    v_high, v_low = split(v)
    dd_high = dden.astype(BF16).astype(F32)
    roll = lambda values: pltpu.roll(values.astype(F32), HEAD_DIM, 1).astype(BF16)
    den_part = jnp.where(lane == 0, dd_high, jnp.where(lane == 1, dden - dd_high, 0.0))
    den_part = den_part.astype(BF16)
    dn_high_beside, dn_low_beside = roll(dn_high), roll(dn_low)
    v_high_beside, v_low_beside = roll(v_high), roll(v_low)

    dfq = jnp.zeros(v.shape, F32)
    dfk = jnp.zeros(v.shape, F32)
    dv = jnp.zeros(v.shape, F32)
    for head in range(width // HEAD_DIM):
        mine = lanes == head
        left = [jnp.where(mine, dn_high, dn_low_beside), jnp.where(mine, den_part, dn_high_beside)]
        right = [jnp.where(mine, v_high, v_high_beside), jnp.where(mine, 1, v_low_beside)]
        dscores = mm(jnp.concatenate(left, axis=1), jnp.concatenate(right, axis=1), NT)
        dscores = jnp.where(mask, dscores, 0.0).astype(BF16)
        scores = mm(jnp.where(mine, fqb, 0), fkb, NT)
        scores = jnp.where(mask, scores, 0.0).astype(BF16)
        dfq = jnp.where(mine, mm(dscores, fkb), dfq)
        dfk = jnp.where(mine, mm(dscores, fqb, TN), dfk)
        dv = jnp.where(mine, mm(scores, dn_high, TN), dv)
    sums, totals = load_state(sh, scal, carry)
    more = mm(dn_high, block_diag(sums).astype(BF16), NT) + dden * totals
    dfq = dfq + jnp.where(rows.came, more, 0.0)
    fqf = fqb.astype(F32)
    used = jnp.where(rows.came, fqf, 0.0)
    store_state(sh, scal, st_out, mm(used.astype(BF16), dn_high, TN), used * dden)
    turned = mm3(dfq * fqf, ph[...], pw[...], NT)
    dq_out[0] = turn(turned, cos[0], -sin[0]).astype(BF16)
    dk_out[0] = dfk
    dv_out[0] = dv


def last_body(sh, k, seq, scal, dfk, dv, fk, vals, carry, cos, sin, ph, pw, dk_out, dv_out):
    fkb = fk[0]
    sums, totals = load_state(sh, scal, carry)
    state = block_diag(sums).astype(BF16)
    goes = Rows(scal, seq, sh.chunk, sh.docs).goes
    more_k = mm(vals[0].astype(BF16), state, NT) + totals
    total_k = dfk[0] + jnp.where(goes, more_k, 0.0)
    dv_out[0] = (dv[0] + jnp.where(goes, mm(fkb, state), 0.0)).astype(BF16)
    turned = mm3(total_k * fkb.astype(F32), ph[...], pw[...], NT)
    dk_out[0] = turn(turned, cos[0], -sin[0]).astype(BF16)


def unit_grad_body(with_got, scal, left, *refs):
    many, with_got = with_got
    rights, refs = refs[:many], refs[many:]
    at, grad = 0, None
    for right in rights:
        part = mm(left[at : at + right.shape[0], :], right[...], TN)
        at += right.shape[0]
        grad = part if grad is None else grad + part
    if not with_got:
        refs[0][0] = grad.astype(BF16)
        return
    value = (grad + refs[0][0].astype(F32)).astype(BF16)
    j = pl.program_id(0)
    for step, out in enumerate(refs[1:]):

        @pl.when(j == step)
        def _():
            out[...] = value


def head_grad_body(sh, with_got, scal, dq, dk, dv, ctx, normed, own, away, *refs):
    scratch = refs[-1]
    for kind, ref in enumerate((dq, dk, dv)):
        scratch[kind] = mm(ref[...], normed[...], TN)
    half = own.shape[0]
    scratch[3] = mm(ctx[:half, :].astype(BF16), own[...], TN) + mm(
        ctx[half:, :].astype(BF16), away[...], TN
    )
    for j in range(sh.chunks):
        rows = slice(j * sh.hu, (j + 1) * sh.hu)
        value = jnp.concatenate([scratch[kind, rows, :] for kind in range(4)], axis=0)
        if with_got:
            refs[1 + j][...] = (value + refs[0][j].astype(F32)).astype(BF16)
        else:
            refs[0][j] = value.astype(BF16)


def rows_grad_body(sh, k, seq, scal, dq, dk, dv, gh, own, away, g1, g2, *refs):
    count = sh.pairs * sh.chunks
    blocks_a, blocks_u = refs[:count], refs[count : 2 * count]
    own_out, away_out, sums, wt, wu, n_ref = refs[2 * count :]

    if k == 0:

        @pl.when(seq == 0)
        def _():
            for kind in range(3):
                fill_rows(sh, wt, blocks_a, kind * sh.hu, sh.hu, kind * sh.width)
            for slot in range(sh.pairs):
                for j in range(sh.chunks):
                    wu[slot, :, j * sh.hf : (j + 1) * sh.hf] = blocks_u[slot * sh.chunks + j][...]
            sums[...] = jnp.zeros(sums.shape, F32)

    x = jnp.where(seq < sh.half, own[0], away[0]).astype(F32)
    n_ref[...] = normalize(x)[0]
    qkv = jnp.concatenate([dq[0], dk[0], dv[0]], axis=1)
    for slot in range(sh.pairs):
        cols = sh.cols(scal, slot)
        one = mm(qkv, wt[slot])
        two = mm(gh[0], wu[slot], NT)
        n = n_ref[:, cols]
        for at, value in enumerate((one * n, one, two * n, two)):
            line = slice(at, at + 1)
            sums[line, cols] = sums[line, cols] + jnp.sum(value, axis=0, keepdims=True)
        e = (one * g1[:, cols] + two * g2[:, cols]).astype(BF16)
        store_half(sh, seq, cols, e, own_out, away_out)


def tokens_grad_body(scal, mine, got, tokens, cot, out):
    e = mine[0].astype(F32) + got[0].astype(F32)
    n, scale = normalize(tokens[0].astype(F32))
    shift = jnp.mean(e, axis=-1, keepdims=True) + n * jnp.mean(e * n, axis=-1, keepdims=True)
    out[0] = cot[0].astype(F32) + scale * (e - shift)


def join_units(scal, keep, got):
    low = scal[3] == 0
    mine, other = keep[...].astype(F32), got[...].astype(F32)
    return jnp.where(low, mine, other), jnp.where(low, other, mine)


def end_units_body(sh, scal, keep_u, got_u, keep_d, got_d, up, down):
    first, second = join_units(scal, keep_u, got_u)
    up[:, : sh.hf] = jnp.transpose(first)
    up[:, sh.hf :] = jnp.transpose(second)
    first, second = join_units(scal, keep_d, got_d)
    down[: sh.hf, :] = first
    down[sh.hf :, :] = second


def end_heads_body(sh, scal, keep, got, *outs):
    first, second = join_units(scal, keep, got)
    for kind in range(4):
        rows = slice(kind * sh.hu, (kind + 1) * sh.hu)
        both = jnp.concatenate([first[rows], second[rows]], axis=0)
        outs[kind][...] = both if kind == 3 else jnp.transpose(both)


class Layout:
    def __init__(self):
        self.seqs, self.parts = lax.axis_size("seq"), lax.axis_size("mp")
        self.pairs, self.chunks = self.seqs // 2, self.parts // 4
        seq, part = lax.axis_index("seq"), lax.axis_index("mp")
        self.pair, self.core = seq // 2, seq % 2
        self.hi, self.lo = part // 4, part % 4

    def move(self, values, rule):
        links = []
        for seq in range(self.seqs):
            for part in range(self.parts):
                there = rule(seq // 2, seq % 2, part // 4, part % 4)
                if there is not None:
                    pair, core, hi, lo = there
                    goal = (pair * 2 + core) * self.parts + hi * 4 + lo
                    links.append((seq * self.parts + part, goal))
        return lax.ppermute(values, AXES, links)

    def core_swap(self, values):
        return self.move(values, lambda p, c, h, l: (p, 1 - c, h, l))

    def lo_swap(self, values, bit):
        return self.move(values, lambda p, c, h, l: (p, c, h, l ^ bit))

    def pair_step(self, values, way):
        return self.move(values, lambda p, c, h, l: ((p + way) % self.pairs, c, h, l))

    def hi_step(self, values, way):
        return self.move(values, lambda p, c, h, l: (p, c, (h + way) % self.chunks, l))


def after(value, *others):
    return lax.optimization_barrier((value,) + others)[0]


def hold(values, *others):
    return lax.optimization_barrier(tuple(values) + others)[: len(values)]


def in_order(lay, one, two):
    flip = lay.lo >= 2
    return jnp.where(flip, two, one), jnp.where(flip, one, two)


def send_states(lay, local, scale, backward):
    states = local.astype(F32).reshape((-1, 2) + local.shape[1:])
    first, second = in_order(lay, states[:, 0], states[:, 1])
    if backward:
        out, goal = first + second * scale(0, 1), 0
    else:
        out, goal = second + first * scale(1, 2), 1
    return lay.move(
        out.astype(BF16), lambda p, c, h, l: (p, c, goal, l) if h != goal else None
    )


def combine_states(lay, local, got, scale, backward):
    states = local.astype(F32).reshape((-1, 2) + local.shape[1:])
    first, second = in_order(lay, states[:, 0], states[:, 1])
    got = got.astype(F32)
    if backward:
        first, second = second + got * scale(1, 2), got
    else:
        first, second = got, first + got * scale(0, 1)
    return jnp.stack(in_order(lay, first, second), 1).reshape(local.shape)


def erf_inverse(target):
    low, high = -6.0, 6.0
    for _ in range(60):
        middle = 0.5 * (low + high)
        low, high = (middle, high) if math.erf(middle) < target else (low, middle)
    guess = 0.5 * (low + high)
    for _ in range(3):
        gap = math.erf(guess) - target
        guess -= gap * math.exp(guess * guess) * math.sqrt(math.pi) / 2.0
    return guess


@functools.lru_cache(None)
def tables(heads):
    primes = prime_list(HEAD_DIM)
    points = np.zeros((FEATS, HEAD_DIM))
    for row in range(FEATS):
        for col in range(HEAD_DIM):
            share = min(max((row + 0.5) * math.sqrt(primes[col]) % 1.0, 0.001), 0.999)
            points[row, col] = math.sqrt(2.0) * erf_inverse(2.0 * float(np.float32(share)) - 1.0)
    cells = np.arange(HEAD_DIM)
    cosine = np.cos(np.pi * (cells[None, :] + 0.5) * cells[:, None] / HEAD_DIM)
    cosine = cosine * math.sqrt(2.0 / HEAD_DIM)
    cosine[0] *= math.sqrt(0.5)
    project = np.kron(np.eye(heads), (points @ cosine).T / math.sqrt(HEAD_DIM))
    project = project.astype(np.float32)
    high = project.astype(BF16)
    low = (project - high.astype(np.float32)).astype(BF16)
    weighting = 1.0 / (1.0 + np.sum(points * points, axis=1) / HEAD_DIM)
    return high, low, np.tile(weighting, heads)[None, :].astype(np.float32)


def team_local(
    tokens,
    ln1_gain,
    ln1_bias,
    ln2_gain,
    ln2_bias,
    q_weight,
    k_weight,
    value_weight,
    out_weight,
    up_weight,
    down_weight,
    lengths,
    cotangent,
):
    lay = Layout()
    micro, rows, dim = tokens.shape
    drows, units = q_weight.shape
    docs = lengths.shape[2]
    chunk = 2 * rows
    half_units, half_ff = units // 2, up_weight.shape[1] // 2
    sh = Shape(lay.pairs, lay.chunks, dim, half_units, half_ff, chunk, docs)
    width, ff, dp = sh.width, sh.ff, sh.dp
    half = 2 * micro
    count = 2 * half
    sh.half = half
    total = count * chunk
    whole_rows = lambda array: array.reshape(total, array.shape[-1])
    bind = lambda body, *first: functools.partial(body, *first)
    gains = [vec.reshape(1, dim) for vec in (ln1_gain, ln1_bias, ln2_gain, ln2_bias)]

    own_lengths = lengths[:, 0]
    table = jnp.stack([own_lengths, lay.core_swap(own_lengths)]).reshape(half, docs)
    seq_ends = jnp.cumsum(table, axis=1)
    seq_starts = seq_ends - table
    starts, ends = jnp.repeat(seq_starts, 2, axis=0), jnp.repeat(seq_ends, 2, axis=0)
    scal = jnp.concatenate(
        [
            jnp.stack([lay.pair, lay.hi, lay.lo, lay.core]).astype(jnp.int32),
            jnp.concatenate([starts, ends], axis=1).reshape(-1).astype(jnp.int32),
        ]
    )
    places = jnp.stack([lay.core, lay.core, lay.core, lay.core]).astype(jnp.int32)
    core_only = places

    block_shape = [(4 * half_units, drows), (drows, half_ff), (half_ff, drows)]
    keep_a, send_a, send_u, send_d = call(
        "pack", pack_body, core_only, (),
        [whole(w) for w in (q_weight, k_weight, value_weight, out_weight, up_weight, down_weight)],
        [whole(new(shape, BF16)) for shape in [block_shape[0]] + block_shape],
    )
    first_core = lay.core == 0

    def join(keep, got, axis):
        return jnp.where(
            first_core, jnp.concatenate([keep, got], axis), jnp.concatenate([got, keep], axis)
        )

    got_a, got_u, got_d = lax.optimization_barrier(
        tuple(lay.core_swap(send) for send in (send_a, send_u, send_d))
    )
    block_a = join(keep_a, got_a, 1)
    split_at = micro // 2

    def first_swaps(values):
        return lay.lo_swap(values, 1), lay.lo_swap(values, 2)

    def second_swaps(by_y, by_z):
        return lay.lo_swap(by_z[:split_at], 1), lay.lo_swap(by_y[split_at:], 2)

    def team_rows(values, by_y, by_z, both):
        both = jnp.concatenate(both, 0)
        own = jnp.stack([jnp.stack([values, by_y], 1), jnp.stack([by_z, both], 1)], 1)
        own = own.reshape(half, chunk, dim)
        return own, lay.core_swap(own)

    def cross(values):
        return lay.pair_step(values, -1)

    def beside(values):
        return lay.hi_step(values, -1)

    block_a, own_tokens = hold((block_a, tokens), got_a)
    by_y, by_z = first_swaps(own_tokens)
    beside_a, cross_a = beside(block_a), cross(block_a)
    late_up, late_down = hold((up_weight, down_weight), block_a)
    keep_u = jnp.where(first_core, late_up[:, :half_ff], late_up[:, half_ff:])
    keep_d = jnp.where(first_core, late_down[:half_ff], late_down[half_ff:])
    block_u, block_d = join(keep_u, got_u, 0), join(keep_d, got_d, 1)
    cross_u = cross(block_u)

    here = (2 * lay.hi + (lay.lo // 2 + jnp.arange(count, dtype=jnp.int32)) % 2) * chunk
    step = jnp.arange(rows, dtype=jnp.int32)
    side = (lay.lo % 2) * rows
    places = here[:, None] + jnp.concatenate([side + step, rows - side + step])[None, :]
    start = jnp.zeros((count, chunk), jnp.int32)
    for doc in range(docs):
        first = starts[:, doc : doc + 1]
        start = jnp.where(places >= first, first, start)
    offset = after((places - start).astype(F32), block_a)
    lane = np.arange(128) % HEAD_DIM
    turned = lane < ROT
    inverse = np.where(turned, 10000.0 ** (-(lane % (ROT // 2)) * 2.0 / ROT), 0.0)
    side = np.where(turned, np.where(lane < ROT // 2, -1.0, 1.0), 0.0)
    angles = offset[:, :, None] * jnp.asarray(inverse, F32)[None, None, :]
    cos = jnp.cos(angles)
    sin = jnp.sin(angles) * jnp.asarray(side, F32)[None, None, :]
    cos, sin = lax.optimization_barrier((cos, sin))

    by_y, by_z, beside_a, cross_a, cross_u, block_d, cos, sin = hold(
        (by_y, by_z, beside_a, cross_a, cross_u, block_d, cos, sin)
    )
    both = second_swaps(by_y, by_z)
    across_a, cross_d = cross(beside_a), cross(block_d)
    both = hold(both, across_a)
    x_own, x_away = team_rows(tokens, by_y, by_z, both)

    high, low, weighting = tables(width // HEAD_DIM)
    maps = [whole(jnp.asarray(high)), whole(jnp.asarray(low))]
    turns = [by_seq(cos, PER), by_seq(sin, PER)]
    turns_one = [by_seq(cos), by_seq(sin)]

    def straddles(first, second):
        lower, higher = jnp.minimum(first, second), jnp.maximum(first, second)
        return jnp.any((seq_starts < lower) & (seq_ends > higher), axis=1).astype(F32)

    edges = [(2 * lay.hi + step) * chunk for step in range(3)]
    scale = lambda a, b: straddles(edges[a], edges[b])[:, None, None]

    rows_new = lambda size, kind: by_seq(new((count, chunk, size), kind), PER)
    rows_one = lambda size, kind: by_seq(new((count, chunk, size), kind))
    state_one = by_seq(new((count, STATE_ROWS, width), BF16))
    norm_ins = [whole(vec) for vec in gains]
    norm_outs = [by_seq(new((count, chunk, dim), BF16))] * 2
    n_one, n_two = call(
        "norms_own", norm_body, core_only, (half,), [by_seq(x_own)] + norm_ins, norm_outs
    )
    n_one, n_two, x_away, block_u, cross_u, block_d, cross_d, cot = hold(
        (n_one, n_two, x_away, block_u, cross_u, block_d, cross_d, cotangent)
    )
    beside_u, across_u = beside(block_u), beside(cross_u)
    cot_y, cot_z = first_swaps(cot)
    beside_d = beside(block_d)
    rest = lambda i, s: (i + half, 0, 0)
    n_one, n_two = call(
        "norms_away", norm_body, core_only, (half,),
        [by_seq(x_away)] + norm_ins + [(n_one, None, None), (n_two, None, None)],
        [(array, block, rest) for array, block, _ in norm_outs], aliases={6: 0, 7: 1},
    )
    in_a = [whole(block) for block in (block_a, beside_a, cross_a, across_a)]
    fq, fk, vals, num, den, state = seq_call(
        "attend", bind(attend_body, sh), scal, count,
        [by_seq(n_one)] + turns_one + maps + [whole(jnp.asarray(weighting))] + in_a,
        [rows_one(width, BF16)] * 2 + [rows_one(width, F32)] * 3 + [state_one],
        [pltpu.VMEM((sh.pairs, 3 * width, dp), BF16)],
        per=1,
    )
    n_two, fq, state, beside_u, across_u, cot_y, cot_z = hold(
        (n_two, fq, state, beside_u, across_u, cot_y, cot_z)
    )
    in_u = [whole(block) for block in (block_u, beside_u, cross_u, across_u)]
    state_got = send_states(lay, state, scale, False)
    cot_both = second_swaps(cot_y, cot_z)
    act, slope = seq_call(
        "up", bind(up_body, sh), scal, count, [by_seq(n_two, PER)] + in_u,
        [rows_new(ff, BF16)] * 2, [pltpu.VMEM((sh.pairs, dp, ff), BF16)],
    )
    act, num, state_got, beside_d, cot_both0, cot_both1 = hold(
        (act, num, state_got, beside_d) + cot_both
    )
    across_d = cross(beside_d)
    g_own, g_away = team_rows(cotangent, cot_y, cot_z, (cot_both0, cot_both1))
    carry = combine_states(lay, state, state_got, scale, False)
    ctx, rden = seq_call(
        "finish", bind(finish_body, sh), scal, count,
        [by_seq(a, PER) for a in (after(num, g_own), den, fq, carry)], [rows_new(width, F32)] * 2,
    )
    g_own, g_away, ctx, across_d = hold((g_own, g_away, ctx, across_d))
    in_d = [whole(block) for block in (block_d, beside_d, cross_d, across_d)]

    def cols_of(array, slot):
        pairs = sh.pairs
        index = lambda *ids: (0, (ids[-1][0] + slot) % pairs)
        return (array, (array.shape[0], dp), index)

    def lanes_of(array, size):
        return (array, (array.shape[0], size), lambda j, s: (0, j))

    def block_of(array):
        rest = tuple(array.shape[1:])
        return (array, (1,) + rest, lambda j, s: (j,) + (0,) * len(rest))

    g_rows = [g.reshape(total // 2, dim) for g in (g_own, g_away)]
    unit_shape, head_shape = (half_ff, dp), (4 * half_units, dp)

    def unit_grads(name, left, rights, slot, got=None):
        final = slot == 0
        outs = [whole(new(unit_shape, BF16))] * sh.chunks
        if not final:
            outs = [block_of(new((sh.chunks,) + unit_shape, BF16))]
        return call(
            name + str(slot), bind(unit_grad_body, (len(rights), got is not None)), scal,
            (sh.chunks,),
            [lanes_of(left, half_ff)] + [cols_of(right, slot) for right in rights]
            + ([] if got is None else [block_of(got)]),
            outs,
        )

    def head_grads(parts, slot, got=None):
        final = slot == 0
        outs = [whole(new(head_shape, BF16))] * sh.chunks
        if not final:
            outs = [whole(new((sh.chunks,) + head_shape, BF16))]
        return call(
            "head_grad" + str(slot), bind(head_grad_body, sh, got is not None), scal, (),
            [whole(whole_rows(a)) for a in parts] + [cols_of(whole_rows(n_one), slot)]
            + [cols_of(g, slot) for g in g_rows] + ([] if got is None else [whole(got)]),
            outs, [pltpu.VMEM((4, width, dp), F32)],
        )

    def pair_sums(make):
        got = None
        for slot in range(sh.pairs - 1, 0, -1):
            part = make(slot, got)[0]
            got = lay.pair_step(part, 1)
        return part, got

    def hi_sums(parts):
        term = parts[sh.chunks - 1]
        for j in range(sh.chunks - 2, -1, -1):
            term = lay.hi_step(term, 1)
            if j:
                term = (term.astype(F32) + parts[j].astype(F32)).astype(BF16)
        return term, parts[0]

    def trade(ends, *others):
        sums = (ends[0].astype(F32) + ends[1].astype(F32)).astype(BF16)
        first, second = sums[:, :drows], sums[:, drows:]
        keep = jnp.where(first_core, first, second)
        send = jnp.where(first_core, second, first)
        return [whole(keep), whole(lay.core_swap(send))]

    down_make = lambda slot, got: unit_grads("down_grad", whole_rows(act), g_rows, slot, got)
    down_part, down_got = pair_sums(down_make)

    ctx = after(ctx, down_part)
    halves_one = [
        own_seq(new((half, chunk, dim), BF16)), away_seq(new((half, chunk, dim), BF16))
    ]
    halves_new = [
        own_seq(new((half, chunk, dim), BF16), PER),
        away_seq(new((half, chunk, dim), BF16), PER),
    ]
    branch_own, branch_away = seq_call(
        "branch", bind(branch_body, sh), scal, count,
        [by_seq(ctx, PER), by_seq(act, PER)] + in_a + in_d, halves_new,
        [pltpu.VMEM((sh.pairs, width, dp), BF16), pltpu.VMEM((sh.pairs, ff, dp), BF16)],
    )

    def first_sums(own, away_got):
        both = (own.astype(F32) + away_got.astype(F32)).reshape(micro, 2, 2, rows, dim)
        by_z, by_y = both[:split_at], both[split_at:]
        sends = by_z[:, 1].astype(BF16), by_y[:, :, 1].astype(BF16)
        return (by_z[:, 0].astype(BF16), by_y[:, :, 0].astype(BF16)), sends

    def second_sums(keeps, gots):
        by_z = keeps[0].astype(F32) + gots[0].astype(F32)
        by_y = keeps[1].astype(F32) + gots[1].astype(F32)
        sends = by_z[:, 1].astype(BF16), by_y[:, 1].astype(BF16)
        return (by_z[:, 0].astype(BF16), by_y[:, 0].astype(BF16)), sends

    def round_one(sends):
        return lay.lo_swap(sends[0], 2), lay.lo_swap(sends[1], 1)

    def round_two(sends):
        return lay.lo_swap(sends[0], 1), lay.lo_swap(sends[1], 2)

    join_micro = lambda parts: jnp.concatenate(parts, 0)
    down_got, branch_own, branch_away, ctx = hold((down_got, branch_own, branch_away, ctx))
    m_got = lay.core_swap(branch_away)

    (grad_hidden,) = seq_call(
        "hidden_grad", bind(hidden_body, sh), scal, count,
        [own_seq(g_own, PER), away_seq(g_away, PER), by_seq(after(slope, branch_own), PER)] + in_d,
        [rows_new(ff, BF16)], [pltpu.VMEM((sh.pairs, ff, dp), BF16)],
    )
    branch_own, m_got, grad_hidden, ctx = hold((branch_own, m_got, grad_hidden, ctx))
    m_keeps, m_sends = first_sums(branch_own, m_got)
    m_gots = round_one(m_sends)
    ctx_back = after(ctx, *m_sends)
    dq, dk_part, dv_part, dstate = seq_call(
        "attend_back", bind(back_body, sh), scal, count,
        [own_seq(g_own), away_seq(g_away)]
        + [by_seq(a) for a in (fq, fk, vals, ctx_back, rden, carry)]
        + turns_one + maps + in_a,
        [rows_one(width, BF16), rows_one(width, F32), rows_one(width, F32), state_one],
        [pltpu.VMEM((sh.pairs, width, dp), BF16)],
        per=1,
    )
    dq, dstate, dk_part, grad_hidden, *m_parts = hold(
        (dq, dstate, dk_part, grad_hidden) + m_keeps + m_gots
    )
    state_got = send_states(lay, dstate, scale, True)
    down_parts = down_make(0, after(down_got, dq))
    dk_part, state_got, grad_hidden, *down_parts = hold(
        (dk_part, state_got, grad_hidden) + tuple(down_parts)
    )
    down_ends = hi_sums(down_parts)
    up_make = lambda slot, got: unit_grads(
        "up_grad", whole_rows(grad_hidden), [whole_rows(n_two)], slot, got
    )
    up_part, up_got = pair_sums(up_make)
    dk_part = after(dk_part, up_part)
    dcarry = combine_states(lay, dstate, state_got, scale, True)
    dk, dv = seq_call(
        "keys_back", bind(last_body, sh), scal, count,
        [by_seq(a, PER) for a in (dk_part, dv_part, fk, vals, dcarry)]
        + turns + maps,
        [rows_new(width, BF16)] * 2,
    )
    dk, up_got, *m_parts = hold((dk, up_got) + tuple(m_parts))
    m_keeps, m_sends = second_sums(m_parts[:2], m_parts[2:])
    m_gots = round_two(m_sends)
    own, away, sums = seq_call(
        "rows_grad", bind(rows_grad_body, sh), scal, count,
        [by_seq(a) for a in (after(dq, *m_sends), dk, dv, grad_hidden)]
        + [own_seq(x_own), away_seq(x_away)]
        + [whole(gains[0]), whole(gains[2])] + in_a + in_u,
        halves_one + [whole(new((8, dim), F32))],
        [
            pltpu.VMEM((sh.pairs, 3 * width, dp), BF16),
            pltpu.VMEM((sh.pairs, dp, ff), BF16),
            pltpu.VMEM((chunk, dim), F32),
        ],
        per=1,
    )
    own, away, sums, dq, down_end0, down_end1, *m_gots = hold(
        (own, away, sums, dq) + down_ends + m_gots
    )
    down_ends = down_end0, down_end1
    mixed = tokens.astype(F32) + join_micro(m_keeps).astype(F32)
    mixed = (mixed + join_micro(m_gots).astype(F32)).astype(BF16)
    e_got = lay.core_swap(away)
    sums = sums[:4]
    sums_got = lay.lo_swap(sums, 1)
    head_make = lambda slot, got: head_grads((dq, dk, dv, ctx), slot, got)
    head_part, head_got = pair_sums(head_make)
    own, e_got, sums_got = hold((own, e_got, sums_got), head_part)
    sums = sums + sums_got
    sums_got = lay.core_swap(sums)
    e_keeps, e_sends = first_sums(own, e_got)
    e_gots = round_one(e_sends)
    up_parts = up_make(0, after(up_got, *e_sends))
    head_got, sums_got, *up_parts = hold((head_got, sums_got) + tuple(up_parts))
    up_ends = hi_sums(up_parts)
    sums = sums + sums_got
    sums_got = lay.move(sums, lambda p, c, h, l: (1 - p, c, h, l))
    head_parts = head_make(0, after(head_got, sums))
    held = hold(e_keeps + e_gots + (sums_got,) + up_ends + tuple(head_parts))
    e_keeps, e_gots, sums_got = held[:2], held[2:4], held[4]
    up_ends, head_parts = held[5:7], held[7:]
    head_ends = hi_sums(head_parts)
    sums = sums + sums_got
    e_keeps, e_sends = second_sums(e_keeps, e_gots)
    e_gots = round_two(e_sends)
    sums_got = lay.lo_swap(after(sums, *e_sends), 2)
    units_ends = trade(hold(up_ends, *e_sends)) + trade(hold(down_ends, *e_sends))
    grads_units = call(
        "end_units", bind(end_units_body, sh), core_only, (), units_ends,
        [whole(new(w.shape, F32)) for w in (up_weight, down_weight)],
    )
    e_got0, e_got1, sums_got = hold(e_gots + (sums_got,), grads_units[0])
    e_gots = e_got0, e_got1
    sums = sums + sums_got
    mine, got = join_micro(e_keeps), join_micro(e_gots)
    (grad_tokens,) = call(
        "tokens_grad", tokens_grad_body, scal, (micro,),
        [by_seq(a) for a in (mine, got, tokens, cotangent)],
        [by_seq(new((micro, rows, dim), F32))],
    )
    sums = sums + lay.move(sums, lambda p, c, h, l: (p, c, 1 - h, l))
    grads = call(
        "end_heads", bind(end_heads_body, sh), core_only, (), trade(head_ends),
        [whole(new(w.shape, F32)) for w in (q_weight, k_weight, value_weight, out_weight)],
    )
    return (
        mixed,
        grad_tokens,
        sums[0],
        sums[1],
        sums[2],
        sums[3],
        grads[0],
        grads[1],
        grads[2],
        grads[3],
        grads_units[0],
        grads_units[1],
    )


def solution(mesh):
    seqs, parts = mesh.shape["seq"], mesh.shape["mp"]

    def body(*args):
        units = args[5].shape[1]
        if parts == 8 and seqs == 4 and units == 2 * HEAD_DIM and args[0].shape[0] % 2 == 0:
            return team_local(*args)
        return plain_local(*args)

    in_specs = (
        P(None, ("seq", "mp"), None),
        P(),
        P(),
        P(),
        P(),
        P("seq", "mp"),
        P("seq", "mp"),
        P("seq", "mp"),
        P("mp", "seq"),
        P("seq", "mp"),
        P("mp", "seq"),
        P(None, "seq", None),
        P(None, ("seq", "mp"), None),
    )
    out_specs = (
        P(None, ("seq", "mp"), None),
        P(None, ("seq", "mp"), None),
        P(),
        P(),
        P(),
        P(),
        P("seq", "mp"),
        P("seq", "mp"),
        P("seq", "mp"),
        P("mp", "seq"),
        P("seq", "mp"),
        P("mp", "seq"),
    )
    return jax.shard_map(body, mesh=mesh, in_specs=in_specs, out_specs=out_specs, check_vma=False)
```

```python
import functools
import math

import jax
import jax.numpy as jnp
import numpy as np
from jax import lax
from jax.experimental import pallas as pl
from jax.experimental.pallas import tpu as pltpu
from jax.sharding import PartitionSpec as P

HEAD_DIM = 64
ROT = 16
FEATS = 64
STATE_ROWS = 80
AXES = ("seq", "mp")
BF16 = jnp.bfloat16
F32 = jnp.float32
VMEM_LIMIT = 56 * 1024 * 1024
PER = 2
NN = (((1,), (0,)), ((), ()))
NT = (((1,), (1,)), ((), ()))
TN = (((0,), (0,)), ((), ()))


def prime_list(wanted):
    found_primes = []
    candidate = 2
    while len(found_primes) < wanted:
        if all((candidate % earlier != 0 for earlier in found_primes)):
            found_primes.append(candidate)
        candidate += 1
    return found_primes


def feature_maps(head_width, feature_count):
    primes_found = prime_list(head_width)
    uniform_rows = [
        [
            min(max((row_idx + 0.5) * math.sqrt(prime_val) % 1.0, 0.001), 0.999)
            for prime_val in primes_found
        ]
        for row_idx in range(feature_count)
    ]
    uniform_pts = jnp.asarray(uniform_rows, jnp.float32)
    points = math.sqrt(2.0) * lax.erf_inv(2.0 * uniform_pts - 1.0)
    cosine_rows = [
        [
            math.sqrt(2.0 / head_width)
            * math.cos(math.pi * (cell_idx + 0.5) * freq_idx / head_width)
            * (math.sqrt(0.5) if freq_idx == 0 else 1.0)
            for cell_idx in range(head_width)
        ]
        for freq_idx in range(head_width)
    ]
    cosine = jnp.asarray(cosine_rows, jnp.float32)
    project = jnp.dot(points, cosine, precision=lax.Precision.HIGHEST)
    project = jnp.transpose(project) * (1.0 / math.sqrt(head_width))
    weighting = 1.0 / (1.0 + jnp.sum(points * points, axis=1) / head_width)
    return (project, weighting)


def rotate_heads(values, offset):
    half_dims = ROT // 2
    inverse = 10000.0 ** (-jnp.arange(half_dims, dtype=jnp.float32) * 2.0 / ROT)
    angles = offset[:, None] * inverse[None, :]
    cosine = jnp.cos(angles)[None, :, :]
    sine_part = jnp.sin(angles)[None, :, :]
    first_half = values[..., :half_dims]
    second = values[..., half_dims:ROT]
    return jnp.concatenate(
        [
            first_half * cosine - second * sine_part,
            second * cosine + first_half * sine_part,
            values[..., ROT:],
        ],
        axis=-1,
    )


def layer_norm(values, gain_vec, bias_vec):
    centered = values - jnp.mean(values, axis=-1, keepdims=True)
    variance = jnp.mean(centered * centered, axis=-1, keepdims=True)
    return centered * lax.rsqrt(variance + 1e-05) * gain_vec + bias_vec


def exact_gelu(values):
    return jax.nn.gelu(values, approximate=False)


def doc_layout(doc_lengths, number_of_tokens):
    doc_ends = jnp.cumsum(doc_lengths).astype(jnp.int32)
    starts = (doc_ends - doc_lengths).astype(jnp.int32)
    places = jnp.arange(number_of_tokens, dtype=jnp.int32)
    segment = jnp.sum((places[:, None] >= doc_ends[None, :]).astype(jnp.int32), axis=1).astype(
        jnp.int32
    )
    member = segment[:, None] == jnp.arange(doc_lengths.shape[0], dtype=jnp.int32)[None, :]
    offset = places - jnp.sum(jnp.where(member, starts[None, :], 0), axis=1).astype(jnp.int32)
    return (segment, offset.astype(jnp.float32))


def contract_rows(left_side, right_side):
    return lax.dot_general(
        left_side, right_side, (((0,), (0,)), ((), ())), preferred_element_type=jnp.float32
    )


def contract_cols(left_side, right_side):
    return lax.dot_general(
        left_side, right_side, (((1,), (1,)), ((), ())), preferred_element_type=jnp.float32
    )


def local_attention(plain_query_rows, key_raw, value_raw, segment, offset, project, weighting):
    maximal_precision_mode = lax.Precision.HIGHEST
    number_of_tokens = plain_query_rows.shape[0]
    head_count = plain_query_rows.shape[1] // HEAD_DIM

    def heads_first(values):
        return jnp.transpose(values.reshape(number_of_tokens, head_count, HEAD_DIM), (1, 0, 2))

    rot_query = rotate_heads(heads_first(plain_query_rows), offset)
    rot_key = rotate_heads(heads_first(key_raw), offset)
    value_heads = heads_first(value_raw)
    feat_query = (
        jnp.exp(jnp.einsum("htd,df->htf", rot_query, project, precision=maximal_precision_mode))
        * weighting
    )
    feat_key = jnp.exp(
        jnp.einsum("htd,df->htf", rot_key, project, precision=maximal_precision_mode)
    )
    rows_per_block = min(512, number_of_tokens)
    block_count = number_of_tokens // rows_per_block

    def split_blocks(values):
        return jnp.transpose(
            values.reshape((head_count, block_count, rows_per_block, values.shape[2])), (1, 0, 2, 3)
        )

    def block_step(carry, pieces):
        kv_state, totals, previous = carry
        block_of_queries, block_of_keys, value_block, block_segment = pieces
        places = jnp.arange(block_segment.shape[0], dtype=jnp.int32)
        attention_scores = jnp.einsum(
            "ugy,uky->ugk", block_of_queries, block_of_keys, precision=maximal_precision_mode
        )
        allowed = (places[:, None] >= places[None, :]) & (
            block_segment[:, None] == block_segment[None, :]
        )
        attention_scores = jnp.where(allowed[None, :, :], attention_scores, 0.0)
        numerator = jnp.einsum(
            "hqk,hkd->hqd", attention_scores, value_block, precision=maximal_precision_mode
        )
        denominator = jnp.sum(attention_scores, axis=2)
        carried_in = (block_segment == previous)[None, :]
        numerator = numerator + jnp.where(
            carried_in[:, :, None],
            jnp.einsum(
                "hqf,hfd->hqd", block_of_queries, kv_state, precision=maximal_precision_mode
            ),
            0.0,
        )
        denominator = denominator + jnp.where(
            carried_in,
            jnp.einsum("hqf,hf->hq", block_of_queries, totals, precision=maximal_precision_mode),
            0.0,
        )
        final_output = block_segment[-1]
        carried_over = final_output == previous
        trailing_mask = (block_segment == final_output).astype(jnp.float32)
        new_state = jnp.where(carried_over, kv_state, 0.0) + jnp.einsum(
            "hrf,hrd,r->hfd",
            block_of_keys,
            value_block,
            trailing_mask,
            precision=maximal_precision_mode,
        )
        new_totals = jnp.where(carried_over, totals, 0.0) + jnp.einsum(
            "hrf,r->hf", block_of_keys, trailing_mask, precision=maximal_precision_mode
        )
        return ((new_state, new_totals, final_output), numerator / denominator[:, :, None])

    start_carry = (
        jnp.zeros((head_count, FEATS, HEAD_DIM), jnp.float32),
        jnp.zeros((head_count, FEATS), jnp.float32),
        jnp.array(-1, jnp.int32),
    )
    _, outputs = lax.scan(
        jax.checkpoint(block_step),
        start_carry,
        (
            split_blocks(feat_query),
            split_blocks(feat_key),
            split_blocks(value_heads),
            segment.reshape(block_count, rows_per_block),
        ),
    )
    joined = jnp.transpose(outputs, (1, 0, 2, 3)).reshape(head_count, number_of_tokens, HEAD_DIM)
    return jnp.transpose(joined, (1, 0, 2)).reshape(number_of_tokens, head_count * HEAD_DIM)


def plain_local(
    tokens,
    ln1_gain,
    ln1_bias,
    ln2_gain,
    ln2_bias,
    q_weight,
    k_weight,
    value_weight,
    out_weight,
    up_weight,
    down_weight,
    lengths,
    cotangent,
):
    micro_count = tokens.shape[0]
    local_rows = tokens.shape[1]
    group_rows = local_rows * lax.axis_size("mp")
    seq_count = lax.axis_size("seq")
    project, weighting = feature_maps(HEAD_DIM, FEATS)
    grad_sums = [
        jnp.zeros((q_weight.shape[0] * seq_count, q_weight.shape[1]), jnp.float32),
        jnp.zeros((k_weight.shape[0] * seq_count, k_weight.shape[1]), jnp.float32),
        jnp.zeros((value_weight.shape[0] * seq_count, value_weight.shape[1]), jnp.float32),
        jnp.zeros((out_weight.shape[0], out_weight.shape[1] * seq_count), jnp.float32),
        jnp.zeros((up_weight.shape[0] * seq_count, up_weight.shape[1]), jnp.float32),
        jnp.zeros((down_weight.shape[0], down_weight.shape[1] * seq_count), jnp.float32),
    ]
    norm_sums = [
        jnp.zeros_like(ln1_gain),
        jnp.zeros_like(ln1_bias),
        jnp.zeros_like(ln2_gain),
        jnp.zeros_like(ln2_bias),
    ]
    mixed_parts = []
    grad_parts = []
    for micro_step in range(micro_count):
        full_weights = (
            lax.all_gather(q_weight, "seq", axis=0, tiled=True),
            lax.all_gather(k_weight, "seq", axis=0, tiled=True),
            lax.all_gather(value_weight, "seq", axis=0, tiled=True),
            lax.all_gather(out_weight, "seq", axis=1, tiled=True),
            lax.all_gather(up_weight, "seq", axis=0, tiled=True),
            lax.all_gather(down_weight, "seq", axis=1, tiled=True),
        )
        w_query, w_key, w_value, w_out, w_up, w_down = full_weights
        rows_in = tokens[micro_step].astype(jnp.float32)
        normed_one, pull_one = jax.vjp(layer_norm, rows_in, ln1_gain, ln1_bias)
        normed_two, pull_two = jax.vjp(layer_norm, rows_in, ln2_gain, ln2_bias)
        group_one, group_two = (
            lax.all_gather(normed_one.astype(jnp.bfloat16), "mp", axis=0, tiled=True),
            lax.all_gather(normed_two.astype(jnp.bfloat16), "mp", axis=0, tiled=True),
        )
        plain_query_rows = jnp.dot(group_one, w_query, preferred_element_type=jnp.float32)
        key_raw = jnp.dot(group_one, w_key, preferred_element_type=jnp.float32)
        value_raw = jnp.dot(group_one, w_value, preferred_element_type=jnp.float32)
        segment, offset = doc_layout(lengths[micro_step, 0], group_rows)
        attend = functools.partial(
            local_attention, segment=segment, offset=offset, project=project, weighting=weighting
        )
        context, pull_attn = jax.vjp(attend, plain_query_rows, key_raw, value_raw)
        context_low = context.astype(jnp.bfloat16)
        hidden = jnp.dot(group_two, w_up, preferred_element_type=jnp.float32)
        activated, pull_gelu = jax.vjp(exact_gelu, hidden)
        activated_low = activated.astype(jnp.bfloat16)
        context_rows = lax.slice_in_dim(context_low, 0, lax.axis_size("mp") * local_rows, axis=0)
        active_rows = lax.slice_in_dim(activated_low, 0, lax.axis_size("mp") * local_rows, axis=0)
        branch_sum = lax.psum_scatter(
            jnp.dot(context_rows, w_out, preferred_element_type=jnp.float32)
            + jnp.dot(active_rows, w_down, preferred_element_type=jnp.float32),
            "mp",
            scatter_dimension=0,
            tiled=True,
        )
        mixed_parts.append((rows_in + branch_sum).astype(jnp.bfloat16))
        grad_group = lax.all_gather(cotangent[micro_step], "mp", axis=0, tiled=True)
        grad_context = contract_cols(grad_group, w_out)
        grad_activated = contract_cols(grad_group, w_down)
        grad_hidden = pull_gelu(grad_activated)[0].astype(jnp.bfloat16)
        grad_query_f, grad_key_f, grad_value_f = pull_attn(grad_context)
        grad_query = grad_query_f.astype(jnp.bfloat16)
        grad_key = grad_key_f.astype(jnp.bfloat16)
        grad_value = grad_value_f.astype(jnp.bfloat16)
        micro_grads = (
            contract_rows(group_one, grad_query),
            contract_rows(group_one, grad_key),
            contract_rows(group_one, grad_value),
            contract_rows(context_low, grad_group),
            contract_rows(group_two, grad_hidden),
            contract_rows(activated_low, grad_group),
        )
        grad_sums = [total + term for total, term in zip(grad_sums, micro_grads)]
        part_one = (
            contract_cols(grad_query, w_query)
            + contract_cols(grad_key, w_key)
            + contract_cols(grad_value, w_value)
        )
        part_two = contract_cols(grad_hidden, w_up)
        sum_one, sum_two = (
            lax.psum_scatter(
                part_one.astype(jnp.bfloat16), "mp", scatter_dimension=0, tiled=True
            ).astype(jnp.float32),
            lax.psum_scatter(
                part_two.astype(jnp.bfloat16), "mp", scatter_dimension=0, tiled=True
            ).astype(jnp.float32),
        )
        grad_in_one, grad_gain_one, grad_bias_one = pull_one(sum_one)
        grad_in_two, grad_gain_two, grad_bias_two = pull_two(sum_two)
        grad_parts.append(cotangent[micro_step].astype(jnp.float32) + grad_in_one + grad_in_two)
        norm_sums = [
            norm_sums[0] + grad_gain_one,
            norm_sums[1] + grad_bias_one,
            norm_sums[2] + grad_gain_two,
            norm_sums[3] + grad_bias_two,
        ]
    weight_grads = (
        lax.psum_scatter(
            grad_sums[0].astype(jnp.bfloat16), "seq", scatter_dimension=0, tiled=True
        ).astype(jnp.float32),
        lax.psum_scatter(
            grad_sums[1].astype(jnp.bfloat16), "seq", scatter_dimension=0, tiled=True
        ).astype(jnp.float32),
        lax.psum_scatter(
            grad_sums[2].astype(jnp.bfloat16), "seq", scatter_dimension=0, tiled=True
        ).astype(jnp.float32),
        lax.psum_scatter(
            grad_sums[3].astype(jnp.bfloat16), "seq", scatter_dimension=1, tiled=True
        ).astype(jnp.float32),
        lax.psum_scatter(
            grad_sums[4].astype(jnp.bfloat16), "seq", scatter_dimension=0, tiled=True
        ).astype(jnp.float32),
        lax.psum_scatter(
            grad_sums[5].astype(jnp.bfloat16), "seq", scatter_dimension=1, tiled=True
        ).astype(jnp.float32),
    )
    norm_grads = lax.psum((norm_sums[0], norm_sums[1], norm_sums[2], norm_sums[3]), ("seq", "mp"))
    return (
        jnp.stack(mixed_parts),
        jnp.stack(grad_parts),
        norm_grads[0],
        norm_grads[1],
        norm_grads[2],
        norm_grads[3],
        weight_grads[0],
        weight_grads[1],
        weight_grads[2],
        weight_grads[3],
        weight_grads[4],
        weight_grads[5],
    )


def mm(left, right, dims=NN):
    return lax.dot_general(left, right, dims, preferred_element_type=F32)


def split(values):
    high = values.astype(BF16)
    return high, (values - high.astype(F32)).astype(BF16)


def mm3(values, high, low, dims=NN):
    first, second = split(values)
    return mm(first, high, dims) + (mm(second, high, dims) + mm(first, low, dims))


def lane_head(shape):
    return lax.broadcasted_iota(jnp.int32, shape, len(shape) - 1) // HEAD_DIM


def block_diag(state):
    width = state.shape[1]
    tall = jnp.concatenate([state] * (width // HEAD_DIM), axis=0)
    rows = lax.broadcasted_iota(jnp.int32, tall.shape, 0) // HEAD_DIM
    return jnp.where(rows == lane_head(tall.shape), tall, 0.0)


def diag_blocks(full):
    width = full.shape[1]
    lanes = lane_head((HEAD_DIM, width))
    total = jnp.zeros((HEAD_DIM, width), F32)
    for head in range(width // HEAD_DIM):
        part = full[head * HEAD_DIM : (head + 1) * HEAD_DIM, :]
        total = total + jnp.where(lanes == head, part, 0.0)
    return total


def head_sums(values):
    width = values.shape[1]
    rows = lax.broadcasted_iota(jnp.int32, (width, width), 0) // HEAD_DIM
    ones = jnp.where(rows == lane_head((width, width)), 1.0, 0.0).astype(BF16)
    high, low = split(values)
    return mm(high, ones) + mm(low, ones)


def swap_halves(values):
    width = values.shape[1]
    half = ROT // 2
    lane = lax.broadcasted_iota(jnp.int32, values.shape, 1) % HEAD_DIM
    return jnp.where(
        lane < half, pltpu.roll(values, width - half, 1), pltpu.roll(values, half, 1)
    )


def turn(values, cos, sin):
    reps = values.shape[1] // cos.shape[1]
    cosw = jnp.concatenate([cos] * reps, axis=1)
    sinw = jnp.concatenate([sin] * reps, axis=1)
    return values * cosw + swap_halves(values) * sinw


def normalize(values):
    centered = values - jnp.mean(values, axis=-1, keepdims=True)
    variance = jnp.mean(centered * centered, axis=-1, keepdims=True)
    scale = lax.rsqrt(variance + 1e-05)
    return centered * scale, scale


class Rows:
    def __init__(self, scal, seq, chunk, docs):
        rows = chunk // 2
        self.here = (scal[1] * 2 + (scal[2] // 2 + seq) % 2) * chunk
        side = scal[2] % 2
        low = self.here + side * rows
        high = self.here + (1 - side) * rows - rows

        def places(shape, axis):
            count = lax.broadcasted_iota(jnp.int32, shape, axis)
            return jnp.where(count < rows, count + low, count + high)

        self.place = places((chunk, 1), 0)
        self.across = places((1, chunk), 1)
        self.start = jnp.zeros((chunk, 1), jnp.int32)
        end = jnp.zeros((chunk, 1), jnp.int32)
        base = 4 + seq * 2 * docs
        for doc in range(docs):
            first, last = scal[base + doc], scal[base + docs + doc]
            inside = (self.place >= first) & (self.place < last)
            self.start = jnp.where(inside, first, self.start)
            end = jnp.where(inside, last, end)
        self.came = self.start < self.here
        self.goes = end > self.here + chunk

    def mask(self):
        return (self.across >= self.start) & (self.across <= self.place)


def whole(array):
    zeros = (0,) * array.ndim
    return (array, tuple(array.shape), lambda *_: zeros)


class Seq(tuple):
    pass


def by_seq(array, per=1):
    rest = (0,) * (array.ndim - 1)
    return Seq((array, (per,) + tuple(array.shape[1:]), lambda i, s: (i,) + rest))


def own_seq(array, per=1):
    rest, most = (0,) * (array.ndim - 1), array.shape[0] // per - 1
    return Seq(
        (array, (per,) + tuple(array.shape[1:]), lambda i, s: (jnp.minimum(i, most),) + rest)
    )


def away_seq(array, per=1):
    rest, count = (0,) * (array.ndim - 1), array.shape[0] // per
    return Seq(
        (array, (per,) + tuple(array.shape[1:]), lambda i, s: (jnp.maximum(i - count, 0),) + rest)
    )


def new(shape, kind):
    return jax.ShapeDtypeStruct(shape, kind)


def call(name, body, scal, grid, ins, outs, scratch=(), aliases=None):
    return pl.pallas_call(
        body,
        name=name,
        grid_spec=pltpu.PrefetchScalarGridSpec(
            num_scalar_prefetch=1,
            grid=grid or (1,),
            in_specs=[
                pl.BlockSpec(block, index) if index else pl.BlockSpec(memory_space=pl.ANY)
                for _, block, index in ins
            ],
            out_specs=[pl.BlockSpec(block, index) for _, block, index in outs],
            scratch_shapes=list(scratch),
        ),
        out_shape=[array for array, _, _ in outs],
        input_output_aliases=aliases or {},
        compiler_params=pltpu.CompilerParams(
            dimension_semantics=("arbitrary",) * max(len(grid), 1), vmem_limit_bytes=VMEM_LIMIT
        ),
    )(scal, *[array for array, _, _ in ins])


def seq_call(name, body, scal, count, ins, outs, scratch=(), per=PER):
    marks = [isinstance(part, Seq) for part in list(ins) + list(outs)]

    def step(scal, *refs):
        for k in range(per):
            views = [ref.at[pl.ds(k, 1)] if mark else ref for ref, mark in zip(refs, marks)]
            body(k, pl.program_id(0) * per + k, scal, *views, *refs[len(marks) :])

    return call(name, step, scal, (count // per,), ins, outs, scratch)


class Shape:
    def __init__(self, pairs, chunks, dim, half_units, half_ff, chunk, docs):
        self.pairs, self.chunks, self.dim = pairs, chunks, dim
        self.hu, self.hf, self.chunk, self.docs = half_units, half_ff, chunk, docs
        self.dp = dim // pairs
        self.width, self.ff = chunks * half_units, chunks * half_ff
        self.half = 0

    def cols(self, scal, slot):
        start = ((scal[0] + slot) % self.pairs) * self.dp
        return pl.ds(pl.multiple_of(start, 128), self.dp)


def fill_rows(sh, target, blocks, first, size, at):
    for slot in range(sh.pairs):
        for j in range(sh.chunks):
            part = blocks[slot * sh.chunks + j][first : first + size, :]
            target[slot, at + j * size : at + (j + 1) * size, :] = part


def pack_body(scal, q, k, v, out, up, down, keep_a, send_a, send_u, send_d):
    low = scal[3] == 0
    parts_keep, parts_send = [], []
    for ref in (q, k, v):
        flat = jnp.transpose(ref[...].astype(F32))
        half = flat.shape[0] // 2
        parts_keep.append(jnp.where(low, flat[:half], flat[half:]))
        parts_send.append(jnp.where(low, flat[half:], flat[:half]))
    flat = out[...].astype(F32)
    half = flat.shape[0] // 2
    parts_keep.append(jnp.where(low, flat[:half], flat[half:]))
    parts_send.append(jnp.where(low, flat[half:], flat[:half]))
    keep_a[...] = jnp.concatenate(parts_keep, 0).astype(BF16)
    send_a[...] = jnp.concatenate(parts_send, 0).astype(BF16)
    half = up.shape[1] // 2
    send_u[...] = jnp.where(low, up[:, half:], up[:, :half])
    half = down.shape[0] // 2
    send_d[...] = jnp.where(low, down[half:, :], down[:half, :])


def norm_body(scal, rows, g1, b1, g2, b2, *refs):
    one, two = refs[-2:]
    n, _ = normalize(rows[0].astype(F32))
    one[0] = (n * g1[...] + b1[...]).astype(BF16)
    two[0] = (n * g2[...] + b2[...]).astype(BF16)


def attend_body(sh, k, seq, scal, normed, cos, sin, ph, pw, wts, *refs):
    blocks = refs[: sh.pairs * sh.chunks]
    fq_out, fk_out, v_out, num_out, den_out, st_out, wt = refs[sh.pairs * sh.chunks :]
    width = sh.width

    if k == 0:

        @pl.when(seq == 0)
        def _():
            for kind in range(3):
                fill_rows(sh, wt, blocks, kind * sh.hu, sh.hu, kind * width)

    qkv = mm(normed[0, :, sh.cols(scal, 0)], wt[0], NT)
    for slot in range(1, sh.pairs):
        qkv = qkv + mm(normed[0, :, sh.cols(scal, slot)], wt[slot], NT)

    def feats(values):
        return jnp.exp(mm3(turn(values, cos[0], sin[0]), ph[...], pw[...]))

    fqb = (feats(qkv[:, :width]) * wts[...]).astype(BF16)
    fk = feats(qkv[:, width : 2 * width])
    fkb = fk.astype(BF16)
    v = qkv[:, 2 * width :]
    vb = v.astype(BF16)
    fq_out[0] = fqb
    fk_out[0] = fkb
    v_out[0] = v
    rows = Rows(scal, seq, sh.chunk, sh.docs)
    mask = rows.mask()
    lanes = lane_head(vb.shape)
    num = jnp.zeros(vb.shape, F32)
    den = jnp.zeros(vb.shape, F32)
    for head in range(width // HEAD_DIM):
        mine = lanes == head
        scores = mm(jnp.where(mine, fqb, 0), fkb, NT)
        scores = jnp.where(mask, scores, 0.0).astype(BF16)
        both = mm(scores, jnp.where(mine, vb, 1))
        num = jnp.where(mine, both, num)
        den = jnp.where(mine, pltpu.roll(both, HEAD_DIM, 1), den)
    num_out[0] = num
    den_out[0] = den
    kept = jnp.where(rows.goes, fk, 0.0)
    store_state(sh, scal, st_out, mm(kept.astype(BF16), vb, TN), kept)


def store_state(sh, scal, st_out, sums, totals):
    tail = jnp.broadcast_to(
        jnp.sum(totals, axis=0, keepdims=True), (STATE_ROWS - HEAD_DIM, sh.width)
    )
    state = jnp.concatenate([diag_blocks(sums), tail], axis=0)
    st_out[0] = pltpu.roll(state, scal[1] * sh.hu, 1).astype(BF16)


def load_state(sh, scal, carry):
    state = pltpu.roll(carry[0], (sh.width - scal[1] * sh.hu) % sh.width, 1)
    return state[:HEAD_DIM], state[HEAD_DIM : HEAD_DIM + 1]


def up_body(sh, k, seq, scal, normed, *refs):
    blocks = refs[: sh.pairs * sh.chunks]
    act_out, slope_out, wu = refs[sh.pairs * sh.chunks :]

    if k == 0:

        @pl.when(seq == 0)
        def _():
            for slot in range(sh.pairs):
                for j in range(sh.chunks):
                    wu[slot, :, j * sh.hf : (j + 1) * sh.hf] = blocks[slot * sh.chunks + j][...]

    hidden = mm(normed[0, :, sh.cols(scal, 0)], wu[0])
    for slot in range(1, sh.pairs):
        hidden = hidden + mm(normed[0, :, sh.cols(scal, slot)], wu[slot])
    cdf = 0.5 + 0.5 * lax.erf(hidden * math.sqrt(0.5))
    act_out[0] = (hidden * cdf).astype(BF16)
    bell = jnp.exp(-0.5 * hidden * hidden) * math.sqrt(0.5 / math.pi)
    slope_out[0] = (cdf + hidden * bell).astype(BF16)


def finish_body(sh, k, seq, scal, num, den, fq, carry, ctx_out, rden_out):
    fqb = fq[0]
    sums, totals = load_state(sh, scal, carry)
    more_num = mm(fqb, block_diag(sums).astype(BF16))
    more_den = head_sums(fqb.astype(F32) * totals)
    came = Rows(scal, seq, sh.chunk, sh.docs).came
    inverse = 1.0 / (den[0] + jnp.where(came, more_den, 0.0))
    ctx_out[0] = (num[0] + jnp.where(came, more_num, 0.0)) * inverse
    rden_out[0] = inverse


def store_half(sh, seq, cols, part, own_out, away_out):
    own_out[0, :, cols] = jnp.where(seq < sh.half, part, own_out[0, :, cols])
    away_out[0, :, cols] = part


def branch_body(sh, k, seq, scal, ctx, act, *refs):
    count = sh.pairs * sh.chunks
    blocks_a, blocks_d = refs[:count], refs[count : 2 * count]
    own_out, away_out, wo, wd = refs[2 * count :]

    if k == 0:

        @pl.when(seq == 0)
        def _():
            fill_rows(sh, wo, blocks_a, 3 * sh.hu, sh.hu, 0)
            fill_rows(sh, wd, blocks_d, 0, sh.hf, 0)

    ctxb = ctx[0].astype(BF16)
    for slot in range(sh.pairs):
        part = (mm(act[0], wd[slot]) + mm(ctxb, wo[slot])).astype(BF16)
        store_half(sh, seq, sh.cols(scal, slot), part, own_out, away_out)


def pick(own, away, seq, scal, sh, slot):
    first = seq < sh.half
    cols = sh.cols(scal, slot)
    return jnp.where(first, own[0, :, cols], away[0, :, cols])


def hidden_body(sh, k, seq, scal, own, away, slope, *refs):
    blocks = refs[: sh.pairs * sh.chunks]
    out, wd = refs[sh.pairs * sh.chunks :]

    if k == 0:

        @pl.when(seq == 0)
        def _():
            fill_rows(sh, wd, blocks, 0, sh.hf, 0)

    grad = mm(pick(own, away, seq, scal, sh, 0), wd[0], NT)
    for slot in range(1, sh.pairs):
        grad = grad + mm(pick(own, away, seq, scal, sh, slot), wd[slot], NT)
    out[0] = (grad * slope[0].astype(F32)).astype(BF16)


def back_body(sh, k, seq, scal, own, away, fq, fk, vals, ctx, rden, carry, cos, sin, ph, pw, *refs):
    blocks = refs[: sh.pairs * sh.chunks]
    dq_out, dk_out, dv_out, st_out, wo = refs[sh.pairs * sh.chunks :]
    width = sh.width

    if k == 0:

        @pl.when(seq == 0)
        def _():
            fill_rows(sh, wo, blocks, 3 * sh.hu, sh.hu, 0)

    gctx = mm(pick(own, away, seq, scal, sh, 0), wo[0], NT)
    for slot in range(1, sh.pairs):
        gctx = gctx + mm(pick(own, away, seq, scal, sh, slot), wo[slot], NT)
    inverse = rden[0]
    dnum = gctx * inverse
    dden = -head_sums(gctx * ctx[0]) * inverse
    fqb, fkb, v = fq[0], fk[0], vals[0]
    rows = Rows(scal, seq, sh.chunk, sh.docs)
    mask = rows.mask()
    lanes = lane_head(v.shape)
    lane = lax.broadcasted_iota(jnp.int32, v.shape, 1) % HEAD_DIM
    dn_high, dn_low = split(dnum)
    v_high, v_low = split(v)
    dd_high = dden.astype(BF16).astype(F32)
    roll = lambda values: pltpu.roll(values.astype(F32), HEAD_DIM, 1).astype(BF16)
    den_part = jnp.where(lane == 0, dd_high, jnp.where(lane == 1, dden - dd_high, 0.0))
    den_part = den_part.astype(BF16)
    dn_high_beside, dn_low_beside = roll(dn_high), roll(dn_low)
    v_high_beside, v_low_beside = roll(v_high), roll(v_low)

    dfq = jnp.zeros(v.shape, F32)
    dfk = jnp.zeros(v.shape, F32)
    dv = jnp.zeros(v.shape, F32)
    for head in range(width // HEAD_DIM):
        mine = lanes == head
        left = [jnp.where(mine, dn_high, dn_low_beside), jnp.where(mine, den_part, dn_high_beside)]
        right = [jnp.where(mine, v_high, v_high_beside), jnp.where(mine, 1, v_low_beside)]
        dscores = mm(jnp.concatenate(left, axis=1), jnp.concatenate(right, axis=1), NT)
        dscores = jnp.where(mask, dscores, 0.0).astype(BF16)
        scores = mm(jnp.where(mine, fqb, 0), fkb, NT)
        scores = jnp.where(mask, scores, 0.0).astype(BF16)
        dfq = jnp.where(mine, mm(dscores, fkb), dfq)
        dfk = jnp.where(mine, mm(dscores, fqb, TN), dfk)
        dv = jnp.where(mine, mm(scores, dn_high, TN), dv)
    sums, totals = load_state(sh, scal, carry)
    more = mm(dn_high, block_diag(sums).astype(BF16), NT) + dden * totals
    dfq = dfq + jnp.where(rows.came, more, 0.0)
    fqf = fqb.astype(F32)
    used = jnp.where(rows.came, fqf, 0.0)
    store_state(sh, scal, st_out, mm(used.astype(BF16), dn_high, TN), used * dden)
    turned = mm3(dfq * fqf, ph[...], pw[...], NT)
    dq_out[0] = turn(turned, cos[0], -sin[0]).astype(BF16)
    dk_out[0] = dfk
    dv_out[0] = dv


def last_body(sh, k, seq, scal, dfk, dv, fk, vals, carry, cos, sin, ph, pw, dk_out, dv_out):
    fkb = fk[0]
    sums, totals = load_state(sh, scal, carry)
    state = block_diag(sums).astype(BF16)
    goes = Rows(scal, seq, sh.chunk, sh.docs).goes
    more_k = mm(vals[0].astype(BF16), state, NT) + totals
    total_k = dfk[0] + jnp.where(goes, more_k, 0.0)
    dv_out[0] = (dv[0] + jnp.where(goes, mm(fkb, state), 0.0)).astype(BF16)
    turned = mm3(total_k * fkb.astype(F32), ph[...], pw[...], NT)
    dk_out[0] = turn(turned, cos[0], -sin[0]).astype(BF16)


def unit_grad_body(with_got, scal, left, *refs):
    many, with_got = with_got
    rights, refs = refs[:many], refs[many:]
    at, grad = 0, None
    for right in rights:
        part = mm(left[at : at + right.shape[0], :], right[...], TN)
        at += right.shape[0]
        grad = part if grad is None else grad + part
    if not with_got:
        refs[0][0] = grad.astype(BF16)
        return
    value = (grad + refs[0][0].astype(F32)).astype(BF16)
    j = pl.program_id(0)
    for step, out in enumerate(refs[1:]):

        @pl.when(j == step)
        def _():
            out[...] = value


def head_grad_body(sh, with_got, scal, dq, dk, dv, ctx, normed, own, away, *refs):
    scratch = refs[-1]
    for kind, ref in enumerate((dq, dk, dv)):
        scratch[kind] = mm(ref[...], normed[...], TN)
    half = own.shape[0]
    scratch[3] = mm(ctx[:half, :].astype(BF16), own[...], TN) + mm(
        ctx[half:, :].astype(BF16), away[...], TN
    )
    for j in range(sh.chunks):
        rows = slice(j * sh.hu, (j + 1) * sh.hu)
        value = jnp.concatenate([scratch[kind, rows, :] for kind in range(4)], axis=0)
        if with_got:
            refs[1 + j][...] = (value + refs[0][j].astype(F32)).astype(BF16)
        else:
            refs[0][j] = value.astype(BF16)


def rows_grad_body(sh, k, seq, scal, dq, dk, dv, gh, own, away, g1, g2, *refs):
    count = sh.pairs * sh.chunks
    blocks_a, blocks_u = refs[:count], refs[count : 2 * count]
    own_out, away_out, sums, wt, wu, n_ref = refs[2 * count :]

    if k == 0:

        @pl.when(seq == 0)
        def _():
            for kind in range(3):
                fill_rows(sh, wt, blocks_a, kind * sh.hu, sh.hu, kind * sh.width)
            for slot in range(sh.pairs):
                for j in range(sh.chunks):
                    wu[slot, :, j * sh.hf : (j + 1) * sh.hf] = blocks_u[slot * sh.chunks + j][...]
            sums[...] = jnp.zeros(sums.shape, F32)

    x = jnp.where(seq < sh.half, own[0], away[0]).astype(F32)
    n_ref[...] = normalize(x)[0]
    qkv = jnp.concatenate([dq[0], dk[0], dv[0]], axis=1)
    for slot in range(sh.pairs):
        cols = sh.cols(scal, slot)
        one = mm(qkv, wt[slot])
        two = mm(gh[0], wu[slot], NT)
        n = n_ref[:, cols]
        for at, value in enumerate((one * n, one, two * n, two)):
            line = slice(at, at + 1)
            sums[line, cols] = sums[line, cols] + jnp.sum(value, axis=0, keepdims=True)
        e = (one * g1[:, cols] + two * g2[:, cols]).astype(BF16)
        store_half(sh, seq, cols, e, own_out, away_out)


def tokens_grad_body(scal, mine, got, tokens, cot, out):
    e = mine[0].astype(F32) + got[0].astype(F32)
    n, scale = normalize(tokens[0].astype(F32))
    shift = jnp.mean(e, axis=-1, keepdims=True) + n * jnp.mean(e * n, axis=-1, keepdims=True)
    out[0] = cot[0].astype(F32) + scale * (e - shift)


def join_units(scal, keep, got):
    low = scal[3] == 0
    mine, other = keep[...].astype(F32), got[...].astype(F32)
    return jnp.where(low, mine, other), jnp.where(low, other, mine)


def end_units_body(sh, scal, keep_u, got_u, keep_d, got_d, up, down):
    first, second = join_units(scal, keep_u, got_u)
    up[:, : sh.hf] = jnp.transpose(first)
    up[:, sh.hf :] = jnp.transpose(second)
    first, second = join_units(scal, keep_d, got_d)
    down[: sh.hf, :] = first
    down[sh.hf :, :] = second


def end_heads_body(sh, scal, keep, got, *outs):
    first, second = join_units(scal, keep, got)
    for kind in range(4):
        rows = slice(kind * sh.hu, (kind + 1) * sh.hu)
        both = jnp.concatenate([first[rows], second[rows]], axis=0)
        outs[kind][...] = both if kind == 3 else jnp.transpose(both)


class Layout:
    def __init__(self):
        self.seqs, self.parts = lax.axis_size("seq"), lax.axis_size("mp")
        self.pairs, self.chunks = self.seqs // 2, self.parts // 4
        seq, part = lax.axis_index("seq"), lax.axis_index("mp")
        self.pair, self.core = seq // 2, seq % 2
        self.hi, self.lo = part // 4, part % 4

    def move(self, values, rule):
        links = []
        for seq in range(self.seqs):
            for part in range(self.parts):
                there = rule(seq // 2, seq % 2, part // 4, part % 4)
                if there is not None:
                    pair, core, hi, lo = there
                    goal = (pair * 2 + core) * self.parts + hi * 4 + lo
                    links.append((seq * self.parts + part, goal))
        return lax.ppermute(values, AXES, links)

    def core_swap(self, values):
        return self.move(values, lambda p, c, h, l: (p, 1 - c, h, l))

    def lo_swap(self, values, bit):
        return self.move(values, lambda p, c, h, l: (p, c, h, l ^ bit))

    def pair_step(self, values, way):
        return self.move(values, lambda p, c, h, l: ((p + way) % self.pairs, c, h, l))

    def hi_step(self, values, way):
        return self.move(values, lambda p, c, h, l: (p, c, (h + way) % self.chunks, l))


def after(value, *others):
    return lax.optimization_barrier((value,) + others)[0]


def hold(values, *others):
    return lax.optimization_barrier(tuple(values) + others)[: len(values)]


def in_order(lay, one, two):
    flip = lay.lo >= 2
    return jnp.where(flip, two, one), jnp.where(flip, one, two)


def send_states(lay, local, scale, backward):
    states = local.astype(F32).reshape((-1, 2) + local.shape[1:])
    first, second = in_order(lay, states[:, 0], states[:, 1])
    if backward:
        out, goal = first + second * scale(0, 1), 0
    else:
        out, goal = second + first * scale(1, 2), 1
    return lay.move(
        out.astype(BF16), lambda p, c, h, l: (p, c, goal, l) if h != goal else None
    )


def combine_states(lay, local, got, scale, backward):
    states = local.astype(F32).reshape((-1, 2) + local.shape[1:])
    first, second = in_order(lay, states[:, 0], states[:, 1])
    got = got.astype(F32)
    if backward:
        first, second = second + got * scale(1, 2), got
    else:
        first, second = got, first + got * scale(0, 1)
    return jnp.stack(in_order(lay, first, second), 1).reshape(local.shape)


def erf_inverse(target):
    low, high = -6.0, 6.0
    for _ in range(60):
        middle = 0.5 * (low + high)
        low, high = (middle, high) if math.erf(middle) < target else (low, middle)
    guess = 0.5 * (low + high)
    for _ in range(3):
        gap = math.erf(guess) - target
        guess -= gap * math.exp(guess * guess) * math.sqrt(math.pi) / 2.0
    return guess


@functools.lru_cache(None)
def tables(heads):
    primes = prime_list(HEAD_DIM)
    points = np.zeros((FEATS, HEAD_DIM))
    for row in range(FEATS):
        for col in range(HEAD_DIM):
            share = min(max((row + 0.5) * math.sqrt(primes[col]) % 1.0, 0.001), 0.999)
            points[row, col] = math.sqrt(2.0) * erf_inverse(2.0 * float(np.float32(share)) - 1.0)
    cells = np.arange(HEAD_DIM)
    cosine = np.cos(np.pi * (cells[None, :] + 0.5) * cells[:, None] / HEAD_DIM)
    cosine = cosine * math.sqrt(2.0 / HEAD_DIM)
    cosine[0] *= math.sqrt(0.5)
    project = np.kron(np.eye(heads), (points @ cosine).T / math.sqrt(HEAD_DIM))
    project = project.astype(np.float32)
    high = project.astype(BF16)
    low = (project - high.astype(np.float32)).astype(BF16)
    weighting = 1.0 / (1.0 + np.sum(points * points, axis=1) / HEAD_DIM)
    return high, low, np.tile(weighting, heads)[None, :].astype(np.float32)


def team_local(
    tokens,
    ln1_gain,
    ln1_bias,
    ln2_gain,
    ln2_bias,
    q_weight,
    k_weight,
    value_weight,
    out_weight,
    up_weight,
    down_weight,
    lengths,
    cotangent,
):
    lay = Layout()
    micro, rows, dim = tokens.shape
    drows, units = q_weight.shape
    docs = lengths.shape[2]
    chunk = 2 * rows
    half_units, half_ff = units // 2, up_weight.shape[1] // 2
    sh = Shape(lay.pairs, lay.chunks, dim, half_units, half_ff, chunk, docs)
    width, ff, dp = sh.width, sh.ff, sh.dp
    half = 2 * micro
    count = 2 * half
    sh.half = half
    total = count * chunk
    whole_rows = lambda array: array.reshape(total, array.shape[-1])
    bind = lambda body, *first: functools.partial(body, *first)
    gains = [vec.reshape(1, dim) for vec in (ln1_gain, ln1_bias, ln2_gain, ln2_bias)]

    own_lengths = lengths[:, 0]
    table = jnp.stack([own_lengths, lay.core_swap(own_lengths)]).reshape(half, docs)
    seq_ends = jnp.cumsum(table, axis=1)
    seq_starts = seq_ends - table
    starts, ends = jnp.repeat(seq_starts, 2, axis=0), jnp.repeat(seq_ends, 2, axis=0)
    scal = jnp.concatenate(
        [
            jnp.stack([lay.pair, lay.hi, lay.lo, lay.core]).astype(jnp.int32),
            jnp.concatenate([starts, ends], axis=1).reshape(-1).astype(jnp.int32),
        ]
    )
    places = jnp.stack([lay.core, lay.core, lay.core, lay.core]).astype(jnp.int32)
    core_only = places

    block_shape = [(4 * half_units, drows), (drows, half_ff), (half_ff, drows)]
    keep_a, send_a, send_u, send_d = call(
        "pack", pack_body, core_only, (),
        [whole(w) for w in (q_weight, k_weight, value_weight, out_weight, up_weight, down_weight)],
        [whole(new(shape, BF16)) for shape in [block_shape[0]] + block_shape],
    )
    first_core = lay.core == 0

    def join(keep, got, axis):
        return jnp.where(
            first_core, jnp.concatenate([keep, got], axis), jnp.concatenate([got, keep], axis)
        )

    got_a, got_u, got_d = lax.optimization_barrier(
        tuple(lay.core_swap(send) for send in (send_a, send_u, send_d))
    )
    block_a = join(keep_a, got_a, 1)
    split_at = micro // 2

    def first_swaps(values):
        return lay.lo_swap(values, 1), lay.lo_swap(values, 2)

    def second_swaps(by_y, by_z):
        return lay.lo_swap(by_z[:split_at], 1), lay.lo_swap(by_y[split_at:], 2)

    def team_rows(values, by_y, by_z, both):
        both = jnp.concatenate(both, 0)
        own = jnp.stack([jnp.stack([values, by_y], 1), jnp.stack([by_z, both], 1)], 1)
        own = own.reshape(half, chunk, dim)
        return own, lay.core_swap(own)

    def cross(values):
        return lay.pair_step(values, -1)

    def beside(values):
        return lay.hi_step(values, -1)

    block_a, own_tokens = hold((block_a, tokens), got_a)
    by_y, by_z = first_swaps(own_tokens)
    beside_a, cross_a = beside(block_a), cross(block_a)
    late_up, late_down = hold((up_weight, down_weight), block_a)
    keep_u = jnp.where(first_core, late_up[:, :half_ff], late_up[:, half_ff:])
    keep_d = jnp.where(first_core, late_down[:half_ff], late_down[half_ff:])
    block_u, block_d = join(keep_u, got_u, 0), join(keep_d, got_d, 1)
    cross_u = cross(block_u)

    here = (2 * lay.hi + (lay.lo // 2 + jnp.arange(count, dtype=jnp.int32)) % 2) * chunk
    step = jnp.arange(rows, dtype=jnp.int32)
    side = (lay.lo % 2) * rows
    places = here[:, None] + jnp.concatenate([side + step, rows - side + step])[None, :]
    start = jnp.zeros((count, chunk), jnp.int32)
    for doc in range(docs):
        first = starts[:, doc : doc + 1]
        start = jnp.where(places >= first, first, start)
    offset = after((places - start).astype(F32), block_a)
    lane = np.arange(128) % HEAD_DIM
    turned = lane < ROT
    inverse = np.where(turned, 10000.0 ** (-(lane % (ROT // 2)) * 2.0 / ROT), 0.0)
    side = np.where(turned, np.where(lane < ROT // 2, -1.0, 1.0), 0.0)
    angles = offset[:, :, None] * jnp.asarray(inverse, F32)[None, None, :]
    cos = jnp.cos(angles)
    sin = jnp.sin(angles) * jnp.asarray(side, F32)[None, None, :]
    cos, sin = lax.optimization_barrier((cos, sin))

    by_y, by_z, beside_a, cross_a, cross_u, block_d, cos, sin = hold(
        (by_y, by_z, beside_a, cross_a, cross_u, block_d, cos, sin)
    )
    both = second_swaps(by_y, by_z)
    across_a, cross_d = cross(beside_a), cross(block_d)
    both = hold(both, across_a)
    x_own, x_away = team_rows(tokens, by_y, by_z, both)

    high, low, weighting = tables(width // HEAD_DIM)
    maps = [whole(jnp.asarray(high)), whole(jnp.asarray(low))]
    turns = [by_seq(cos, PER), by_seq(sin, PER)]
    turns_one = [by_seq(cos), by_seq(sin)]

    def straddles(first, second):
        lower, higher = jnp.minimum(first, second), jnp.maximum(first, second)
        return jnp.any((seq_starts < lower) & (seq_ends > higher), axis=1).astype(F32)

    edges = [(2 * lay.hi + step) * chunk for step in range(3)]
    scale = lambda a, b: straddles(edges[a], edges[b])[:, None, None]

    rows_new = lambda size, kind: by_seq(new((count, chunk, size), kind), PER)
    rows_one = lambda size, kind: by_seq(new((count, chunk, size), kind))
    state_one = by_seq(new((count, STATE_ROWS, width), BF16))
    norm_ins = [whole(vec) for vec in gains]
    norm_outs = [by_seq(new((count, chunk, dim), BF16))] * 2
    n_one, n_two = call(
        "norms_own", norm_body, core_only, (half,), [by_seq(x_own)] + norm_ins, norm_outs
    )
    n_one, n_two, x_away, block_u, cross_u, block_d, cross_d, cot = hold(
        (n_one, n_two, x_away, block_u, cross_u, block_d, cross_d, cotangent)
    )
    beside_u, across_u = beside(block_u), beside(cross_u)
    cot_y, cot_z = first_swaps(cot)
    beside_d = beside(block_d)
    rest = lambda i, s: (i + half, 0, 0)
    n_one, n_two = call(
        "norms_away", norm_body, core_only, (half,),
        [by_seq(x_away)] + norm_ins + [(n_one, None, None), (n_two, None, None)],
        [(array, block, rest) for array, block, _ in norm_outs], aliases={6: 0, 7: 1},
    )
    in_a = [whole(block) for block in (block_a, beside_a, cross_a, across_a)]
    fq, fk, vals, num, den, state = seq_call(
        "attend", bind(attend_body, sh), scal, count,
        [by_seq(n_one)] + turns_one + maps + [whole(jnp.asarray(weighting))] + in_a,
        [rows_one(width, BF16)] * 2 + [rows_one(width, F32)] * 3 + [state_one],
        [pltpu.VMEM((sh.pairs, 3 * width, dp), BF16)],
        per=1,
    )
    n_two, fq, state, beside_u, across_u, cot_y, cot_z = hold(
        (n_two, fq, state, beside_u, across_u, cot_y, cot_z)
    )
    in_u = [whole(block) for block in (block_u, beside_u, cross_u, across_u)]
    state_got = send_states(lay, state, scale, False)
    cot_both = second_swaps(cot_y, cot_z)
    act, slope = seq_call(
        "up", bind(up_body, sh), scal, count, [by_seq(n_two, PER)] + in_u,
        [rows_new(ff, BF16)] * 2, [pltpu.VMEM((sh.pairs, dp, ff), BF16)],
    )
    act, num, state_got, beside_d, cot_both0, cot_both1 = hold(
        (act, num, state_got, beside_d) + cot_both
    )
    across_d = cross(beside_d)
    g_own, g_away = team_rows(cotangent, cot_y, cot_z, (cot_both0, cot_both1))
    carry = combine_states(lay, state, state_got, scale, False)
    ctx, rden = seq_call(
        "finish", bind(finish_body, sh), scal, count,
        [by_seq(a, PER) for a in (after(num, g_own), den, fq, carry)], [rows_new(width, F32)] * 2,
    )
    g_own, g_away, ctx, across_d = hold((g_own, g_away, ctx, across_d))
    in_d = [whole(block) for block in (block_d, beside_d, cross_d, across_d)]

    def cols_of(array, slot):
        pairs = sh.pairs
        index = lambda *ids: (0, (ids[-1][0] + slot) % pairs)
        return (array, (array.shape[0], dp), index)

    def lanes_of(array, size):
        return (array, (array.shape[0], size), lambda j, s: (0, j))

    def block_of(array):
        rest = tuple(array.shape[1:])
        return (array, (1,) + rest, lambda j, s: (j,) + (0,) * len(rest))

    g_rows = [g.reshape(total // 2, dim) for g in (g_own, g_away)]
    unit_shape, head_shape = (half_ff, dp), (4 * half_units, dp)

    def unit_grads(name, left, rights, slot, got=None):
        final = slot == 0
        outs = [whole(new(unit_shape, BF16))] * sh.chunks
        if not final:
            outs = [block_of(new((sh.chunks,) + unit_shape, BF16))]
        return call(
            name + str(slot), bind(unit_grad_body, (len(rights), got is not None)), scal,
            (sh.chunks,),
            [lanes_of(left, half_ff)] + [cols_of(right, slot) for right in rights]
            + ([] if got is None else [block_of(got)]),
            outs,
        )

    def head_grads(parts, slot, got=None):
        final = slot == 0
        outs = [whole(new(head_shape, BF16))] * sh.chunks
        if not final:
            outs = [whole(new((sh.chunks,) + head_shape, BF16))]
        return call(
            "head_grad" + str(slot), bind(head_grad_body, sh, got is not None), scal, (),
            [whole(whole_rows(a)) for a in parts] + [cols_of(whole_rows(n_one), slot)]
            + [cols_of(g, slot) for g in g_rows] + ([] if got is None else [whole(got)]),
            outs, [pltpu.VMEM((4, width, dp), F32)],
        )

    def pair_sums(make):
        got = None
        for slot in range(sh.pairs - 1, 0, -1):
            part = make(slot, got)[0]
            got = lay.pair_step(part, 1)
        return part, got

    def hi_sums(parts):
        term = parts[sh.chunks - 1]
        for j in range(sh.chunks - 2, -1, -1):
            term = lay.hi_step(term, 1)
            if j:
                term = (term.astype(F32) + parts[j].astype(F32)).astype(BF16)
        return term, parts[0]

    def trade(ends, *others):
        sums = (ends[0].astype(F32) + ends[1].astype(F32)).astype(BF16)
        first, second = sums[:, :drows], sums[:, drows:]
        keep = jnp.where(first_core, first, second)
        send = jnp.where(first_core, second, first)
        return [whole(keep), whole(lay.core_swap(send))]

    down_make = lambda slot, got: unit_grads("down_grad", whole_rows(act), g_rows, slot, got)
    down_part, down_got = pair_sums(down_make)

    ctx = after(ctx, down_part)
    halves_one = [
        own_seq(new((half, chunk, dim), BF16)), away_seq(new((half, chunk, dim), BF16))
    ]
    halves_new = [
        own_seq(new((half, chunk, dim), BF16), PER),
        away_seq(new((half, chunk, dim), BF16), PER),
    ]
    branch_own, branch_away = seq_call(
        "branch", bind(branch_body, sh), scal, count,
        [by_seq(ctx, PER), by_seq(act, PER)] + in_a + in_d, halves_new,
        [pltpu.VMEM((sh.pairs, width, dp), BF16), pltpu.VMEM((sh.pairs, ff, dp), BF16)],
    )

    def first_sums(own, away_got):
        both = (own.astype(F32) + away_got.astype(F32)).reshape(micro, 2, 2, rows, dim)
        by_z, by_y = both[:split_at], both[split_at:]
        sends = by_z[:, 1].astype(BF16), by_y[:, :, 1].astype(BF16)
        return (by_z[:, 0].astype(BF16), by_y[:, :, 0].astype(BF16)), sends

    def second_sums(keeps, gots):
        by_z = keeps[0].astype(F32) + gots[0].astype(F32)
        by_y = keeps[1].astype(F32) + gots[1].astype(F32)
        sends = by_z[:, 1].astype(BF16), by_y[:, 1].astype(BF16)
        return (by_z[:, 0].astype(BF16), by_y[:, 0].astype(BF16)), sends

    def round_one(sends):
        return lay.lo_swap(sends[0], 2), lay.lo_swap(sends[1], 1)

    def round_two(sends):
        return lay.lo_swap(sends[0], 1), lay.lo_swap(sends[1], 2)

    join_micro = lambda parts: jnp.concatenate(parts, 0)
    down_got, branch_own, branch_away, ctx = hold((down_got, branch_own, branch_away, ctx))
    m_got = lay.core_swap(branch_away)

    (grad_hidden,) = seq_call(
        "hidden_grad", bind(hidden_body, sh), scal, count,
        [own_seq(g_own, PER), away_seq(g_away, PER), by_seq(after(slope, branch_own), PER)] + in_d,
        [rows_new(ff, BF16)], [pltpu.VMEM((sh.pairs, ff, dp), BF16)],
    )
    branch_own, m_got, grad_hidden, ctx = hold((branch_own, m_got, grad_hidden, ctx))
    m_keeps, m_sends = first_sums(branch_own, m_got)
    m_gots = round_one(m_sends)
    ctx_back = after(ctx, *m_sends)
    dq, dk_part, dv_part, dstate = seq_call(
        "attend_back", bind(back_body, sh), scal, count,
        [own_seq(g_own, PER), away_seq(g_away, PER)]
        + [by_seq(a, PER) for a in (fq, fk, vals, ctx_back, rden, carry)]
        + turns + maps + in_a,
        [rows_new(width, BF16), rows_new(width, F32), rows_new(width, F32), by_seq(new((count, STATE_ROWS, width), BF16), PER)],
        [pltpu.VMEM((sh.pairs, width, dp), BF16)],
    )
    dq, dstate, dk_part, grad_hidden, *m_parts = hold(
        (dq, dstate, dk_part, grad_hidden) + m_keeps + m_gots
    )
    state_got = send_states(lay, dstate, scale, True)
    down_parts = down_make(0, after(down_got, dq))
    dk_part, state_got, grad_hidden, *down_parts = hold(
        (dk_part, state_got, grad_hidden) + tuple(down_parts)
    )
    down_ends = hi_sums(down_parts)
    up_make = lambda slot, got: unit_grads(
        "up_grad", whole_rows(grad_hidden), [whole_rows(n_two)], slot, got
    )
    up_part, up_got = pair_sums(up_make)
    dk_part = after(dk_part, up_part)
    dcarry = combine_states(lay, dstate, state_got, scale, True)
    dk, dv = seq_call(
        "keys_back", bind(last_body, sh), scal, count,
        [by_seq(a, PER) for a in (dk_part, dv_part, fk, vals, dcarry)]
        + turns + maps,
        [rows_new(width, BF16)] * 2,
    )
    dk, up_got, *m_parts = hold((dk, up_got) + tuple(m_parts))
    m_keeps, m_sends = second_sums(m_parts[:2], m_parts[2:])
    m_gots = round_two(m_sends)
    own, away, sums = seq_call(
        "rows_grad", bind(rows_grad_body, sh), scal, count,
        [by_seq(a) for a in (after(dq, *m_sends), dk, dv, grad_hidden)]
        + [own_seq(x_own), away_seq(x_away)]
        + [whole(gains[0]), whole(gains[2])] + in_a + in_u,
        halves_one + [whole(new((8, dim), F32))],
        [
            pltpu.VMEM((sh.pairs, 3 * width, dp), BF16),
            pltpu.VMEM((sh.pairs, dp, ff), BF16),
            pltpu.VMEM((chunk, dim), F32),
        ],
        per=1,
    )
    own, away, sums, dq, down_end0, down_end1, *m_gots = hold(
        (own, away, sums, dq) + down_ends + m_gots
    )
    down_ends = down_end0, down_end1
    mixed = tokens.astype(F32) + join_micro(m_keeps).astype(F32)
    mixed = (mixed + join_micro(m_gots).astype(F32)).astype(BF16)
    e_got = lay.core_swap(away)
    sums = sums[:4]
    sums_got = lay.lo_swap(sums, 1)
    head_make = lambda slot, got: head_grads((dq, dk, dv, ctx), slot, got)
    head_part, head_got = pair_sums(head_make)
    own, e_got, sums_got = hold((own, e_got, sums_got), head_part)
    sums = sums + sums_got
    sums_got = lay.core_swap(sums)
    e_keeps, e_sends = first_sums(own, e_got)
    e_gots = round_one(e_sends)
    up_parts = up_make(0, after(up_got, *e_sends))
    head_got, sums_got, *up_parts = hold((head_got, sums_got) + tuple(up_parts))
    up_ends = hi_sums(up_parts)
    sums = sums + sums_got
    sums_got = lay.move(sums, lambda p, c, h, l: (1 - p, c, h, l))
    head_parts = head_make(0, after(head_got, sums))
    held = hold(e_keeps + e_gots + (sums_got,) + up_ends + tuple(head_parts))
    e_keeps, e_gots, sums_got = held[:2], held[2:4], held[4]
    up_ends, head_parts = held[5:7], held[7:]
    head_ends = hi_sums(head_parts)
    sums = sums + sums_got
    e_keeps, e_sends = second_sums(e_keeps, e_gots)
    e_gots = round_two(e_sends)
    sums_got = lay.lo_swap(after(sums, *e_sends), 2)
    units_ends = trade(hold(up_ends, *e_sends)) + trade(hold(down_ends, *e_sends))
    grads_units = call(
        "end_units", bind(end_units_body, sh), core_only, (), units_ends,
        [whole(new(w.shape, F32)) for w in (up_weight, down_weight)],
    )
    e_got0, e_got1, sums_got = hold(e_gots + (sums_got,), grads_units[0])
    e_gots = e_got0, e_got1
    sums = sums + sums_got
    mine, got = join_micro(e_keeps), join_micro(e_gots)
    (grad_tokens,) = call(
        "tokens_grad", tokens_grad_body, scal, (micro,),
        [by_seq(a) for a in (mine, got, tokens, cotangent)],
        [by_seq(new((micro, rows, dim), F32))],
    )
    sums = sums + lay.move(sums, lambda p, c, h, l: (p, c, 1 - h, l))
    grads = call(
        "end_heads", bind(end_heads_body, sh), core_only, (), trade(head_ends),
        [whole(new(w.shape, F32)) for w in (q_weight, k_weight, value_weight, out_weight)],
    )
    return (
        mixed,
        grad_tokens,
        sums[0],
        sums[1],
        sums[2],
        sums[3],
        grads[0],
        grads[1],
        grads[2],
        grads[3],
        grads_units[0],
        grads_units[1],
    )


def solution(mesh):
    seqs, parts = mesh.shape["seq"], mesh.shape["mp"]

    def body(*args):
        units = args[5].shape[1]
        if parts == 8 and seqs == 4 and units == 2 * HEAD_DIM and args[0].shape[0] % 2 == 0:
            return team_local(*args)
        return plain_local(*args)

    in_specs = (
        P(None, ("seq", "mp"), None),
        P(),
        P(),
        P(),
        P(),
        P("seq", "mp"),
        P("seq", "mp"),
        P("seq", "mp"),
        P("mp", "seq"),
        P("seq", "mp"),
        P("mp", "seq"),
        P(None, "seq", None),
        P(None, ("seq", "mp"), None),
    )
    out_specs = (
        P(None, ("seq", "mp"), None),
        P(None, ("seq", "mp"), None),
        P(),
        P(),
        P(),
        P(),
        P("seq", "mp"),
        P("seq", "mp"),
        P("seq", "mp"),
        P("mp", "seq"),
        P("seq", "mp"),
        P("mp", "seq"),
    )
    return jax.shard_map(body, mesh=mesh, in_specs=in_specs, out_specs=out_specs, check_vma=False)
```
